512 devices in a mesh: space: 32 (over z, x), vel: 16 (over y, core).
Axes of the slice: x: 4, y: 8, z: 8, core: 2. Of those that a mesh axis runs over, the one named last changes fastest.
Arguments:
- distribution: float32 [128, 32, 2, 4096], P('space', None, None, 'vel'), may hold values from 0.0004 to 1, as said below
- wall_mask: int32 [128, 2, 2], P('space'), may hold values 0 or 1
- grid_point: int32 [4096], P('vel'), may hold values from 0 to 4095, as said below
- mirror_slot: int32 [4096], P('vel'), may hold values from 0 to 4095, as said below
Outputs:
- swept: float32 [128, 32, 2, 4096], P('space', None, None, 'vel')
The draws below stay inside these ranges and needn't reach their ends.
Inputs may be any that keep to these rules, and one draw needn't show every extreme that they name: grid_point is a permutation of 0 .. 4095. mirror_slot is a permutation; slot mirror_slot[s] holds the velocity of slot s with its second component negated. `distribution`: every entry is positive.
All inputs are finite; a program needn't handle non-finite values. No bound on the sum of `wall_mask` on one device may be relied on, other than what follows from the above.
Results may differ from the reference program's by a relative error of at most 0.0003.
Values sent between devices are 32-bit elements; how exact they have to be, the bound alone decides.
No kernel may reach another device: no remote copies, remote signals or barrier semaphores. Data moves between devices by JAX's collectives and lax.ppermute only.
A program may use at most 64 MiB of HBM per device.

```python
import math
import jax
import jax.numpy as jnp
from jax import lax

VS = 16
V = 4096
NY = 32
NZ = 2
NX = 128


def velocity_pairs(key):
    order = jax.random.permutation(jax.random.fold_in(key, 11), V).astype(jnp.int32)
    inverse = jnp.zeros((V,), jnp.int32).at[order].set(jnp.arange(V, dtype=jnp.int32))
    first = order // (VS * VS)
    quadratic_average = order // VS % VS
    third = order % VS
    mirrored = first * VS * VS + (VS - 1 - quadratic_average) * VS + third
    return (order, inverse[mirrored])


def draw_grid_point(key, part):
    return velocity_pairs(key)[0]


def draw_mirror_slot(key, part):
    return velocity_pairs(key)[1]


def draw_distribution(key, part):
    order = velocity_pairs(key)[0]
    spacing = 8.0 / VS
    half = (VS - 1) / 2.0
    first = ((order // (VS * VS)).astype(jnp.float32) - half) * spacing
    quadratic_average = ((order // VS % VS).astype(jnp.float32) - half) * spacing
    third = ((order % VS).astype(jnp.float32) - half) * spacing
    keys = jax.random.split(jax.random.fold_in(key, 23), 10)
    line = (NX, 1, 1, 1)
    direction = jnp.where(jax.random.uniform(keys[0], line) < 0.5, -1.0, 1.0)
    beam_speed = direction * jax.random.uniform(keys[1], line, minval=2.2, maxval=3.0)
    bulk_speed = -direction * jax.random.uniform(keys[2], line, minval=0.2, maxval=0.6)
    share = jax.random.uniform(keys[3], line, minval=0.15, maxval=0.3)
    beam_var = jax.random.uniform(keys[4], line, minval=0.15, maxval=0.3)
    bulk_var = jax.random.uniform(keys[5], line, minval=0.5, maxval=0.9)
    spread = jax.random.uniform(keys[6], line, minval=1.5, maxval=2.5)
    beam_part = share / jnp.sqrt(beam_var) * jnp.exp(-(first - beam_speed) ** 2 / (2.0 * beam_var))
    bulk_part = (1.0 - share) / jnp.sqrt(bulk_var) * jnp.exp(-(first - bulk_speed) ** 2 / (2.0 * bulk_var))
    across = jnp.exp(-(quadratic_average * quadratic_average + third * third) / (2.0 * spread))
    profile = 0.002 + 0.8 * (beam_part + bulk_part) * across
    full = (NX, NY, NZ, V)
    noise = jnp.exp(jax.random.uniform(keys[9], full, minval=math.log(0.4), maxval=0.0))
    return (profile * noise).astype(jnp.float32)


def plant(entries, rng, low, high):
    longest = entries.shape.index(max(entries.shape))
    spots = []
    for shift in (0, 1):
        where = [jax.random.randint(jax.random.fold_in(rng, axis), (), 0, length) for axis, length in enumerate(entries.shape)]
        where[longest] = (where[longest] + shift) % entries.shape[longest]
        spots.append(tuple(where))
    return entries.at[spots[0]].set(low).at[spots[1]].set(high)


def setup_inputs(seed: int = 0) -> dict:
    splits = jax.random.split(jax.random.key(seed), 5)
    distribution = draw_distribution(jax.random.fold_in(splits[4], 71), 0)
    wall_mask = plant((jax.random.randint(splits[1], (NX, 2, NZ), 0, 4) < 3).astype(jnp.int32), jax.random.fold_in(splits[1], 1), 0, 1)
    grid_point = draw_grid_point(jax.random.fold_in(splits[4], 71), 0)
    mirror_slot = draw_mirror_slot(jax.random.fold_in(splits[4], 71), 0)
    return dict(distribution=distribution, wall_mask=wall_mask, grid_point=grid_point, mirror_slot=mirror_slot)


stream_x = 40.0
stream_y = 0.15
stream_z = 0.05
relaxation_multiplier = 0.05
shear_power_index = 0.81
diffusivity_ratio = 2.0 / 3.0


def velocity_table(grid_point, side):
    spacing = 8.0 / side
    half = (side - 1) / 2.0
    first = (grid_point // (side * side)).astype(jnp.float32)
    quadratic_average = ((grid_point // side) % side).astype(jnp.float32)
    third = (grid_point % side).astype(jnp.float32)
    return jnp.stack([(first - half) * spacing, (quadratic_average - half) * spacing, (third - half) * spacing])


def equilibrium(phase_occupancy_line, xi, integration_coefficient):
    particle_concentration = integration_coefficient * jnp.sum(phase_occupancy_line, -1)
    flow = [integration_coefficient * jnp.sum(phase_occupancy_line * xi[k], -1) / particle_concentration for k in range(3)]
    peculiar = [xi[k] - flow[k][..., None] for k in range(3)]
    magnitude_square = peculiar[0] * peculiar[0] + peculiar[1] * peculiar[1] + peculiar[2] * peculiar[2]
    kinetic_heat_level = integration_coefficient * jnp.sum(magnitude_square * phase_occupancy_line, -1) / (3.0 * particle_concentration)
    heat = [0.5 * integration_coefficient * jnp.sum(peculiar[k] * magnitude_square * phase_occupancy_line, -1) for k in range(3)]
    thermal_level_group = kinetic_heat_level[..., None]
    particle_concentration_local = particle_concentration[..., None]
    gaussian_equilibrium = particle_concentration_local / (2.0 * math.pi * thermal_level_group) ** 1.5 * jnp.exp(-magnitude_square / (2.0 * thermal_level_group))
    lengthwise = peculiar[0] * heat[0][..., None] + peculiar[1] * heat[1][..., None] + peculiar[2] * heat[2][..., None]
    corrected_equilibrium = gaussian_equilibrium * (1.0 + (1.0 - diffusivity_ratio) * lengthwise / (5.0 * particle_concentration_local * thermal_level_group * thermal_level_group) * (magnitude_square / thermal_level_group - 5.0))
    relaxation_frequency = relaxation_multiplier * particle_concentration * kinetic_heat_level ** (1.0 - shear_power_index)
    return corrected_equilibrium, relaxation_frequency


def row_terms(phase_occupancy_line, mask_row, xi, mirror_slot, integration_coefficient):
    corrected_equilibrium, relaxation_frequency = equilibrium(phase_occupancy_line, xi, integration_coefficient)
    ghost_low = jnp.where(mask_row[0][:, None] == 1, phase_occupancy_line[0][:, mirror_slot], corrected_equilibrium[0])
    ghost_high = jnp.where(mask_row[1][:, None] == 1, phase_occupancy_line[-1][:, mirror_slot], corrected_equilibrium[-1])
    padded = jnp.concatenate([ghost_low[None], phase_occupancy_line, ghost_high[None]], axis=0)
    below = padded[:-2]
    above = padded[2:]
    y_flux = xi[1] * jnp.where(xi[1] > 0, phase_occupancy_line - below, above - phase_occupancy_line)
    z_flux = xi[2] * jnp.where(xi[2] > 0, phase_occupancy_line - jnp.roll(phase_occupancy_line, 1, axis=1), jnp.roll(phase_occupancy_line, -1, axis=1) - phase_occupancy_line)
    sigma = stream_x * jnp.abs(xi[0])
    denom = 1.0 + sigma + relaxation_frequency[..., None]
    coef_a = sigma / denom
    coef_b = (phase_occupancy_line + relaxation_frequency[..., None] * corrected_equilibrium - stream_y * y_flux - stream_z * z_flux) / denom
    return coef_a, coef_b


def reference(distribution, wall_mask, grid_point, mirror_slot):
    xi = velocity_table(grid_point, VS)
    integration_coefficient = (8.0 / VS) ** 3

    def one_row(pair):
        return row_terms(pair[0], pair[1], xi, mirror_slot, integration_coefficient)

    coef_a, coef_b = lax.map(one_row, (distribution, wall_mask))
    first_target = equilibrium(distribution[0], xi, integration_coefficient)[0]
    last_target = equilibrium(distribution[-1], xi, integration_coefficient)[0]

    def advance(prev, pair):
        value = pair[0] * prev + pair[1]
        return value, value

    downstream = lax.scan(advance, first_target, (coef_a, coef_b))[1]
    upstream = lax.scan(advance, last_target, (coef_a, coef_b), reverse=True)[1]
    return jnp.where(xi[0] > 0, downstream, upstream)
```

```python
import math

import jax
import jax.numpy as jnp
from jax import lax
from jax.experimental import pallas as pl
from jax.experimental.pallas import tpu as pltpu
from jax.sharding import PartitionSpec as P

VS = 16
SPACING = 8.0 / VS
HALF = (VS - 1) / 2.0
WEIGHT = SPACING**3

stream_x = 40.0
stream_y = 0.15
stream_z = 0.05
relaxation_multiplier = 0.05
shear_power_index = 0.81
diffusivity_ratio = 2.0 / 3.0

DEPTH, ROWS, PLANES, WIDTH = 4, 32, 2, 256
LANES = 128
XROWS = ROWS * 2 * PLANES
F32 = jnp.float32


def velocity(points):
    first = (points >> 8).astype(F32)
    second = ((points >> 4) & 15).astype(F32)
    third = (points & 15).astype(F32)
    return [(v - HALF) * SPACING for v in (first, second, third)]


def sublane(shape):
    return lax.broadcasted_iota(jnp.int32, shape, 0)


def by_half(pair):
    low = jnp.broadcast_to(pair[0:1], (8, LANES))
    high = jnp.broadcast_to(pair[1:2], (8, LANES))
    return jnp.where((sublane((8, LANES)) & 2) == 0, low, high)


def moments_kernel(f_ref, point_ref, out_ref):
    points = point_ref[...]
    tables = []
    for half in range(2):
        x1, x2, x3 = velocity(points[half : half + 1])
        square = x1 * x1 + x2 * x2 + x3 * x3
        zero = jnp.zeros_like(x1)
        tables += [
            jnp.ones_like(x1), x1, x2, x3,
            x1 * x1, x2 * x2, x3 * x3, x1 * x2,
            x1 * x3, x2 * x3, x1 * square, x2 * square,
            x3 * square, zero, zero, zero,
        ]
    table = jnp.concatenate(tables, axis=0)
    low_lane = (lax.broadcasted_iota(jnp.int32, (8, LANES), 1) & 2) == 0
    x2 = velocity(points)[1]
    for x in range(DEPTH):
        sums = lax.dot_general(
            table,
            f_ref[pl.ds(x * XROWS, XROWS), :],
            (((1,), (1,)), ((), ())),
            precision=lax.Precision.HIGHEST,
            preferred_element_type=F32,
        )
        packed = jnp.where(
            low_lane,
            sums[0:8] + pltpu.roll(sums[16:24], LANES - 2, 1),
            sums[24:32] + pltpu.roll(sums[8:16], 2, 1),
        )
        out_ref[pl.ds(x, 8, stride=DEPTH), :] = packed
        for half in range(2):
            low = f_ref[pl.ds(x * XROWS + 2 * half, 2), :]
            high = f_ref[pl.ds((x + 1) * XROWS - 4 + 2 * half, 2), :]
            out_ref[pl.ds(32 + 8 * half + 2 * x, 2), :] = jnp.where(
                x2[half : half + 1] < 0, low, high
            )


def cell_quantities(sums):
    low_lane = (lax.broadcasted_iota(jnp.int32, (DEPTH, LANES), 1) & 2) == 0
    low, high = [], []
    for m in range(8):
        own = sums[DEPTH * m : DEPTH * (m + 1)] * WEIGHT
        other = jnp.where(low_lane, pltpu.roll(own, LANES - 2, 1), pltpu.roll(own, 2, 1))
        low.append(jnp.where(low_lane, own, other))
        high.append(jnp.where(low_lane, other, own))
    n = low[0]
    inv = 1.0 / n
    u = [low[1 + k] * inv for k in range(3)]
    pressure = {(0, 0): low[4], (1, 1): low[5], (2, 2): low[6]}
    pressure.update({(0, 1): low[7], (0, 2): high[0], (1, 2): high[1]})
    energy = low[4] + low[5] + low[6]
    speed = u[0] * u[0] + u[1] * u[1] + u[2] * u[2]
    temperature = (energy - n * speed) * inv * (1.0 / 3.0)
    heat = []
    for k in range(3):
        cross = sum(u[j] * pressure[min(j, k), max(j, k)] for j in range(3))
        heat.append(0.5 * (high[2 + k] - 2.0 * cross + u[k] * (2.0 * n * speed - energy)))
    inv_t = 1.0 / temperature
    scale = (1.0 - diffusivity_ratio) / 5.0 * inv * inv_t * inv_t
    arg = 2.0 * math.pi * temperature
    norm = n / (arg * jnp.sqrt(arg))
    rate = relaxation_multiplier * n * jnp.exp((1.0 - shear_power_index) * jnp.log(temperature))
    return u + [h * scale for h in heat] + [inv_t, norm, rate]


def blocks_kernel(
    ends_ref, wall_ref, got_ref, f_ref, point_ref, mirror_ref, send_ref, a_ref, h_ref
):
    sums = got_ref[0, 0:32, :]
    for k in range(1, 16):
        sums = sums + got_ref[k, 0:32, :]
    quantities = cell_quantities(sums)
    filler = jnp.zeros((LANES - DEPTH * len(quantities), LANES), F32)
    columns = jnp.concatenate(quantities + [filler], axis=0).T

    mirror = mirror_ref[...]
    found = []
    for half in range(2):
        slot = jnp.broadcast_to(mirror[half : half + 1], (8, LANES))
        lane, group = slot & (LANES - 1), slot >> 7
        value = jnp.zeros((8, LANES), F32)
        for source in range(32):
            piece = got_ref[source // 2, pl.ds(32 + 8 * (source % 2), 8), :]
            value = jnp.where(
                group == source, jnp.take_along_axis(piece, lane, axis=1), value
            )
        found.append(value)

    x1, x2, x3 = [by_half(v) for v in velocity(point_ref[...])]
    ahead = x1 > 0
    upward = x2 > 0
    sigma = stream_x * jnp.abs(x1)
    sigma1 = 1.0 + sigma
    flux_y = stream_y * jnp.abs(x2)
    flux_z = stream_z * jnp.abs(x3)
    own = 1.0 - flux_y - flux_z
    row = sublane((8, LANES))
    first_plane = (row & 1) == 0
    lower = row < 4
    edge = jnp.where(ahead, ends_ref[0], ends_ref[1]) == 1

    ghosts = []
    for x in range(DEPTH):
        four = jnp.concatenate(
            [found[0][2 * x : 2 * x + 2], found[1][2 * x : 2 * x + 2]], axis=0
        )
        ghosts.append(jnp.concatenate([four, four], axis=0))

    for i in range(XROWS // 8):
        a, b, target = [], [], []
        for x in range(DEPTH):
            def column(q):
                at = DEPTH * q + x
                return jnp.broadcast_to(
                    columns[8 * i : 8 * i + 8, at : at + 1], (8, LANES)
                )

            base = x * XROWS + 8 * i
            f = f_ref[pl.ds(base, 8), :]
            c1, c2, c3 = x1 - column(0), x2 - column(1), x3 - column(2)
            square = c1 * c1 + c2 * c2 + c3 * c3
            along = c1 * column(3) + c2 * column(4) + c3 * column(5)
            ratio = square * column(6)
            shakhov = column(7) * jnp.exp(-0.5 * ratio) * (1.0 + along * (ratio - 5.0))
            rate = column(8)

            def ghost(wall):
                plane0, plane1 = wall_ref[x, wall, 0], wall_ref[x, wall, 1]
                mask = jnp.where(first_plane, plane0, plane1)
                return jnp.where(mask == 1, ghosts[x], shakhov)

            if i == 0:
                below = jnp.where(lower, ghost(0), pltpu.roll(f, 4, 0))
            else:
                below = f_ref[pl.ds(base - 4, 8), :]
            if i == XROWS // 8 - 1:
                above = jnp.where(lower, pltpu.roll(f, 4, 0), ghost(1))
            else:
                above = f_ref[pl.ds(base + 4, 8), :]
            upwind = jnp.where(upward, below, above)
            other = jnp.where(first_plane, pltpu.roll(f, 7, 0), pltpu.roll(f, 1, 0))
            inverse = 1.0 / (sigma1 + rate)
            a.append(sigma * inverse)
            b.append(
                (own * f + rate * shakhov + flux_y * upwind + flux_z * other) * inverse
            )
            target.append(shakhov)
        order = lambda v, t: jnp.where(ahead, v[t], v[DEPTH - 1 - t])
        a0 = order(a, 0)
        hold = order(b, 0) + jnp.where(edge, a0 * order(target, 0), 0.0)
        gain = jnp.where(edge, 0.0, a0)
        a_ref[pl.ds(8 * i, 8), :] = gain
        h_ref[pl.ds(8 * i, 8), :] = hold
        for t in range(1, DEPTH):
            at = order(a, t)
            gain = at * gain
            hold = at * hold + order(b, t)
            a_ref[pl.ds(t * XROWS + 8 * i, 8), :] = gain
            h_ref[pl.ds(t * XROWS + 8 * i, 8), :] = hold
        send_ref[2 * i] = jnp.where(lower, gain, pltpu.roll(hold, 4, 0))
        send_ref[2 * i + 1] = jnp.where(lower, pltpu.roll(gain, 4, 0), hold)


def chain_kernel(blocks, got_ref, point_ref, out_ref, keep_ref):
    ahead = (by_half(velocity(point_ref[...])[0]) > 0)[0:4]
    enter = jnp.zeros((4, LANES), F32)
    for k in range(blocks):
        keep_ref[k] = enter
        gain = jnp.where(ahead, got_ref[k, 0:4, :], got_ref[blocks - 1 - k, 0:4, :])
        hold = jnp.where(ahead, got_ref[k, 4:8, :], got_ref[blocks - 1 - k, 4:8, :])
        enter = gain * enter + hold
    for k in range(blocks):
        out_ref[k] = jnp.where(ahead, keep_ref[k], keep_ref[blocks - 1 - k])


def finish_kernel(enter_ref, a_ref, h_ref, point_ref, out_ref):
    ahead = by_half(velocity(point_ref[...])[0]) > 0
    for i in range(XROWS // 8):
        enter = enter_ref[pl.ds(8 * i, 8), :]
        value = []
        for t in range(DEPTH):
            at = pl.ds(t * XROWS + 8 * i, 8)
            value.append(a_ref[at, :] * enter + h_ref[at, :])
        for x in range(DEPTH):
            out_ref[pl.ds(x * XROWS + 8 * i, 8), :] = jnp.where(
                ahead, value[x], value[DEPTH - 1 - x]
            )


def call(kernel, shapes, scratch=(), scalars=0, inputs=0):
    specs = [pl.BlockSpec(memory_space=pltpu.SMEM)] * scalars
    specs += [pl.BlockSpec(memory_space=pltpu.VMEM)] * inputs
    outs = [jax.ShapeDtypeStruct(s, F32) for s in shapes]
    vmem = pl.BlockSpec(memory_space=pltpu.VMEM)
    single = len(outs) == 1
    return pl.pallas_call(
        kernel,
        out_shape=outs[0] if single else outs,
        in_specs=specs,
        out_specs=vmem if single else [vmem] * len(outs),
        scratch_shapes=list(scratch),
    )


def shards(distribution, wall_mask, grid_point, mirror_slot):
    blocks = lax.axis_size("space")
    here = lax.axis_index("space")
    ends = jnp.stack([here == 0, here == blocks - 1]).astype(jnp.int32)
    f = distribution.reshape(DEPTH, ROWS, PLANES, 2, LANES)
    f = f.transpose(0, 1, 3, 2, 4).reshape(DEPTH * XROWS, LANES)
    point = grid_point.reshape(2, LANES)
    mirror = mirror_slot.reshape(2, LANES)

    mine = call(moments_kernel, [(48, LANES)], inputs=2)(f, point)
    everyone = lax.all_gather(mine, "vel")
    send, gains, holds = call(
        blocks_kernel,
        [(ROWS, 8, LANES), (DEPTH * XROWS, LANES), (DEPTH * XROWS, LANES)],
        scalars=2,
        inputs=4,
    )(ends, wall_mask, everyone, f, point, mirror)
    chain = lax.all_to_all(send, "space", 0, 0, tiled=True)
    enters = call(
        lambda *refs: chain_kernel(blocks, *refs),
        [(ROWS, 4, LANES)],
        scratch=[pltpu.VMEM((ROWS, 4, LANES), F32)],
        inputs=2,
    )(chain, point)
    enter = lax.all_to_all(enters, "space", 0, 0, tiled=True)
    out = call(finish_kernel, [(DEPTH * XROWS, LANES)], inputs=4)(
        enter.reshape(XROWS, LANES), gains, holds, point
    )
    out = out.reshape(DEPTH, ROWS, 2, PLANES, LANES).transpose(0, 1, 3, 2, 4)
    return out.reshape(DEPTH, ROWS, PLANES, WIDTH)


def solution(mesh):
    placed = (P("space", None, None, "vel"), P("space", None, None), P("vel"), P("vel"))
    return jax.shard_map(
        shards, mesh=mesh, in_specs=placed, out_specs=P("space", None, None, "vel"), check_vma=False
    )
```

```python
import math

import jax
import jax.numpy as jnp
from jax import lax
from jax.experimental import pallas as pl
from jax.experimental.pallas import tpu as pltpu
from jax.sharding import PartitionSpec as P

VS = 16
SPACING = 8.0 / VS
HALF = (VS - 1) / 2.0
WEIGHT = SPACING**3

stream_x = 40.0
stream_y = 0.15
stream_z = 0.05
relaxation_multiplier = 0.05
shear_power_index = 0.81
diffusivity_ratio = 2.0 / 3.0

DEPTH, ROWS, PLANES, WIDTH = 4, 32, 2, 256
LANES = 128
XROWS = ROWS * 2 * PLANES
F32 = jnp.float32


def velocity(points):
    first = (points >> 8).astype(F32)
    second = ((points >> 4) & 15).astype(F32)
    third = (points & 15).astype(F32)
    return [(v - HALF) * SPACING for v in (first, second, third)]


def sublane(shape):
    return lax.broadcasted_iota(jnp.int32, shape, 0)


def by_half(pair):
    low = jnp.broadcast_to(pair[0:1], (8, LANES))
    high = jnp.broadcast_to(pair[1:2], (8, LANES))
    return jnp.where((sublane((8, LANES)) & 2) == 0, low, high)


def moments_kernel(
    f_hbm, point_hbm, mirror_hbm, wall_hbm,
    out_ref, f_ref, pattern_ref, slot_ref,
    point_ref, mirror_ref, wall_ref, f_sem, small_sem,
):
    small = [
        pltpu.make_async_copy(src, dst, small_sem.at[k])
        for k, (src, dst) in enumerate(
            [(point_hbm, point_ref), (wall_hbm, wall_ref), (mirror_hbm, mirror_ref)]
        )
    ]
    for copy in small:
        copy.start()
    chunks = []
    for x in range(DEPTH):
        rows = pl.ds(x * XROWS, XROWS)
        chunks.append(pltpu.make_async_copy(f_hbm.at[rows], f_ref.at[rows], f_sem.at[x]))
        chunks[x].start()

    small[0].wait()
    points = point_ref[...]
    tables = []
    for half in range(2):
        x1, x2, x3 = velocity(points[half : half + 1])
        square = x1 * x1 + x2 * x2 + x3 * x3
        zero = jnp.zeros_like(x1)
        tables += [
            jnp.ones_like(x1), x1, x2, x3,
            x1 * x1, x2 * x2, x3 * x3, x1 * x2,
            x1 * x3, x2 * x3, x1 * square, x2 * square,
            x3 * square, zero, zero, zero,
        ]
    table = jnp.concatenate(tables, axis=0)
    low_lane = (lax.broadcasted_iota(jnp.int32, (8, LANES), 1) & 2) == 0
    pairs = velocity(points)
    for k in range(3):
        pattern_ref[k] = by_half(pairs[k])
    small[1].wait()
    for x in range(DEPTH):
        for wall in range(2):
            planes = wall_ref[wall, :, x : x + 1].astype(F32)
            planes = jnp.broadcast_to(planes, (PLANES, LANES))
            pattern_ref[3 + 2 * x + wall] = jnp.concatenate([planes] * 4, axis=0)
    small[2].wait()
    for half in range(2):
        slot_ref[half] = jnp.broadcast_to(mirror_ref[half : half + 1], (8, LANES))

    x2 = pairs[1]
    for x in range(DEPTH):
        chunks[x].wait()
        sums = lax.dot_general(
            table,
            f_ref[pl.ds(x * XROWS, XROWS), :],
            (((1,), (1,)), ((), ())),
            precision=lax.Precision.HIGHEST,
            preferred_element_type=F32,
        )
        packed = jnp.where(
            low_lane,
            sums[0:8] + pltpu.roll(sums[16:24], LANES - 2, 1),
            sums[24:32] + pltpu.roll(sums[8:16], 2, 1),
        )
        out_ref[pl.ds(x, 8, stride=DEPTH), :] = packed
        for half in range(2):
            low = f_ref[pl.ds(x * XROWS + 2 * half, 2), :]
            high = f_ref[pl.ds((x + 1) * XROWS - 4 + 2 * half, 2), :]
            out_ref[pl.ds(32 + 8 * half + 2 * x, 2), :] = jnp.where(
                x2[half : half + 1] < 0, low, high
            )


def cell_quantities(sums):
    low_lane = (lax.broadcasted_iota(jnp.int32, (DEPTH, LANES), 1) & 2) == 0
    low, high = [], []
    for m in range(8):
        own = sums[DEPTH * m : DEPTH * (m + 1)] * WEIGHT
        other = jnp.where(low_lane, pltpu.roll(own, LANES - 2, 1), pltpu.roll(own, 2, 1))
        low.append(jnp.where(low_lane, own, other))
        high.append(jnp.where(low_lane, other, own))
    n = low[0]
    inv = 1.0 / n
    u = [low[1 + k] * inv for k in range(3)]
    pressure = {(0, 0): low[4], (1, 1): low[5], (2, 2): low[6]}
    pressure.update({(0, 1): low[7], (0, 2): high[0], (1, 2): high[1]})
    energy = low[4] + low[5] + low[6]
    speed = u[0] * u[0] + u[1] * u[1] + u[2] * u[2]
    temperature = (energy - n * speed) * inv * (1.0 / 3.0)
    heat = []
    for k in range(3):
        cross = sum(u[j] * pressure[min(j, k), max(j, k)] for j in range(3))
        heat.append(0.5 * (high[2 + k] - 2.0 * cross + u[k] * (2.0 * n * speed - energy)))
    inv_t = 1.0 / temperature
    scale = (1.0 - diffusivity_ratio) / 5.0 * inv * inv_t * inv_t
    arg = 2.0 * math.pi * temperature
    norm = n / (arg * jnp.sqrt(arg))
    rate = relaxation_multiplier * n * jnp.exp((1.0 - shear_power_index) * jnp.log(temperature))
    return u + [h * scale for h in heat] + [inv_t, norm, rate]


def blocks_kernel(got_ref, f_ref, pattern_ref, slot_ref, send_ref, a_ref, h_ref):
    sums = got_ref[0, 0:32, :]
    for k in range(1, 16):
        sums = sums + got_ref[k, 0:32, :]
    quantities = cell_quantities(sums)
    filler = jnp.zeros((LANES - DEPTH * len(quantities), LANES), F32)
    columns = jnp.concatenate(quantities + [filler], axis=0).T

    found = []
    for half in range(2):
        slot = slot_ref[half]
        lane, group = slot & (LANES - 1), slot >> 7
        value = jnp.zeros((8, LANES), F32)
        for source in range(32):
            piece = got_ref[source // 2, pl.ds(32 + 8 * (source % 2), 8), :]
            value = jnp.where(
                group == source, jnp.take_along_axis(piece, lane, axis=1), value
            )
        found.append(value)

    x1, x2, x3 = pattern_ref[0], pattern_ref[1], pattern_ref[2]
    ahead = x1 > 0
    upward = x2 > 0
    sigma = stream_x * jnp.abs(x1)
    sigma1 = 1.0 + sigma
    flux_y = stream_y * jnp.abs(x2)
    flux_z = stream_z * jnp.abs(x3)
    own = 1.0 - flux_y - flux_z
    row = sublane((8, LANES))
    first_plane = (row & 1) == 0
    lower = row < 4
    here = lax.axis_index("space")
    edge = here == jnp.where(ahead, 0, lax.axis_size("space") - 1)

    ghosts = []
    for x in range(DEPTH):
        four = jnp.concatenate(
            [found[0][2 * x : 2 * x + 2], found[1][2 * x : 2 * x + 2]], axis=0
        )
        ghosts.append(jnp.concatenate([four, four], axis=0))

    for i in range(XROWS // 8):
        a, b, target = [], [], []
        for x in range(DEPTH):
            def column(q):
                at = DEPTH * q + x
                return jnp.broadcast_to(
                    columns[8 * i : 8 * i + 8, at : at + 1], (8, LANES)
                )

            base = x * XROWS + 8 * i
            f = f_ref[pl.ds(base, 8), :]
            c1, c2, c3 = x1 - column(0), x2 - column(1), x3 - column(2)
            square = c1 * c1 + c2 * c2 + c3 * c3
            along = c1 * column(3) + c2 * column(4) + c3 * column(5)
            ratio = square * column(6)
            shakhov = column(7) * jnp.exp(-0.5 * ratio) * (1.0 + along * (ratio - 5.0))
            rate = column(8)

            def ghost(wall):
                mask = pattern_ref[3 + 2 * x + wall]
                return jnp.where(mask == 1.0, ghosts[x], shakhov)

            if i == 0:
                below = jnp.where(lower, ghost(0), pltpu.roll(f, 4, 0))
            else:
                below = f_ref[pl.ds(base - 4, 8), :]
            if i == XROWS // 8 - 1:
                above = jnp.where(lower, pltpu.roll(f, 4, 0), ghost(1))
            else:
                above = f_ref[pl.ds(base + 4, 8), :]
            upwind = jnp.where(upward, below, above)
            other = jnp.where(first_plane, pltpu.roll(f, 7, 0), pltpu.roll(f, 1, 0))
            inverse = 1.0 / (sigma1 + rate)
            a.append(sigma * inverse)
            b.append(
                (own * f + rate * shakhov + flux_y * upwind + flux_z * other) * inverse
            )
            target.append(shakhov)
        order = lambda v, t: jnp.where(ahead, v[t], v[DEPTH - 1 - t])
        a0 = order(a, 0)
        hold = order(b, 0) + jnp.where(edge, a0 * order(target, 0), 0.0)
        gain = jnp.where(edge, 0.0, a0)
        a_ref[pl.ds(8 * i, 8), :] = gain
        h_ref[pl.ds(8 * i, 8), :] = hold
        for t in range(1, DEPTH):
            at = order(a, t)
            gain = at * gain
            hold = at * hold + order(b, t)
            a_ref[pl.ds(t * XROWS + 8 * i, 8), :] = gain
            h_ref[pl.ds(t * XROWS + 8 * i, 8), :] = hold
        send_ref[2 * i] = jnp.where(lower, gain, pltpu.roll(hold, 4, 0))
        send_ref[2 * i + 1] = jnp.where(lower, pltpu.roll(gain, 4, 0), hold)


def chain_kernel(blocks, got_ref, pattern_ref, out_ref, keep_ref):
    ahead = pattern_ref[0, 0:4, :] > 0
    enter = jnp.zeros((4, LANES), F32)
    for k in range(blocks):
        keep_ref[k] = enter
        gain = jnp.where(ahead, got_ref[k, 0:4, :], got_ref[blocks - 1 - k, 0:4, :])
        hold = jnp.where(ahead, got_ref[k, 4:8, :], got_ref[blocks - 1 - k, 4:8, :])
        enter = gain * enter + hold
    for k in range(blocks):
        out_ref[k] = jnp.where(ahead, keep_ref[k], keep_ref[blocks - 1 - k])


def finish_kernel(enter_ref, a_ref, h_ref, pattern_ref, out_hbm, out_ref, sem):
    ahead = pattern_ref[0] > 0
    copies = []
    for x, mate in ((0, DEPTH - 1), (1, DEPTH - 2)):
        for i in range(XROWS // 8):
            enter = enter_ref[pl.ds(8 * i, 8), :]
            value = []
            for t in (x, mate):
                at = pl.ds(t * XROWS + 8 * i, 8)
                value.append(a_ref[at, :] * enter + h_ref[at, :])
            out_ref[pl.ds(x * XROWS + 8 * i, 8), :] = jnp.where(ahead, value[0], value[1])
            out_ref[pl.ds(mate * XROWS + 8 * i, 8), :] = jnp.where(ahead, value[1], value[0])
        for t in (x, mate):
            rows = pl.ds(t * XROWS, XROWS)
            copies.append(pltpu.make_async_copy(out_ref.at[rows], out_hbm.at[rows], sem.at[t]))
            copies[-1].start()
    for copy in copies:
        copy.wait()


ON_CHIP = pl.BlockSpec(memory_space=pltpu.VMEM)
ANYWHERE = pl.BlockSpec(memory_space=pl.ANY)


def held(x):
    return pltpu.with_memory_space_constraint(x, pltpu.VMEM)


def shards(distribution, wall_mask, grid_point, mirror_slot):
    blocks = lax.axis_size("space")
    f = distribution.reshape(DEPTH, ROWS, PLANES, 2, LANES)
    f = f.transpose(0, 1, 3, 2, 4).reshape(DEPTH * XROWS, LANES)
    point = grid_point.reshape(2, LANES)
    mirror = mirror_slot.reshape(2, LANES)
    wall = wall_mask.transpose(1, 2, 0)

    mine, kept, pattern, slots = pl.pallas_call(
        moments_kernel,
        out_shape=[
            pltpu.VMEM((48, LANES), F32),
            pltpu.VMEM((DEPTH * XROWS, LANES), F32),
            pltpu.VMEM((3 + 2 * DEPTH, 8, LANES), F32),
            pltpu.VMEM((2, 8, LANES), jnp.int32),
        ],
        in_specs=[ANYWHERE] * 4,
        out_specs=[ON_CHIP] * 4,
        scratch_shapes=[
            pltpu.VMEM((2, LANES), jnp.int32),
            pltpu.VMEM((2, LANES), jnp.int32),
            pltpu.VMEM((2, PLANES, DEPTH), jnp.int32),
            pltpu.SemaphoreType.DMA((DEPTH,)),
            pltpu.SemaphoreType.DMA((3,)),
        ],
    )(f, point, mirror, wall)
    everyone = lax.all_gather(mine, "vel")
    send, gains, holds = pl.pallas_call(
        blocks_kernel,
        out_shape=[
            pltpu.VMEM((ROWS, 8, LANES), F32),
            pltpu.VMEM((DEPTH * XROWS, LANES), F32),
            pltpu.VMEM((DEPTH * XROWS, LANES), F32),
        ],
        in_specs=[ON_CHIP] * 4,
        out_specs=[ON_CHIP] * 3,
    )(held(everyone), held(kept), held(pattern), held(slots))
    chain = lax.all_to_all(send, "space", 0, 0, tiled=True)
    enters = pl.pallas_call(
        lambda *refs: chain_kernel(blocks, *refs),
        out_shape=pltpu.VMEM((ROWS, 4, LANES), F32),
        in_specs=[ON_CHIP] * 2,
        out_specs=ON_CHIP,
        scratch_shapes=[pltpu.VMEM((ROWS, 4, LANES), F32)],
    )(held(chain), held(pattern))
    enter = lax.all_to_all(enters, "space", 0, 0, tiled=True)
    out = pl.pallas_call(
        finish_kernel,
        out_shape=jax.ShapeDtypeStruct((DEPTH * XROWS, LANES), F32),
        in_specs=[ON_CHIP] * 4,
        out_specs=ANYWHERE,
        scratch_shapes=[
            pltpu.VMEM((DEPTH * XROWS, LANES), F32),
            pltpu.SemaphoreType.DMA((DEPTH,)),
        ],
    )(held(enter.reshape(XROWS, LANES)), held(gains), held(holds), held(pattern))
    out = out.reshape(DEPTH, ROWS, 2, PLANES, LANES).transpose(0, 1, 3, 2, 4)
    return out.reshape(DEPTH, ROWS, PLANES, WIDTH)


def solution(mesh):
    placed = (P("space", None, None, "vel"), P("space", None, None), P("vel"), P("vel"))
    return jax.shard_map(
        shards, mesh=mesh, in_specs=placed, out_specs=P("space", None, None, "vel"), check_vma=False
    )
```

```python
import math

import jax
import jax.numpy as jnp
from jax import lax
from jax.experimental import pallas as pl
from jax.experimental.pallas import tpu as pltpu
from jax.sharding import PartitionSpec as P

VS = 16
SPACING = 8.0 / VS
HALF = (VS - 1) / 2.0
WEIGHT = SPACING**3

stream_x = 40.0
stream_y = 0.15
stream_z = 0.05
relaxation_multiplier = 0.05
shear_power_index = 0.81
diffusivity_ratio = 2.0 / 3.0

DEPTH, ROWS, PLANES, WIDTH = 4, 32, 2, 256
LANES = 128
XROWS = ROWS * 2 * PLANES
F32 = jnp.float32

CHUNKS = 8
CHUNK_ROWS = 17


def velocity(points):
    first = (points >> 8).astype(F32)
    second = ((points >> 4) & 15).astype(F32)
    third = (points & 15).astype(F32)
    return [(v - HALF) * SPACING for v in (first, second, third)]


def sublane(shape):
    return lax.broadcasted_iota(jnp.int32, shape, 0)


def by_half(pair):
    low = jnp.broadcast_to(pair[0:1], (8, LANES))
    high = jnp.broadcast_to(pair[1:2], (8, LANES))
    return jnp.where((sublane((8, LANES)) & 2) == 0, low, high)


def moments_kernel(
    f_hbm, point_hbm, mirror_hbm, wall_hbm,
    out_ref, f_ref, pattern_ref, slot_ref,
    point_ref, mirror_ref, wall_ref, f_sem, small_sem,
):
    small = [
        pltpu.make_async_copy(src, dst, small_sem.at[k])
        for k, (src, dst) in enumerate(
            [(point_hbm, point_ref), (wall_hbm, wall_ref), (mirror_hbm, mirror_ref)]
        )
    ]
    for copy in small:
        copy.start()
    chunks = []
    for x in range(DEPTH):
        rows = pl.ds(x * XROWS, XROWS)
        chunks.append(pltpu.make_async_copy(f_hbm.at[rows], f_ref.at[rows], f_sem.at[x]))
        chunks[x].start()

    small[0].wait()
    points = point_ref[...]
    tables = []
    for half in range(2):
        x1, x2, x3 = velocity(points[half : half + 1])
        square = x1 * x1 + x2 * x2 + x3 * x3
        zero = jnp.zeros_like(x1)
        tables += [
            jnp.ones_like(x1), x1, x2, x3,
            x1 * x1, x2 * x2, x3 * x3, x1 * x2,
            x1 * x3, x2 * x3, x1 * square, x2 * square,
            x3 * square, zero, zero, zero,
        ]
    table = jnp.concatenate(tables, axis=0)
    low_lane = (lax.broadcasted_iota(jnp.int32, (8, LANES), 1) & 2) == 0
    pairs = velocity(points)
    for k in range(3):
        pattern_ref[k] = by_half(pairs[k])
    small[1].wait()
    for x in range(DEPTH):
        for wall in range(2):
            planes = wall_ref[wall, :, x : x + 1].astype(F32)
            planes = jnp.broadcast_to(planes, (PLANES, LANES))
            pattern_ref[3 + 2 * x + wall] = jnp.concatenate([planes] * 4, axis=0)
    small[2].wait()
    for half in range(2):
        slot_ref[half] = jnp.broadcast_to(mirror_ref[half : half + 1], (8, LANES))

    x2 = pairs[1]
    for x in range(DEPTH):
        chunks[x].wait()
        sums = lax.dot_general(
            table,
            f_ref[pl.ds(x * XROWS, XROWS), :],
            (((1,), (1,)), ((), ())),
            precision=lax.Precision.HIGHEST,
            preferred_element_type=F32,
        )
        packed = jnp.where(
            low_lane,
            sums[0:8] + pltpu.roll(sums[16:24], LANES - 2, 1),
            sums[24:32] + pltpu.roll(sums[8:16], 2, 1),
        )
        out_ref[pl.ds(x, 8, stride=DEPTH), :] = packed
        for half in range(2):
            low = f_ref[pl.ds(x * XROWS + 2 * half, 2), :]
            high = f_ref[pl.ds((x + 1) * XROWS - 4 + 2 * half, 2), :]
            out_ref[pl.ds(32 + 8 * half + 2 * x, 2), :] = jnp.where(
                x2[half : half + 1] < 0, low, high
            )


def cell_quantities(sums):
    low_lane = (lax.broadcasted_iota(jnp.int32, (DEPTH, LANES), 1) & 2) == 0
    low, high = [], []
    for m in range(8):
        own = sums[DEPTH * m : DEPTH * (m + 1)] * WEIGHT
        other = jnp.where(low_lane, pltpu.roll(own, LANES - 2, 1), pltpu.roll(own, 2, 1))
        low.append(jnp.where(low_lane, own, other))
        high.append(jnp.where(low_lane, other, own))
    n = low[0]
    inv = 1.0 / n
    u = [low[1 + k] * inv for k in range(3)]
    pressure = {(0, 0): low[4], (1, 1): low[5], (2, 2): low[6]}
    pressure.update({(0, 1): low[7], (0, 2): high[0], (1, 2): high[1]})
    energy = low[4] + low[5] + low[6]
    speed = u[0] * u[0] + u[1] * u[1] + u[2] * u[2]
    temperature = (energy - n * speed) * inv * (1.0 / 3.0)
    heat = []
    for k in range(3):
        cross = sum(u[j] * pressure[min(j, k), max(j, k)] for j in range(3))
        heat.append(0.5 * (high[2 + k] - 2.0 * cross + u[k] * (2.0 * n * speed - energy)))
    inv_t = 1.0 / temperature
    scale = (1.0 - diffusivity_ratio) / 5.0 * inv * inv_t * inv_t
    arg = 2.0 * math.pi * temperature
    norm = n / (arg * jnp.sqrt(arg))
    rate = relaxation_multiplier * n * jnp.exp((1.0 - shear_power_index) * jnp.log(temperature))
    return u + [h * scale for h in heat] + [inv_t, norm, rate]


def blocks_kernel(copies, got_ref, f_ref, pattern_ref, slot_ref, send_ref, a_ref, h_ref):
    sums = got_ref[0, 0:32, :]
    for k in range(1, 16):
        sums = sums + got_ref[k, 0:32, :]
    quantities = cell_quantities(sums)
    filler = jnp.zeros((LANES - DEPTH * len(quantities), LANES), F32)
    columns = jnp.concatenate(quantities + [filler], axis=0).T

    lane = lax.broadcasted_iota(jnp.int32, (8, LANES), 1)
    cell = (lane >> 3) & 7
    source = 16 * sublane((8, LANES)) + 4 * (cell >> 1) + (cell & 1)
    speed = stream_x * SPACING * ((lane & 7).astype(F32) + 0.5)
    chunk_gain = jnp.ones((8, LANES), F32)
    for x in range(DEPTH):
        rate = jnp.broadcast_to(quantities[8][x : x + 1], (8, LANES))
        rate = jnp.take_along_axis(rate, source, axis=1)
        chunk_gain = chunk_gain * (speed / (1.0 + speed + rate))
    for to in range(copies * CHUNKS):
        at = to % CHUNKS
        send_ref[pl.ds(CHUNK_ROWS * to + 16, 1), :] = chunk_gain[at : at + 1]

    found = []
    for half in range(2):
        slot = slot_ref[half]
        lane, group = slot & (LANES - 1), slot >> 7
        value = jnp.zeros((8, LANES), F32)
        for source in range(32):
            piece = got_ref[source // 2, pl.ds(32 + 8 * (source % 2), 8), :]
            value = jnp.where(
                group == source, jnp.take_along_axis(piece, lane, axis=1), value
            )
        found.append(value)

    x1, x2, x3 = pattern_ref[0], pattern_ref[1], pattern_ref[2]
    ahead = x1 > 0
    upward = x2 > 0
    sigma = stream_x * jnp.abs(x1)
    sigma1 = 1.0 + sigma
    flux_y = stream_y * jnp.abs(x2)
    flux_z = stream_z * jnp.abs(x3)
    own = 1.0 - flux_y - flux_z
    row = sublane((8, LANES))
    first_plane = (row & 1) == 0
    lower = row < 4
    here = lax.axis_index("space")
    edge = here == jnp.where(ahead, 0, lax.axis_size("space") - 1)

    ghosts = []
    for x in range(DEPTH):
        four = jnp.concatenate(
            [found[0][2 * x : 2 * x + 2], found[1][2 * x : 2 * x + 2]], axis=0
        )
        ghosts.append(jnp.concatenate([four, four], axis=0))

    for i in range(XROWS // 8):
        a, b, target = [], [], []
        for x in range(DEPTH):
            def column(q):
                at = DEPTH * q + x
                return jnp.broadcast_to(
                    columns[8 * i : 8 * i + 8, at : at + 1], (8, LANES)
                )

            base = x * XROWS + 8 * i
            f = f_ref[pl.ds(base, 8), :]
            c1, c2, c3 = x1 - column(0), x2 - column(1), x3 - column(2)
            square = c1 * c1 + c2 * c2 + c3 * c3
            along = c1 * column(3) + c2 * column(4) + c3 * column(5)
            ratio = square * column(6)
            shakhov = column(7) * jnp.exp(-0.5 * ratio) * (1.0 + along * (ratio - 5.0))
            rate = column(8)

            def ghost(wall):
                mask = pattern_ref[3 + 2 * x + wall]
                return jnp.where(mask == 1.0, ghosts[x], shakhov)

            if i == 0:
                below = jnp.where(lower, ghost(0), pltpu.roll(f, 4, 0))
            else:
                below = f_ref[pl.ds(base - 4, 8), :]
            if i == XROWS // 8 - 1:
                above = jnp.where(lower, pltpu.roll(f, 4, 0), ghost(1))
            else:
                above = f_ref[pl.ds(base + 4, 8), :]
            upwind = jnp.where(upward, below, above)
            other = jnp.where(first_plane, pltpu.roll(f, 7, 0), pltpu.roll(f, 1, 0))
            inverse = 1.0 / (sigma1 + rate)
            a.append(sigma * inverse)
            b.append(
                (own * f + rate * shakhov + flux_y * upwind + flux_z * other) * inverse
            )
            target.append(shakhov)
        order = lambda v, t: jnp.where(ahead, v[t], v[DEPTH - 1 - t])
        a0 = order(a, 0)
        hold = order(b, 0) + jnp.where(edge, a0 * order(target, 0), 0.0)
        gain = jnp.where(edge, 0.0, a0)
        a_ref[pl.ds(8 * i, 8), :] = gain
        h_ref[pl.ds(8 * i, 8), :] = hold
        for t in range(1, DEPTH):
            at = order(a, t)
            gain = at * gain
            hold = at * hold + order(b, t)
            a_ref[pl.ds(t * XROWS + 8 * i, 8), :] = gain
            h_ref[pl.ds(t * XROWS + 8 * i, 8), :] = hold
        for copy in range(copies):
            to = copy * CHUNKS + i // 2
            send_ref[pl.ds(CHUNK_ROWS * to + 8 * (i % 2), 8), :] = hold


def chain_kernel(copies, got_ref, pattern_ref, out_ref, gain_ref, keep_ref):
    blocks = copies * CHUNKS
    ahead = pattern_ref[0] > 0
    which = (jnp.abs(pattern_ref[0]) * (1.0 / SPACING) - 0.5).astype(jnp.int32)
    row = sublane((8, LANES))
    for half in range(2):
        cell = 2 * (2 * half + (row >> 2)) + (row & 1)
        source = 8 * cell + which
        for k in range(blocks):
            gain = jnp.broadcast_to(got_ref[pl.ds(CHUNK_ROWS * k + 16, 1), :], (8, LANES))
            gain_ref[k] = jnp.take_along_axis(gain, source, axis=1)
        enter = jnp.zeros((8, LANES), F32)
        for k in range(blocks):
            keep_ref[half, k] = enter
            back = blocks - 1 - k
            gain = jnp.where(ahead, gain_ref[k], gain_ref[back])
            hold = jnp.where(
                ahead,
                got_ref[pl.ds(CHUNK_ROWS * k + 8 * half, 8), :],
                got_ref[pl.ds(CHUNK_ROWS * back + 8 * half, 8), :],
            )
            enter = gain * enter + hold
    first = lax.axis_index("space") // CHUNKS * CHUNKS
    for half in range(2):
        for x in range(CHUNKS):
            out_ref[x, pl.ds(8 * half, 8), :] = jnp.where(
                ahead, keep_ref[half, first + x], keep_ref[half, blocks - 1 - x - first]
            )


def finish_kernel(enter_ref, a_ref, h_ref, pattern_ref, out_hbm, out_ref, sem):
    ahead = pattern_ref[0] > 0
    copies = []
    for x, mate in ((0, DEPTH - 1), (1, DEPTH - 2)):
        for i in range(XROWS // 8):
            enter = enter_ref[pl.ds(8 * i, 8), :]
            value = []
            for t in (x, mate):
                at = pl.ds(t * XROWS + 8 * i, 8)
                value.append(a_ref[at, :] * enter + h_ref[at, :])
            out_ref[pl.ds(x * XROWS + 8 * i, 8), :] = jnp.where(ahead, value[0], value[1])
            out_ref[pl.ds(mate * XROWS + 8 * i, 8), :] = jnp.where(ahead, value[1], value[0])
        for t in (x, mate):
            rows = pl.ds(t * XROWS, XROWS)
            copies.append(pltpu.make_async_copy(out_ref.at[rows], out_hbm.at[rows], sem.at[t]))
            copies[-1].start()
    for copy in copies:
        copy.wait()


ON_CHIP = pl.BlockSpec(memory_space=pltpu.VMEM)
ANYWHERE = pl.BlockSpec(memory_space=pl.ANY)


def held(x):
    return pltpu.with_memory_space_constraint(x, pltpu.VMEM)


def shards(distribution, wall_mask, grid_point, mirror_slot):
    blocks = lax.axis_size("space")
    copies = blocks // CHUNKS
    f = distribution.reshape(DEPTH, ROWS, PLANES, 2, LANES)
    f = f.transpose(0, 1, 3, 2, 4).reshape(DEPTH * XROWS, LANES)
    point = grid_point.reshape(2, LANES)
    mirror = mirror_slot.reshape(2, LANES)
    wall = wall_mask.transpose(1, 2, 0)

    mine, kept, pattern, slots = pl.pallas_call(
        moments_kernel,
        out_shape=[
            pltpu.VMEM((48, LANES), F32),
            pltpu.VMEM((DEPTH * XROWS, LANES), F32),
            pltpu.VMEM((3 + 2 * DEPTH, 8, LANES), F32),
            pltpu.VMEM((2, 8, LANES), jnp.int32),
        ],
        in_specs=[ANYWHERE] * 4,
        out_specs=[ON_CHIP] * 4,
        scratch_shapes=[
            pltpu.VMEM((2, LANES), jnp.int32),
            pltpu.VMEM((2, LANES), jnp.int32),
            pltpu.VMEM((2, PLANES, DEPTH), jnp.int32),
            pltpu.SemaphoreType.DMA((DEPTH,)),
            pltpu.SemaphoreType.DMA((3,)),
        ],
    )(f, point, mirror, wall)
    everyone = lax.all_gather(mine, "vel")
    send, gains, holds = pl.pallas_call(
        lambda *refs: blocks_kernel(copies, *refs),
        out_shape=[
            pltpu.VMEM((blocks * CHUNK_ROWS, LANES), F32),
            pltpu.VMEM((DEPTH * XROWS, LANES), F32),
            pltpu.VMEM((DEPTH * XROWS, LANES), F32),
        ],
        in_specs=[ON_CHIP] * 4,
        out_specs=[ON_CHIP] * 3,
    )(held(everyone), held(kept), held(pattern), held(slots))
    chain = lax.all_to_all(
        send.reshape(blocks, 1, CHUNK_ROWS * LANES), "space", 0, 0, tiled=True
    ).reshape(blocks * CHUNK_ROWS, LANES)
    enters = pl.pallas_call(
        lambda *refs: chain_kernel(copies, *refs),
        out_shape=pltpu.VMEM((CHUNKS, 16, LANES), F32),
        in_specs=[ON_CHIP] * 2,
        out_specs=ON_CHIP,
        scratch_shapes=[
            pltpu.VMEM((blocks, 8, LANES), F32),
            pltpu.VMEM((2, blocks, 8, LANES), F32),
        ],
    )(held(chain), held(pattern))
    lines = [[CHUNKS * z + x for x in range(CHUNKS)] for z in range(copies)]
    enter = lax.all_to_all(enters, "space", 0, 0, axis_index_groups=lines, tiled=True)
    out = pl.pallas_call(
        finish_kernel,
        out_shape=jax.ShapeDtypeStruct((DEPTH * XROWS, LANES), F32),
        in_specs=[ON_CHIP] * 4,
        out_specs=ANYWHERE,
        scratch_shapes=[
            pltpu.VMEM((DEPTH * XROWS, LANES), F32),
            pltpu.SemaphoreType.DMA((DEPTH,)),
        ],
    )(held(enter.reshape(XROWS, LANES)), held(gains), held(holds), held(pattern))
    out = out.reshape(DEPTH, ROWS, 2, PLANES, LANES).transpose(0, 1, 3, 2, 4)
    return out.reshape(DEPTH, ROWS, PLANES, WIDTH)


def solution(mesh):
    placed = (P("space", None, None, "vel"), P("space", None, None), P("vel"), P("vel"))
    return jax.shard_map(
        shards, mesh=mesh, in_specs=placed, out_specs=P("space", None, None, "vel"), check_vma=False
    )
```

```python
import math

import jax
import jax.numpy as jnp
from jax import lax
from jax.experimental import pallas as pl
from jax.experimental.pallas import tpu as pltpu
from jax.sharding import PartitionSpec as P

VS = 16
SPACING = 8.0 / VS
HALF = (VS - 1) / 2.0
WEIGHT = SPACING**3

stream_x = 40.0
stream_y = 0.15
stream_z = 0.05
relaxation_multiplier = 0.05
shear_power_index = 0.81
diffusivity_ratio = 2.0 / 3.0

DEPTH, ROWS, PLANES, WIDTH = 4, 32, 2, 256
LANES = 128
XROWS = ROWS * 2 * PLANES
F32 = jnp.float32
BF16 = jnp.bfloat16

CHUNKS = 8
CHUNK_ROWS = 17


def velocity(points):
    first = (points >> 8).astype(F32)
    second = ((points >> 4) & 15).astype(F32)
    third = (points & 15).astype(F32)
    return [(v - HALF) * SPACING for v in (first, second, third)]


def sublane(shape):
    return lax.broadcasted_iota(jnp.int32, shape, 0)


def by_half(pair):
    low = jnp.broadcast_to(pair[0:1], (8, LANES))
    high = jnp.broadcast_to(pair[1:2], (8, LANES))
    return jnp.where((sublane((8, LANES)) & 2) == 0, low, high)


def moments_kernel(
    f_hbm, point_hbm, mirror_hbm, wall_hbm,
    out_ref, f_ref, pattern_ref, slot_ref,
    point_ref, mirror_ref, wall_ref, f_sem, small_sem,
):
    small = [
        pltpu.make_async_copy(src, dst, small_sem.at[k])
        for k, (src, dst) in enumerate(
            [(point_hbm, point_ref), (wall_hbm, wall_ref), (mirror_hbm, mirror_ref)]
        )
    ]
    for copy in small:
        copy.start()
    chunks = []
    for x in range(2):
        rows = pl.ds(2 * x * XROWS, 2 * XROWS)
        chunks.append(pltpu.make_async_copy(f_hbm.at[rows], f_ref.at[rows], f_sem.at[x]))
        chunks[x].start()

    small[0].wait()
    points = point_ref[...]
    tables = []
    for half in range(2):
        x1, x2, x3 = velocity(points[half : half + 1])
        square = x1 * x1 + x2 * x2 + x3 * x3
        cubes = [x1 * square, x2 * square, x3 * square]
        coarse = [c.astype(BF16).astype(F32) for c in cubes]
        tables += [
            jnp.ones_like(x1), x1, x2, x3,
            x1 * x1, x2 * x2, x3 * x3, x1 * x2,
            x1 * x3, x2 * x3, *coarse,
            *[c - r for c, r in zip(cubes, coarse)],
        ]
    table = jnp.concatenate(tables, axis=0).astype(BF16)
    table = jnp.concatenate([table] * 3, axis=1)
    low_lane = (lax.broadcasted_iota(jnp.int32, (8, LANES), 1) & 2) == 0
    pairs = velocity(points)
    for k in range(3):
        pattern_ref[k] = by_half(pairs[k])
    small[1].wait()
    for x in range(DEPTH):
        for wall in range(2):
            planes = wall_ref[wall, :, x : x + 1].astype(F32)
            planes = jnp.broadcast_to(planes, (PLANES, LANES))
            pattern_ref[3 + 2 * x + wall] = jnp.concatenate([planes] * 4, axis=0)
    small[2].wait()
    for half in range(2):
        slot_ref[half] = jnp.broadcast_to(mirror_ref[half : half + 1], (8, LANES))

    x2 = pairs[1]
    for x in range(DEPTH):
        if x % 2 == 0:
            chunks[x // 2].wait()
            f = f_ref[pl.ds(x * XROWS, 2 * XROWS), :]
            high = f.astype(BF16)
            rest = f - high.astype(F32)
            middle = rest.astype(BF16)
            low = (rest - middle.astype(F32)).astype(BF16)
            both = lax.dot_general(
                table,
                jnp.concatenate([high, middle, low], axis=1),
                (((1,), (1,)), ((), ())),
                preferred_element_type=F32,
            )
        sums = both[:, XROWS * (x % 2) : XROWS * (x % 2 + 1)]
        packed = jnp.where(
            low_lane,
            sums[0:8] + pltpu.roll(sums[16:24], LANES - 2, 1),
            sums[24:32] + pltpu.roll(sums[8:16], 2, 1),
        )
        out_ref[pl.ds(x, 8, stride=DEPTH), :] = packed
        for half in range(2):
            low = f_ref[pl.ds(x * XROWS + 2 * half, 2), :]
            high = f_ref[pl.ds((x + 1) * XROWS - 4 + 2 * half, 2), :]
            out_ref[pl.ds(32 + 8 * half + 2 * x, 2), :] = jnp.where(
                x2[half : half + 1] < 0, low, high
            )


def cell_quantities(sums):
    low_lane = (lax.broadcasted_iota(jnp.int32, (DEPTH, LANES), 1) & 2) == 0
    low, high = [], []
    for m in range(8):
        own = sums[DEPTH * m : DEPTH * (m + 1)] * WEIGHT
        other = jnp.where(low_lane, pltpu.roll(own, LANES - 2, 1), pltpu.roll(own, 2, 1))
        low.append(jnp.where(low_lane, own, other))
        high.append(jnp.where(low_lane, other, own))
    n = low[0]
    inv = 1.0 / n
    u = [low[1 + k] * inv for k in range(3)]
    pressure = {(0, 0): low[4], (1, 1): low[5], (2, 2): low[6]}
    pressure.update({(0, 1): low[7], (0, 2): high[0], (1, 2): high[1]})
    energy = low[4] + low[5] + low[6]
    speed = u[0] * u[0] + u[1] * u[1] + u[2] * u[2]
    temperature = (energy - n * speed) * inv * (1.0 / 3.0)
    heat = []
    for k in range(3):
        cross = sum(u[j] * pressure[min(j, k), max(j, k)] for j in range(3))
        heat.append(0.5 * (high[2 + k] + high[5 + k] - 2.0 * cross + u[k] * (2.0 * n * speed - energy)))
    inv_t = 1.0 / temperature
    scale = (1.0 - diffusivity_ratio) / 5.0 * inv * inv_t * inv_t
    arg = 2.0 * math.pi * temperature
    norm = n / (arg * jnp.sqrt(arg))
    rate = relaxation_multiplier * n * jnp.exp((1.0 - shear_power_index) * jnp.log(temperature))
    return u + [h * scale for h in heat] + [inv_t, norm, rate]


def blocks_kernel(copies, got_ref, f_ref, pattern_ref, slot_ref, send_ref, a_ref, h_ref):
    sums = got_ref[0, 0:32, :]
    for k in range(1, 16):
        sums = sums + got_ref[k, 0:32, :]
    quantities = cell_quantities(sums)
    filler = jnp.zeros((LANES - DEPTH * len(quantities), LANES), F32)
    columns = jnp.concatenate(quantities + [filler], axis=0).T

    lane = lax.broadcasted_iota(jnp.int32, (8, LANES), 1)
    cell = (lane >> 3) & 7
    source = 16 * sublane((8, LANES)) + 4 * (cell >> 1) + (cell & 1)
    speed = stream_x * SPACING * ((lane & 7).astype(F32) + 0.5)
    chunk_gain = jnp.ones((8, LANES), F32)
    for x in range(DEPTH):
        rate = jnp.broadcast_to(quantities[8][x : x + 1], (8, LANES))
        rate = jnp.take_along_axis(rate, source, axis=1)
        chunk_gain = chunk_gain * (speed / (1.0 + speed + rate))
    for to in range(copies * CHUNKS):
        at = to % CHUNKS
        send_ref[pl.ds(CHUNK_ROWS * to + 16, 1), :] = chunk_gain[at : at + 1]

    found = []
    for half in range(2):
        slot = slot_ref[half]
        lane, group = slot & (LANES - 1), slot >> 7
        value = jnp.zeros((8, LANES), F32)
        for source in range(32):
            piece = got_ref[source // 2, pl.ds(32 + 8 * (source % 2), 8), :]
            value = jnp.where(
                group == source, jnp.take_along_axis(piece, lane, axis=1), value
            )
        found.append(value)

    x1, x2, x3 = pattern_ref[0], pattern_ref[1], pattern_ref[2]
    ahead = x1 > 0
    upward = x2 > 0
    sigma = stream_x * jnp.abs(x1)
    sigma1 = 1.0 + sigma
    flux_y = stream_y * jnp.abs(x2)
    flux_z = stream_z * jnp.abs(x3)
    own = 1.0 - flux_y - flux_z
    row = sublane((8, LANES))
    first_plane = (row & 1) == 0
    lower = row < 4
    here = lax.axis_index("space")
    edge = here == jnp.where(ahead, 0, lax.axis_size("space") - 1)

    ghosts = []
    for x in range(DEPTH):
        four = jnp.concatenate(
            [found[0][2 * x : 2 * x + 2], found[1][2 * x : 2 * x + 2]], axis=0
        )
        ghosts.append(jnp.concatenate([four, four], axis=0))

    for i in range(XROWS // 8):
        a, b, target = [], [], []
        for x in range(DEPTH):
            def column(q):
                at = DEPTH * q + x
                return jnp.broadcast_to(
                    columns[8 * i : 8 * i + 8, at : at + 1], (8, LANES)
                )

            base = x * XROWS + 8 * i
            f = f_ref[pl.ds(base, 8), :]
            c1, c2, c3 = x1 - column(0), x2 - column(1), x3 - column(2)
            square = c1 * c1 + c2 * c2 + c3 * c3
            along = c1 * column(3) + c2 * column(4) + c3 * column(5)
            ratio = square * column(6)
            shakhov = column(7) * jnp.exp(-0.5 * ratio) * (1.0 + along * (ratio - 5.0))
            rate = column(8)

            def ghost(wall):
                mask = pattern_ref[3 + 2 * x + wall]
                return jnp.where(mask == 1.0, ghosts[x], shakhov)

            if i == 0:
                below = jnp.where(lower, ghost(0), pltpu.roll(f, 4, 0))
            else:
                below = f_ref[pl.ds(base - 4, 8), :]
            if i == XROWS // 8 - 1:
                above = jnp.where(lower, pltpu.roll(f, 4, 0), ghost(1))
            else:
                above = f_ref[pl.ds(base + 4, 8), :]
            upwind = jnp.where(upward, below, above)
            other = jnp.where(first_plane, pltpu.roll(f, 7, 0), pltpu.roll(f, 1, 0))
            inverse = 1.0 / (sigma1 + rate)
            a.append(sigma * inverse)
            b.append(
                (own * f + rate * shakhov + flux_y * upwind + flux_z * other) * inverse
            )
            target.append(shakhov)
        order = lambda v, t: jnp.where(ahead, v[t], v[DEPTH - 1 - t])
        a0 = order(a, 0)
        hold = order(b, 0) + jnp.where(edge, a0 * order(target, 0), 0.0)
        gain = jnp.where(edge, 0.0, a0)
        a_ref[pl.ds(8 * i, 8), :] = gain
        h_ref[pl.ds(8 * i, 8), :] = hold
        for t in range(1, DEPTH):
            at = order(a, t)
            gain = at * gain
            hold = at * hold + order(b, t)
            a_ref[pl.ds(t * XROWS + 8 * i, 8), :] = gain
            h_ref[pl.ds(t * XROWS + 8 * i, 8), :] = hold
        for copy in range(copies):
            to = copy * CHUNKS + i // 2
            send_ref[pl.ds(CHUNK_ROWS * to + 8 * (i % 2), 8), :] = hold


def chain_kernel(copies, got_ref, pattern_ref, out_ref, gain_ref, keep_ref):
    blocks = copies * CHUNKS
    ahead = pattern_ref[0] > 0
    which = (jnp.abs(pattern_ref[0]) * (1.0 / SPACING) - 0.5).astype(jnp.int32)
    row = sublane((8, LANES))
    for half in range(2):
        cell = 2 * (2 * half + (row >> 2)) + (row & 1)
        source = 8 * cell + which
        for k in range(blocks):
            gain = jnp.broadcast_to(got_ref[pl.ds(CHUNK_ROWS * k + 16, 1), :], (8, LANES))
            gain_ref[k] = jnp.take_along_axis(gain, source, axis=1)
        enter = jnp.zeros((8, LANES), F32)
        for k in range(blocks):
            keep_ref[half, k] = enter
            back = blocks - 1 - k
            gain = jnp.where(ahead, gain_ref[k], gain_ref[back])
            hold = jnp.where(
                ahead,
                got_ref[pl.ds(CHUNK_ROWS * k + 8 * half, 8), :],
                got_ref[pl.ds(CHUNK_ROWS * back + 8 * half, 8), :],
            )
            enter = gain * enter + hold
    first = lax.axis_index("space") // CHUNKS * CHUNKS
    for half in range(2):
        for x in range(CHUNKS):
            out_ref[x, pl.ds(8 * half, 8), :] = jnp.where(
                ahead, keep_ref[half, first + x], keep_ref[half, blocks - 1 - x - first]
            )


def finish_kernel(enter_ref, a_ref, h_ref, pattern_ref, out_hbm, out_ref, sem):
    ahead = pattern_ref[0] > 0
    copies = []
    for x, mate in ((0, DEPTH - 1), (1, DEPTH - 2)):
        for i in range(XROWS // 8):
            enter = enter_ref[pl.ds(8 * i, 8), :]
            value = []
            for t in (x, mate):
                at = pl.ds(t * XROWS + 8 * i, 8)
                value.append(a_ref[at, :] * enter + h_ref[at, :])
            out_ref[pl.ds(x * XROWS + 8 * i, 8), :] = jnp.where(ahead, value[0], value[1])
            out_ref[pl.ds(mate * XROWS + 8 * i, 8), :] = jnp.where(ahead, value[1], value[0])
        for t in (x, mate):
            rows = pl.ds(t * XROWS, XROWS)
            copies.append(pltpu.make_async_copy(out_ref.at[rows], out_hbm.at[rows], sem.at[t]))
            copies[-1].start()
    for copy in copies:
        copy.wait()


ON_CHIP = pl.BlockSpec(memory_space=pltpu.VMEM)
ANYWHERE = pl.BlockSpec(memory_space=pl.ANY)


def held(x):
    return pltpu.with_memory_space_constraint(x, pltpu.VMEM)


def shards(distribution, wall_mask, grid_point, mirror_slot):
    blocks = lax.axis_size("space")
    copies = blocks // CHUNKS
    f = distribution.reshape(DEPTH, ROWS, PLANES, 2, LANES)
    f = f.transpose(0, 1, 3, 2, 4).reshape(DEPTH * XROWS, LANES)
    point = grid_point.reshape(2, LANES)
    mirror = mirror_slot.reshape(2, LANES)
    wall = wall_mask.transpose(1, 2, 0)

    mine, kept, pattern, slots = pl.pallas_call(
        moments_kernel,
        out_shape=[
            pltpu.VMEM((48, LANES), F32),
            pltpu.VMEM((DEPTH * XROWS, LANES), F32),
            pltpu.VMEM((3 + 2 * DEPTH, 8, LANES), F32),
            pltpu.VMEM((2, 8, LANES), jnp.int32),
        ],
        in_specs=[ANYWHERE] * 4,
        out_specs=[ON_CHIP] * 4,
        scratch_shapes=[
            pltpu.VMEM((2, LANES), jnp.int32),
            pltpu.VMEM((2, LANES), jnp.int32),
            pltpu.VMEM((2, PLANES, DEPTH), jnp.int32),
            pltpu.SemaphoreType.DMA((2,)),
            pltpu.SemaphoreType.DMA((3,)),
        ],
    )(f, point, mirror, wall)
    everyone = lax.all_gather(mine, "vel")
    send, gains, holds = pl.pallas_call(
        lambda *refs: blocks_kernel(copies, *refs),
        out_shape=[
            pltpu.VMEM((blocks * CHUNK_ROWS, LANES), F32),
            pltpu.VMEM((DEPTH * XROWS, LANES), F32),
            pltpu.VMEM((DEPTH * XROWS, LANES), F32),
        ],
        in_specs=[ON_CHIP] * 4,
        out_specs=[ON_CHIP] * 3,
    )(held(everyone), held(kept), held(pattern), held(slots))
    chain = lax.all_to_all(
        send.reshape(blocks, 1, CHUNK_ROWS * LANES), "space", 0, 0, tiled=True
    ).reshape(blocks * CHUNK_ROWS, LANES)
    enters = pl.pallas_call(
        lambda *refs: chain_kernel(copies, *refs),
        out_shape=pltpu.VMEM((CHUNKS, 16, LANES), F32),
        in_specs=[ON_CHIP] * 2,
        out_specs=ON_CHIP,
        scratch_shapes=[
            pltpu.VMEM((blocks, 8, LANES), F32),
            pltpu.VMEM((2, blocks, 8, LANES), F32),
        ],
    )(held(chain), held(pattern))
    lines = [[CHUNKS * z + x for x in range(CHUNKS)] for z in range(copies)]
    enter = lax.all_to_all(enters, "space", 0, 0, axis_index_groups=lines, tiled=True)
    out = pl.pallas_call(
        finish_kernel,
        out_shape=jax.ShapeDtypeStruct((DEPTH * XROWS, LANES), F32),
        in_specs=[ON_CHIP] * 4,
        out_specs=ANYWHERE,
        scratch_shapes=[
            pltpu.VMEM((DEPTH * XROWS, LANES), F32),
            pltpu.SemaphoreType.DMA((DEPTH,)),
        ],
    )(held(enter.reshape(XROWS, LANES)), held(gains), held(holds), held(pattern))
    out = out.reshape(DEPTH, ROWS, 2, PLANES, LANES).transpose(0, 1, 3, 2, 4)
    return out.reshape(DEPTH, ROWS, PLANES, WIDTH)


def solution(mesh):
    placed = (P("space", None, None, "vel"), P("space", None, None), P("vel"), P("vel"))
    return jax.shard_map(
        shards, mesh=mesh, in_specs=placed, out_specs=P("space", None, None, "vel"), check_vma=False
    )
```

```python
import math

import jax
import jax.numpy as jnp
from jax import lax
from jax.experimental import pallas as pl
from jax.experimental.pallas import tpu as pltpu
from jax.sharding import PartitionSpec as P

VS = 16
SPACING = 8.0 / VS
HALF = (VS - 1) / 2.0
WEIGHT = SPACING**3

stream_x = 40.0
stream_y = 0.15
stream_z = 0.05
relaxation_multiplier = 0.05
shear_power_index = 0.81
diffusivity_ratio = 2.0 / 3.0

DEPTH, ROWS, PLANES, WIDTH = 4, 32, 2, 256
LANES = 128
XROWS = ROWS * 2 * PLANES
F32 = jnp.float32
BF16 = jnp.bfloat16

CHUNKS = 8
CHUNK_ROWS = 17

SHARE = 23


def velocity(points):
    first = (points >> 8).astype(F32)
    second = ((points >> 4) & 15).astype(F32)
    third = (points & 15).astype(F32)
    return [(v - HALF) * SPACING for v in (first, second, third)]


def sublane(shape):
    return lax.broadcasted_iota(jnp.int32, shape, 0)


def by_half(pair):
    low = jnp.broadcast_to(pair[0:1], (8, LANES))
    high = jnp.broadcast_to(pair[1:2], (8, LANES))
    return jnp.where((sublane((8, LANES)) & 2) == 0, low, high)


def moments_kernel(
    f_hbm, point_hbm, mirror_hbm, wall_hbm,
    send_ref, f_ref, pattern_ref,
    half_ref, point_ref, mirror_ref, wall_ref, f_sem, small_sem,
):
    small = [
        pltpu.make_async_copy(src, dst, small_sem.at[k])
        for k, (src, dst) in enumerate(
            [(point_hbm, point_ref), (wall_hbm, wall_ref), (mirror_hbm, mirror_ref)]
        )
    ]
    for copy in small:
        copy.start()
    chunks = []
    for x in range(2):
        rows = pl.ds(2 * x * XROWS, 2 * XROWS)
        chunks.append(pltpu.make_async_copy(f_hbm.at[rows], f_ref.at[rows], f_sem.at[x]))
        chunks[x].start()

    small[0].wait()
    points = point_ref[...]
    tables = []
    for half in range(2):
        x1, x2, x3 = velocity(points[half : half + 1])
        square = x1 * x1 + x2 * x2 + x3 * x3
        cubes = [x1 * square, x2 * square, x3 * square]
        coarse = [c.astype(BF16).astype(F32) for c in cubes]
        tables += [
            jnp.ones_like(x1), x1, x2, x3,
            x1 * x1, x2 * x2, x3 * x3, x1 * x2,
            x1 * x3, x2 * x3, *coarse,
            *[c - r for c, r in zip(cubes, coarse)],
        ]
    table = jnp.concatenate(tables, axis=0).astype(BF16)
    table = jnp.concatenate([table] * 3, axis=1)
    low_lane = (lax.broadcasted_iota(jnp.int32, (8, LANES), 1) & 2) == 0
    pairs = velocity(points)
    for k in range(3):
        pattern_ref[k] = by_half(pairs[k])
    small[1].wait()
    for x in range(DEPTH):
        for wall in range(2):
            planes = wall_ref[wall, :, x : x + 1].astype(F32)
            planes = jnp.broadcast_to(planes, (PLANES, LANES))
            pattern_ref[3 + 2 * x + wall] = jnp.concatenate([planes] * 4, axis=0)
    small[2].wait()
    for core in range(2):
        half_ref[core, 21:23, :] = mirror_ref[...].astype(F32)

    x2 = pairs[1]
    for x in range(DEPTH):
        if x % 2 == 0:
            chunks[x // 2].wait()
            f = f_ref[pl.ds(x * XROWS, 2 * XROWS), :]
            high = f.astype(BF16)
            rest = f - high.astype(F32)
            middle = rest.astype(BF16)
            low = (rest - middle.astype(F32)).astype(BF16)
            both = lax.dot_general(
                table,
                jnp.concatenate([high, middle, low], axis=1),
                (((1,), (1,)), ((), ())),
                preferred_element_type=F32,
            )
        sums = both[:, XROWS * (x % 2) : XROWS * (x % 2 + 1)]
        packed = jnp.where(
            low_lane,
            sums[0:8] + pltpu.roll(sums[16:24], LANES - 2, 1),
            sums[24:32] + pltpu.roll(sums[8:16], 2, 1),
        )
        core, second = divmod(x, 2)
        tail = packed[5:8]
        half_ref[core, pl.ds(5 * second, 2), :] = packed[0:2]
        half_ref[core, pl.ds(5 * second + 2, 3), :] = packed[2:5] + jnp.where(
            low_lane[0:3], 0.0, tail
        )
        if second:
            half_ref[core, 10:13, :] = jnp.where(
                low_lane[0:3], before, pltpu.roll(packed, 2, 1)[5:8]
            )
        before = tail
        for half in range(2):
            low = f_ref[pl.ds(x * XROWS + 2 * half, 2), :]
            high = f_ref[pl.ds((x + 1) * XROWS - 4 + 2 * half, 2), :]
            half_ref[core, pl.ds(13 + 4 * half + 2 * second, 2), :] = jnp.where(
                x2[half : half + 1] < 0, low, high
            )
        if second:
            for to in range(core, send_ref.shape[0] // SHARE, 2):
                send_ref[pl.ds(SHARE * to, SHARE), :] = half_ref[core, 0:SHARE, :]


def cell_quantities(sums):
    low_lane = (lax.broadcasted_iota(jnp.int32, (2, LANES), 1) & 2) == 0
    low, high = [], []
    for m in range(8):
        if m < 5:
            own = jnp.concatenate([sums[m : m + 1], sums[5 + m : 6 + m]], axis=0)
            own = own * WEIGHT
            other = jnp.where(
                low_lane, pltpu.roll(own, LANES - 2, 1), pltpu.roll(own, 2, 1)
            )
            low.append(jnp.where(low_lane, own, other))
            high.append(jnp.where(low_lane, other, own))
        else:
            own = jnp.broadcast_to(sums[5 + m : 6 + m], (2, LANES)) * WEIGHT
            first = jnp.where(low_lane, own, pltpu.roll(own, 2, 1))
            second = jnp.where(low_lane, pltpu.roll(own, LANES - 2, 1), own)
            low.append(jnp.where(sublane((2, LANES)) == 0, first, second))
    n = low[0]
    inv = 1.0 / n
    u = [low[1 + k] * inv for k in range(3)]
    pressure = {(0, 0): low[4], (1, 1): low[5], (2, 2): low[6]}
    pressure.update({(0, 1): low[7], (0, 2): high[0], (1, 2): high[1]})
    energy = low[4] + low[5] + low[6]
    speed = u[0] * u[0] + u[1] * u[1] + u[2] * u[2]
    temperature = (energy - n * speed) * inv * (1.0 / 3.0)
    heat = []
    for k in range(3):
        cross = sum(u[j] * pressure[min(j, k), max(j, k)] for j in range(3))
        heat.append(0.5 * (high[2 + k] - 2.0 * cross + u[k] * (2.0 * n * speed - energy)))
    inv_t = 1.0 / temperature
    scale = (1.0 - diffusivity_ratio) / 5.0 * inv * inv_t * inv_t
    arg = 2.0 * math.pi * temperature
    norm = n / (arg * jnp.sqrt(arg))
    rate = relaxation_multiplier * n * jnp.exp((1.0 - shear_power_index) * jnp.log(temperature))
    return u + [h * scale for h in heat] + [inv_t, norm, rate]


def cells_kernel(sources, got_ref, out_ref):
    sums = got_ref[pl.ds(0, 16), :]
    for k in range(1, sources):
        sums = sums + got_ref[pl.ds(SHARE * k, 16), :]
    quantities = cell_quantities(sums)
    filler = jnp.zeros((24 - 2 * len(quantities), LANES), F32)
    table = jnp.concatenate(quantities + [filler], axis=0)
    for k in range(3):
        out_ref[k] = table[8 * k : 8 * k + 8]

    upper = (sublane((8, LANES)) >> 2) & 1
    even = lax.axis_index("vel") // 2 * 2
    lanes, kept, rolled, values = [], [], [], []
    for core in range(2):
        at = SHARE * (even + core) + 21
        first = jnp.broadcast_to(got_ref[pl.ds(at, 1), :], (8, LANES))
        second = jnp.broadcast_to(got_ref[pl.ds(at + 1, 1), :], (8, LANES))
        slot = jnp.where(upper == 0, first, second).astype(jnp.int32)
        lanes.append(slot & (LANES - 1))
        kept.append((slot >> 7) - upper)
        rolled.append((slot >> 7) + upper)
        values.append(jnp.zeros((8, LANES), F32))
    for k in range(sources):
        piece = got_ref[pl.ds(SHARE * k + 13, 8), :]
        swapped = pltpu.roll(piece, 4, 0)
        for core in range(2):
            there = jnp.take_along_axis(piece, lanes[core], axis=1)
            across = jnp.take_along_axis(swapped, lanes[core], axis=1)
            value = jnp.where(kept[core] == 2 * k, there, values[core])
            values[core] = jnp.where(rolled[core] == 2 * k + 1, across, value)
    for core in range(2):
        out_ref[3 + core] = values[core]


def blocks_kernel(copies, got_ref, f_ref, pattern_ref, send_ref, a_ref, h_ref):
    parts = [got_ref[half, k] for half in range(2) for k in range(3)]
    filler = jnp.zeros((LANES - 48, LANES), F32)
    columns = jnp.concatenate(parts + [filler], axis=0).T
    core = lax.axis_index("vel") % 2
    found = [got_ref[half, 3 + core] for half in range(2)]

    lane = lax.broadcasted_iota(jnp.int32, (8, LANES), 1)
    cell = (lane >> 3) & 7
    source = 16 * sublane((8, LANES)) + 4 * (cell >> 1) + (cell & 1)
    speed = stream_x * SPACING * ((lane & 7).astype(F32) + 0.5)
    chunk_gain = jnp.ones((8, LANES), F32)
    for x in range(DEPTH):
        rate = jnp.broadcast_to(parts[3 * (x // 2) + 2][x % 2 : x % 2 + 1], (8, LANES))
        rate = jnp.take_along_axis(rate, source, axis=1)
        chunk_gain = chunk_gain * (speed / (1.0 + speed + rate))
    for to in range(copies * CHUNKS):
        at = to % CHUNKS
        send_ref[pl.ds(CHUNK_ROWS * to + 16, 1), :] = chunk_gain[at : at + 1]

    x1, x2, x3 = pattern_ref[0], pattern_ref[1], pattern_ref[2]
    ahead = x1 > 0
    upward = x2 > 0
    sigma = stream_x * jnp.abs(x1)
    sigma1 = 1.0 + sigma
    flux_y = stream_y * jnp.abs(x2)
    flux_z = stream_z * jnp.abs(x3)
    own = 1.0 - flux_y - flux_z
    row = sublane((8, LANES))
    first_plane = (row & 1) == 0
    lower = row < 4
    here = lax.axis_index("space")
    edge = here == jnp.where(ahead, 0, lax.axis_size("space") - 1)

    ghosts = []
    for x in range(DEPTH):
        wall = found[x // 2]
        at = 2 * (x % 2)
        four = jnp.concatenate([wall[at : at + 2], wall[at + 4 : at + 6]], axis=0)
        ghosts.append(jnp.concatenate([four, four], axis=0))

    for i in range(XROWS // 8):
        a, b, target = [], [], []
        for x in range(DEPTH):
            def column(q):
                at = 24 * (x // 2) + 2 * q + x % 2
                return jnp.broadcast_to(
                    columns[8 * i : 8 * i + 8, at : at + 1], (8, LANES)
                )

            base = x * XROWS + 8 * i
            f = f_ref[pl.ds(base, 8), :]
            c1, c2, c3 = x1 - column(0), x2 - column(1), x3 - column(2)
            square = c1 * c1 + c2 * c2 + c3 * c3
            along = c1 * column(3) + c2 * column(4) + c3 * column(5)
            ratio = square * column(6)
            shakhov = column(7) * jnp.exp(-0.5 * ratio) * (1.0 + along * (ratio - 5.0))
            rate = column(8)

            def ghost(wall):
                mask = pattern_ref[3 + 2 * x + wall]
                return jnp.where(mask == 1.0, ghosts[x], shakhov)

            if i == 0:
                below = jnp.where(lower, ghost(0), pltpu.roll(f, 4, 0))
            else:
                below = f_ref[pl.ds(base - 4, 8), :]
            if i == XROWS // 8 - 1:
                above = jnp.where(lower, pltpu.roll(f, 4, 0), ghost(1))
            else:
                above = f_ref[pl.ds(base + 4, 8), :]
            upwind = jnp.where(upward, below, above)
            other = jnp.where(first_plane, pltpu.roll(f, 7, 0), pltpu.roll(f, 1, 0))
            inverse = 1.0 / (sigma1 + rate)
            a.append(sigma * inverse)
            b.append(
                (own * f + rate * shakhov + flux_y * upwind + flux_z * other) * inverse
            )
            target.append(shakhov)
        order = lambda v, t: jnp.where(ahead, v[t], v[DEPTH - 1 - t])
        a0 = order(a, 0)
        hold = order(b, 0) + jnp.where(edge, a0 * order(target, 0), 0.0)
        gain = jnp.where(edge, 0.0, a0)
        a_ref[pl.ds(8 * i, 8), :] = gain
        h_ref[pl.ds(8 * i, 8), :] = hold
        for t in range(1, DEPTH):
            at = order(a, t)
            gain = at * gain
            hold = at * hold + order(b, t)
            a_ref[pl.ds(t * XROWS + 8 * i, 8), :] = gain
            h_ref[pl.ds(t * XROWS + 8 * i, 8), :] = hold
        for copy in range(copies):
            to = copy * CHUNKS + i // 2
            send_ref[pl.ds(CHUNK_ROWS * to + 8 * (i % 2), 8), :] = hold


def chain_kernel(copies, got_ref, pattern_ref, out_ref, gain_ref, keep_ref):
    blocks = copies * CHUNKS
    ahead = pattern_ref[0] > 0
    which = (jnp.abs(pattern_ref[0]) * (1.0 / SPACING) - 0.5).astype(jnp.int32)
    row = sublane((8, LANES))
    for half in range(2):
        cell = 2 * (2 * half + (row >> 2)) + (row & 1)
        source = 8 * cell + which
        for k in range(blocks):
            gain = jnp.broadcast_to(got_ref[pl.ds(CHUNK_ROWS * k + 16, 1), :], (8, LANES))
            gain_ref[k] = jnp.take_along_axis(gain, source, axis=1)
        enter = jnp.zeros((8, LANES), F32)
        for k in range(blocks):
            keep_ref[half, k] = enter
            back = blocks - 1 - k
            gain = jnp.where(ahead, gain_ref[k], gain_ref[back])
            hold = jnp.where(
                ahead,
                got_ref[pl.ds(CHUNK_ROWS * k + 8 * half, 8), :],
                got_ref[pl.ds(CHUNK_ROWS * back + 8 * half, 8), :],
            )
            enter = gain * enter + hold
    first = lax.axis_index("space") // CHUNKS * CHUNKS
    for half in range(2):
        for x in range(CHUNKS):
            out_ref[x, pl.ds(8 * half, 8), :] = jnp.where(
                ahead, keep_ref[half, first + x], keep_ref[half, blocks - 1 - x - first]
            )


def finish_kernel(enter_ref, a_ref, h_ref, pattern_ref, out_hbm, out_ref, sem):
    ahead = pattern_ref[0] > 0
    copies = []
    for x, mate in ((0, DEPTH - 1), (1, DEPTH - 2)):
        for i in range(XROWS // 8):
            enter = enter_ref[pl.ds(8 * i, 8), :]
            value = []
            for t in (x, mate):
                at = pl.ds(t * XROWS + 8 * i, 8)
                value.append(a_ref[at, :] * enter + h_ref[at, :])
            out_ref[pl.ds(x * XROWS + 8 * i, 8), :] = jnp.where(ahead, value[0], value[1])
            out_ref[pl.ds(mate * XROWS + 8 * i, 8), :] = jnp.where(ahead, value[1], value[0])
        for t in (x, mate):
            rows = pl.ds(t * XROWS, XROWS)
            copies.append(pltpu.make_async_copy(out_ref.at[rows], out_hbm.at[rows], sem.at[t]))
            copies[-1].start()
    for copy in copies:
        copy.wait()


ON_CHIP = pl.BlockSpec(memory_space=pltpu.VMEM)
ANYWHERE = pl.BlockSpec(memory_space=pl.ANY)


def held(x):
    return pltpu.with_memory_space_constraint(x, pltpu.VMEM)


def shards(distribution, wall_mask, grid_point, mirror_slot):
    blocks = lax.axis_size("space")
    copies = blocks // CHUNKS
    f = distribution.reshape(DEPTH, ROWS, PLANES, 2, LANES)
    f = f.transpose(0, 1, 3, 2, 4).reshape(DEPTH * XROWS, LANES)
    point = grid_point.reshape(2, LANES)
    mirror = mirror_slot.reshape(2, LANES)
    wall = wall_mask.transpose(1, 2, 0)

    sources = lax.axis_size("vel")
    shares, kept, pattern = pl.pallas_call(
        moments_kernel,
        out_shape=[
            pltpu.VMEM((sources * SHARE, LANES), F32),
            pltpu.VMEM((DEPTH * XROWS, LANES), F32),
            pltpu.VMEM((3 + 2 * DEPTH, 8, LANES), F32),
        ],
        in_specs=[ANYWHERE] * 4,
        out_specs=[ON_CHIP] * 3,
        scratch_shapes=[
            pltpu.VMEM((2, 24, LANES), F32),
            pltpu.VMEM((2, LANES), jnp.int32),
            pltpu.VMEM((2, LANES), jnp.int32),
            pltpu.VMEM((2, PLANES, DEPTH), jnp.int32),
            pltpu.SemaphoreType.DMA((2,)),
            pltpu.SemaphoreType.DMA((3,)),
        ],
    )(f, point, mirror, wall)
    partial = lax.all_to_all(
        shares.reshape(sources, 1, SHARE * LANES), "vel", 0, 0, tiled=True
    ).reshape(sources * SHARE, LANES)
    cells = pl.pallas_call(
        lambda *refs: cells_kernel(sources, *refs),
        out_shape=pltpu.VMEM((5, 8, LANES), F32),
        in_specs=[ON_CHIP],
        out_specs=ON_CHIP,
    )(held(partial))
    pairs = [[k, k + 1] for k in range(0, sources, 2)]
    everyone = lax.all_gather(cells, "vel", axis_index_groups=pairs)
    send, gains, holds = pl.pallas_call(
        lambda *refs: blocks_kernel(copies, *refs),
        out_shape=[
            pltpu.VMEM((blocks * CHUNK_ROWS, LANES), F32),
            pltpu.VMEM((DEPTH * XROWS, LANES), F32),
            pltpu.VMEM((DEPTH * XROWS, LANES), F32),
        ],
        in_specs=[ON_CHIP] * 3,
        out_specs=[ON_CHIP] * 3,
    )(held(everyone), held(kept), held(pattern))
    chain = lax.all_to_all(
        send.reshape(blocks, 1, CHUNK_ROWS * LANES), "space", 0, 0, tiled=True
    ).reshape(blocks * CHUNK_ROWS, LANES)
    enters = pl.pallas_call(
        lambda *refs: chain_kernel(copies, *refs),
        out_shape=pltpu.VMEM((CHUNKS, 16, LANES), F32),
        in_specs=[ON_CHIP] * 2,
        out_specs=ON_CHIP,
        scratch_shapes=[
            pltpu.VMEM((blocks, 8, LANES), F32),
            pltpu.VMEM((2, blocks, 8, LANES), F32),
        ],
    )(held(chain), held(pattern))
    lines = [[CHUNKS * z + x for x in range(CHUNKS)] for z in range(copies)]
    enter = lax.all_to_all(enters, "space", 0, 0, axis_index_groups=lines, tiled=True)
    out = pl.pallas_call(
        finish_kernel,
        out_shape=jax.ShapeDtypeStruct((DEPTH * XROWS, LANES), F32),
        in_specs=[ON_CHIP] * 4,
        out_specs=ANYWHERE,
        scratch_shapes=[
            pltpu.VMEM((DEPTH * XROWS, LANES), F32),
            pltpu.SemaphoreType.DMA((DEPTH,)),
        ],
    )(held(enter.reshape(XROWS, LANES)), held(gains), held(holds), held(pattern))
    out = out.reshape(DEPTH, ROWS, 2, PLANES, LANES).transpose(0, 1, 3, 2, 4)
    return out.reshape(DEPTH, ROWS, PLANES, WIDTH)


def solution(mesh):
    placed = (P("space", None, None, "vel"), P("space", None, None), P("vel"), P("vel"))
    return jax.shard_map(
        shards, mesh=mesh, in_specs=placed, out_specs=P("space", None, None, "vel"), check_vma=False
    )
```

```python
import math

import jax
import jax.numpy as jnp
from jax import lax
from jax.experimental import pallas as pl
from jax.experimental.pallas import tpu as pltpu
from jax.sharding import PartitionSpec as P

VS = 16
SPACING = 8.0 / VS
HALF = (VS - 1) / 2.0
WEIGHT = SPACING**3

stream_x = 40.0
stream_y = 0.15
stream_z = 0.05
relaxation_multiplier = 0.05
shear_power_index = 0.81
diffusivity_ratio = 2.0 / 3.0

DEPTH, ROWS, PLANES, WIDTH = 4, 32, 2, 256
LANES = 128
XROWS = ROWS * 2 * PLANES
F32 = jnp.float32
BF16 = jnp.bfloat16

CHUNKS = 8
CHUNK_ROWS = 17


def velocity(points):
    first = (points >> 8).astype(F32)
    second = ((points >> 4) & 15).astype(F32)
    third = (points & 15).astype(F32)
    return [(v - HALF) * SPACING for v in (first, second, third)]


def sublane(shape):
    return lax.broadcasted_iota(jnp.int32, shape, 0)


def by_half(pair):
    low = jnp.broadcast_to(pair[0:1], (8, LANES))
    high = jnp.broadcast_to(pair[1:2], (8, LANES))
    return jnp.where((sublane((8, LANES)) & 2) == 0, low, high)


def moments_kernel(
    f_hbm, point_hbm, mirror_hbm, wall_hbm,
    out_ref, f_ref, pattern_ref, slot_ref, weight_ref,
    point_ref, mirror_ref, wall_ref, f_sem, small_sem,
):
    small = [
        pltpu.make_async_copy(src, dst, small_sem.at[k])
        for k, (src, dst) in enumerate(
            [(point_hbm, point_ref), (wall_hbm, wall_ref), (mirror_hbm, mirror_ref)]
        )
    ]
    for copy in small:
        copy.start()
    chunks = []
    for x in range(2):
        rows = pl.ds(2 * x * XROWS, 2 * XROWS)
        chunks.append(pltpu.make_async_copy(f_hbm.at[rows], f_ref.at[rows], f_sem.at[x]))
        chunks[x].start()

    small[0].wait()
    points = point_ref[...]
    tables = []
    for half in range(2):
        x1, x2, x3 = velocity(points[half : half + 1])
        square = x1 * x1 + x2 * x2 + x3 * x3
        cubes = [x1 * square, x2 * square, x3 * square]
        coarse = [c.astype(BF16).astype(F32) for c in cubes]
        tables += [
            jnp.ones_like(x1), x1, x2, x3,
            x1 * x1, x2 * x2, x3 * x3, x1 * x2,
            x1 * x3, x2 * x3, *coarse,
            *[c - r for c, r in zip(cubes, coarse)],
        ]
    weights = []
    for half in range(2):
        x1, x2, x3 = velocity(points[half : half + 1])
        square = x1 * x1 + x2 * x2 + x3 * x3
        coarse = square.astype(BF16).astype(F32)
        one, zero = jnp.ones_like(x1), jnp.zeros_like(x1)
        left = [one, x1, x2, x3, coarse, square - coarse] + [zero] * 10
        right = [zero] * 6 + [one, x1, x2, x3] + [zero] * 6
        weights += [jnp.concatenate(pair, axis=1) for pair in zip(left, right)]
    weights = jnp.concatenate(weights, axis=0).astype(BF16)
    weight_ref[...] = jnp.concatenate([weights] * 3 + [jnp.zeros_like(weights)], axis=0)
    table = jnp.concatenate(tables, axis=0).astype(BF16)
    table = jnp.concatenate([table] * 3, axis=1)
    low_lane = (lax.broadcasted_iota(jnp.int32, (8, LANES), 1) & 2) == 0
    pairs = velocity(points)
    for k in range(3):
        pattern_ref[k] = by_half(pairs[k])
    small[1].wait()
    for x in range(DEPTH):
        for wall in range(2):
            planes = wall_ref[wall, :, x : x + 1].astype(F32)
            planes = jnp.broadcast_to(planes, (PLANES, LANES))
            pattern_ref[3 + 2 * x + wall] = jnp.concatenate([planes] * 4, axis=0)
    small[2].wait()
    for half in range(2):
        slot_ref[half] = jnp.broadcast_to(mirror_ref[half : half + 1], (8, LANES))

    x2 = pairs[1]
    for x in range(DEPTH):
        if x % 2 == 0:
            chunks[x // 2].wait()
            f = f_ref[pl.ds(x * XROWS, 2 * XROWS), :]
            high = f.astype(BF16)
            rest = f - high.astype(F32)
            middle = rest.astype(BF16)
            low = (rest - middle.astype(F32)).astype(BF16)
            both = lax.dot_general(
                table,
                jnp.concatenate([high, middle, low], axis=1),
                (((1,), (1,)), ((), ())),
                preferred_element_type=F32,
            )
        sums = both[:, XROWS * (x % 2) : XROWS * (x % 2 + 1)]
        packed = jnp.where(
            low_lane,
            sums[0:8] + pltpu.roll(sums[16:24], LANES - 2, 1),
            sums[24:32] + pltpu.roll(sums[8:16], 2, 1),
        )
        out_ref[pl.ds(x, 8, stride=DEPTH), :] = packed
        for half in range(2):
            low = f_ref[pl.ds(x * XROWS + 2 * half, 2), :]
            high = f_ref[pl.ds((x + 1) * XROWS - 4 + 2 * half, 2), :]
            out_ref[pl.ds(32 + 8 * half + 2 * x, 2), :] = jnp.where(
                x2[half : half + 1] < 0, low, high
            )


def cell_quantities(sums):
    low_lane = (lax.broadcasted_iota(jnp.int32, (DEPTH, LANES), 1) & 2) == 0
    low, high = [], []
    for m in range(8):
        own = sums[DEPTH * m : DEPTH * (m + 1)] * WEIGHT
        other = jnp.where(low_lane, pltpu.roll(own, LANES - 2, 1), pltpu.roll(own, 2, 1))
        low.append(jnp.where(low_lane, own, other))
        high.append(jnp.where(low_lane, other, own))
    n = low[0]
    inv = 1.0 / n
    u = [low[1 + k] * inv for k in range(3)]
    pressure = {(0, 0): low[4], (1, 1): low[5], (2, 2): low[6]}
    pressure.update({(0, 1): low[7], (0, 2): high[0], (1, 2): high[1]})
    energy = low[4] + low[5] + low[6]
    speed = u[0] * u[0] + u[1] * u[1] + u[2] * u[2]
    temperature = (energy - n * speed) * inv * (1.0 / 3.0)
    heat = []
    for k in range(3):
        cross = sum(u[j] * pressure[min(j, k), max(j, k)] for j in range(3))
        heat.append(0.5 * (high[2 + k] + high[5 + k] - 2.0 * cross + u[k] * (2.0 * n * speed - energy)))
    inv_t = 1.0 / temperature
    scale = (1.0 - diffusivity_ratio) / 5.0 * inv * inv_t * inv_t
    arg = 2.0 * math.pi * temperature
    norm = n / (arg * jnp.sqrt(arg))
    heat = [h * scale for h in heat]
    rate = relaxation_multiplier * n * jnp.exp((1.0 - shear_power_index) * jnp.log(temperature))
    ratio = [speed * inv_t] + [-2.0 * v * inv_t for v in u] + [inv_t]
    along = [-(u[0] * heat[0] + u[1] * heat[1] + u[2] * heat[2])] + heat
    return ratio + along, norm, rate


def blocks_kernel(
    copies, got_ref, f_ref, pattern_ref, slot_ref, weight_ref, send_ref, a_ref, h_ref, poly_ref
):
    sums = got_ref[0, 0:32, :]
    for k in range(1, 16):
        sums = sums + got_ref[k, 0:32, :]
    coefficients, norm, rates = cell_quantities(sums)
    parts = [[], [], []]
    for c in coefficients:
        for part in parts:
            piece = c.astype(BF16).astype(F32)
            part.append(piece)
            c = c - piece
    rows = parts[0] + parts[1] + parts[2] + [norm, rates]
    filler = jnp.zeros((LANES - DEPTH * len(rows), LANES), F32)
    columns = jnp.concatenate(rows + [filler], axis=0).T

    lane = lax.broadcasted_iota(jnp.int32, (8, LANES), 1)
    term = lane & 15
    term = jnp.where(term > 9, 0, jnp.where(term > 4, term - 1, term))
    part = jnp.where(lane < 96, lane >> 5, 0)
    source = DEPTH * (len(coefficients) * part + term)
    same = ((sublane((8, LANES)) >> 1) & 1) == ((lane >> 4) & 1)
    left = []
    for x in range(DEPTH):
        for i in range(XROWS // 8):
            value = jnp.take_along_axis(columns[8 * i : 8 * i + 8], source + x, axis=1)
            left.append(jnp.where(same, value, 0.0))
    poly_ref[...] = lax.dot_general(
        jnp.concatenate(left, axis=0).astype(BF16),
        weight_ref[...],
        (((1,), (0,)), ((), ())),
        preferred_element_type=F32,
    )

    lane = lax.broadcasted_iota(jnp.int32, (8, LANES), 1)
    cell = (lane >> 3) & 7
    source = 16 * sublane((8, LANES)) + 4 * (cell >> 1) + (cell & 1)
    speed = stream_x * SPACING * ((lane & 7).astype(F32) + 0.5)
    chunk_gain = jnp.ones((8, LANES), F32)
    for x in range(DEPTH):
        rate = jnp.broadcast_to(rates[x : x + 1], (8, LANES))
        rate = jnp.take_along_axis(rate, source, axis=1)
        chunk_gain = chunk_gain * (speed / (1.0 + speed + rate))
    for to in range(copies * CHUNKS):
        at = to % CHUNKS
        send_ref[pl.ds(CHUNK_ROWS * to + 16, 1), :] = chunk_gain[at : at + 1]

    found = []
    for half in range(2):
        slot = slot_ref[half]
        lane, group = slot & (LANES - 1), slot >> 7
        value = jnp.zeros((8, LANES), F32)
        for source in range(32):
            piece = got_ref[source // 2, pl.ds(32 + 8 * (source % 2), 8), :]
            value = jnp.where(
                group == source, jnp.take_along_axis(piece, lane, axis=1), value
            )
        found.append(value)

    x1, x2, x3 = pattern_ref[0], pattern_ref[1], pattern_ref[2]
    ahead = x1 > 0
    upward = x2 > 0
    sigma = stream_x * jnp.abs(x1)
    sigma1 = 1.0 + sigma
    flux_y = stream_y * jnp.abs(x2)
    flux_z = stream_z * jnp.abs(x3)
    own = 1.0 - flux_y - flux_z
    row = sublane((8, LANES))
    first_plane = (row & 1) == 0
    lower = row < 4
    here = lax.axis_index("space")
    edge = here == jnp.where(ahead, 0, lax.axis_size("space") - 1)

    ghosts = []
    for x in range(DEPTH):
        four = jnp.concatenate(
            [found[0][2 * x : 2 * x + 2], found[1][2 * x : 2 * x + 2]], axis=0
        )
        ghosts.append(jnp.concatenate([four, four], axis=0))

    for i in range(XROWS // 8):
        a, b, target = [], [], []
        for x in range(DEPTH):
            def column(q):
                at = DEPTH * (3 * len(coefficients) + q) + x
                return jnp.broadcast_to(
                    columns[8 * i : 8 * i + 8, at : at + 1], (8, LANES)
                )

            base = x * XROWS + 8 * i
            f = f_ref[pl.ds(base, 8), :]
            ratio = poly_ref[pl.ds(base, 8), 0:LANES]
            along = poly_ref[pl.ds(base, 8), LANES : 2 * LANES]
            shakhov = column(0) * jnp.exp(-0.5 * ratio) * (1.0 + along * (ratio - 5.0))
            rate = column(1)

            def ghost(wall):
                mask = pattern_ref[3 + 2 * x + wall]
                return jnp.where(mask == 1.0, ghosts[x], shakhov)

            if i == 0:
                below = jnp.where(lower, ghost(0), pltpu.roll(f, 4, 0))
            else:
                below = f_ref[pl.ds(base - 4, 8), :]
            if i == XROWS // 8 - 1:
                above = jnp.where(lower, pltpu.roll(f, 4, 0), ghost(1))
            else:
                above = f_ref[pl.ds(base + 4, 8), :]
            upwind = jnp.where(upward, below, above)
            other = jnp.where(first_plane, pltpu.roll(f, 7, 0), pltpu.roll(f, 1, 0))
            inverse = 1.0 / (sigma1 + rate)
            a.append(sigma * inverse)
            b.append(
                (own * f + rate * shakhov + flux_y * upwind + flux_z * other) * inverse
            )
            target.append(shakhov)
        order = lambda v, t: jnp.where(ahead, v[t], v[DEPTH - 1 - t])
        a0 = order(a, 0)
        hold = order(b, 0) + jnp.where(edge, a0 * order(target, 0), 0.0)
        gain = jnp.where(edge, 0.0, a0)
        a_ref[pl.ds(8 * i, 8), :] = gain
        h_ref[pl.ds(8 * i, 8), :] = hold
        for t in range(1, DEPTH):
            at = order(a, t)
            gain = at * gain
            hold = at * hold + order(b, t)
            a_ref[pl.ds(t * XROWS + 8 * i, 8), :] = gain
            h_ref[pl.ds(t * XROWS + 8 * i, 8), :] = hold
        for copy in range(copies):
            to = copy * CHUNKS + i // 2
            send_ref[pl.ds(CHUNK_ROWS * to + 8 * (i % 2), 8), :] = hold


def chain_kernel(copies, got_ref, pattern_ref, out_ref, gain_ref, keep_ref):
    blocks = copies * CHUNKS
    ahead = pattern_ref[0] > 0
    which = (jnp.abs(pattern_ref[0]) * (1.0 / SPACING) - 0.5).astype(jnp.int32)
    row = sublane((8, LANES))
    for half in range(2):
        cell = 2 * (2 * half + (row >> 2)) + (row & 1)
        source = 8 * cell + which
        for k in range(blocks):
            gain = jnp.broadcast_to(got_ref[pl.ds(CHUNK_ROWS * k + 16, 1), :], (8, LANES))
            gain_ref[k] = jnp.take_along_axis(gain, source, axis=1)
        enter = jnp.zeros((8, LANES), F32)
        for k in range(blocks):
            keep_ref[half, k] = enter
            back = blocks - 1 - k
            gain = jnp.where(ahead, gain_ref[k], gain_ref[back])
            hold = jnp.where(
                ahead,
                got_ref[pl.ds(CHUNK_ROWS * k + 8 * half, 8), :],
                got_ref[pl.ds(CHUNK_ROWS * back + 8 * half, 8), :],
            )
            enter = gain * enter + hold
    first = lax.axis_index("space") // CHUNKS * CHUNKS
    for half in range(2):
        for x in range(CHUNKS):
            out_ref[x, pl.ds(8 * half, 8), :] = jnp.where(
                ahead, keep_ref[half, first + x], keep_ref[half, blocks - 1 - x - first]
            )


def finish_kernel(enter_ref, a_ref, h_ref, pattern_ref, out_hbm, out_ref, sem):
    ahead = pattern_ref[0] > 0
    copies = []
    for x, mate in ((0, DEPTH - 1), (1, DEPTH - 2)):
        for i in range(XROWS // 8):
            enter = enter_ref[pl.ds(8 * i, 8), :]
            value = []
            for t in (x, mate):
                at = pl.ds(t * XROWS + 8 * i, 8)
                value.append(a_ref[at, :] * enter + h_ref[at, :])
            out_ref[pl.ds(x * XROWS + 8 * i, 8), :] = jnp.where(ahead, value[0], value[1])
            out_ref[pl.ds(mate * XROWS + 8 * i, 8), :] = jnp.where(ahead, value[1], value[0])
        for t in (x, mate):
            rows = pl.ds(t * XROWS, XROWS)
            copies.append(pltpu.make_async_copy(out_ref.at[rows], out_hbm.at[rows], sem.at[t]))
            copies[-1].start()
    for copy in copies:
        copy.wait()


ON_CHIP = pl.BlockSpec(memory_space=pltpu.VMEM)
ANYWHERE = pl.BlockSpec(memory_space=pl.ANY)


def held(x):
    return pltpu.with_memory_space_constraint(x, pltpu.VMEM)


def shards(distribution, wall_mask, grid_point, mirror_slot):
    blocks = lax.axis_size("space")
    copies = blocks // CHUNKS
    f = distribution.reshape(DEPTH, ROWS, PLANES, 2, LANES)
    f = f.transpose(0, 1, 3, 2, 4).reshape(DEPTH * XROWS, LANES)
    point = grid_point.reshape(2, LANES)
    mirror = mirror_slot.reshape(2, LANES)
    wall = wall_mask.transpose(1, 2, 0)

    mine, kept, pattern, slots, weights = pl.pallas_call(
        moments_kernel,
        out_shape=[
            pltpu.VMEM((48, LANES), F32),
            pltpu.VMEM((DEPTH * XROWS, LANES), F32),
            pltpu.VMEM((3 + 2 * DEPTH, 8, LANES), F32),
            pltpu.VMEM((2, 8, LANES), jnp.int32),
            pltpu.VMEM((LANES, 2 * LANES), BF16),
        ],
        in_specs=[ANYWHERE] * 4,
        out_specs=[ON_CHIP] * 5,
        scratch_shapes=[
            pltpu.VMEM((2, LANES), jnp.int32),
            pltpu.VMEM((2, LANES), jnp.int32),
            pltpu.VMEM((2, PLANES, DEPTH), jnp.int32),
            pltpu.SemaphoreType.DMA((2,)),
            pltpu.SemaphoreType.DMA((3,)),
        ],
    )(f, point, mirror, wall)
    everyone = lax.all_gather(mine, "vel")
    send, gains, holds = pl.pallas_call(
        lambda *refs: blocks_kernel(copies, *refs),
        out_shape=[
            pltpu.VMEM((blocks * CHUNK_ROWS, LANES), F32),
            pltpu.VMEM((DEPTH * XROWS, LANES), F32),
            pltpu.VMEM((DEPTH * XROWS, LANES), F32),
        ],
        in_specs=[ON_CHIP] * 5,
        out_specs=[ON_CHIP] * 3,
        scratch_shapes=[pltpu.VMEM((DEPTH * XROWS, 2 * LANES), F32)],
    )(held(everyone), held(kept), held(pattern), held(slots), held(weights))
    chain = lax.all_to_all(
        send.reshape(blocks, 1, CHUNK_ROWS * LANES), "space", 0, 0, tiled=True
    ).reshape(blocks * CHUNK_ROWS, LANES)
    enters = pl.pallas_call(
        lambda *refs: chain_kernel(copies, *refs),
        out_shape=pltpu.VMEM((CHUNKS, 16, LANES), F32),
        in_specs=[ON_CHIP] * 2,
        out_specs=ON_CHIP,
        scratch_shapes=[
            pltpu.VMEM((blocks, 8, LANES), F32),
            pltpu.VMEM((2, blocks, 8, LANES), F32),
        ],
    )(held(chain), held(pattern))
    lines = [[CHUNKS * z + x for x in range(CHUNKS)] for z in range(copies)]
    enter = lax.all_to_all(enters, "space", 0, 0, axis_index_groups=lines, tiled=True)
    out = pl.pallas_call(
        finish_kernel,
        out_shape=jax.ShapeDtypeStruct((DEPTH * XROWS, LANES), F32),
        in_specs=[ON_CHIP] * 4,
        out_specs=ANYWHERE,
        scratch_shapes=[
            pltpu.VMEM((DEPTH * XROWS, LANES), F32),
            pltpu.SemaphoreType.DMA((DEPTH,)),
        ],
    )(held(enter.reshape(XROWS, LANES)), held(gains), held(holds), held(pattern))
    out = out.reshape(DEPTH, ROWS, 2, PLANES, LANES).transpose(0, 1, 3, 2, 4)
    return out.reshape(DEPTH, ROWS, PLANES, WIDTH)


def solution(mesh):
    placed = (P("space", None, None, "vel"), P("space", None, None), P("vel"), P("vel"))
    return jax.shard_map(
        shards, mesh=mesh, in_specs=placed, out_specs=P("space", None, None, "vel"), check_vma=False
    )
```

```python
import math

import jax
import jax.numpy as jnp
from jax import lax
from jax.experimental import pallas as pl
from jax.experimental.pallas import tpu as pltpu
from jax.sharding import PartitionSpec as P

VS = 16
SPACING = 8.0 / VS
HALF = (VS - 1) / 2.0
WEIGHT = SPACING**3

stream_x = 40.0
stream_y = 0.15
stream_z = 0.05
relaxation_multiplier = 0.05
shear_power_index = 0.81
diffusivity_ratio = 2.0 / 3.0

DEPTH, ROWS, PLANES, WIDTH = 4, 32, 2, 256
LANES = 128
XROWS = ROWS * 2 * PLANES
F32 = jnp.float32
BF16 = jnp.bfloat16

CHUNKS = 8
CHUNK_ROWS = 17

ORDER = list(range(31, -1, -1))
LINE = [7, 6, 5, 4, 3, 2, 1, 0]


def velocity(points):
    first = (points >> 8).astype(F32)
    second = ((points >> 4) & 15).astype(F32)
    third = (points & 15).astype(F32)
    return [(v - HALF) * SPACING for v in (first, second, third)]


def sublane(shape):
    return lax.broadcasted_iota(jnp.int32, shape, 0)


def by_half(pair):
    low = jnp.broadcast_to(pair[0:1], (8, LANES))
    high = jnp.broadcast_to(pair[1:2], (8, LANES))
    return jnp.where((sublane((8, LANES)) & 2) == 0, low, high)


def moments_kernel(
    f_hbm, point_hbm, mirror_hbm, wall_hbm,
    out_ref, f_ref, pattern_ref, slot_ref, weight_ref,
    point_ref, mirror_ref, wall_ref, f_sem, small_sem,
):
    small = [
        pltpu.make_async_copy(src, dst, small_sem.at[k])
        for k, (src, dst) in enumerate(
            [(point_hbm, point_ref), (wall_hbm, wall_ref), (mirror_hbm, mirror_ref)]
        )
    ]
    for copy in small:
        copy.start()
    chunks = []
    for x in range(2):
        rows = pl.ds(2 * x * XROWS, 2 * XROWS)
        chunks.append(pltpu.make_async_copy(f_hbm.at[rows], f_ref.at[rows], f_sem.at[x]))
        chunks[x].start()

    small[0].wait()
    points = point_ref[...]
    tables = []
    for half in range(2):
        x1, x2, x3 = velocity(points[half : half + 1])
        square = x1 * x1 + x2 * x2 + x3 * x3
        cubes = [x1 * square, x2 * square, x3 * square]
        coarse = [c.astype(BF16).astype(F32) for c in cubes]
        tables += [
            jnp.ones_like(x1), x1, x2, x3,
            x1 * x1, x2 * x2, x3 * x3, x1 * x2,
            x1 * x3, x2 * x3, *coarse,
            *[c - r for c, r in zip(cubes, coarse)],
        ]
    weights = []
    for half in range(2):
        x1, x2, x3 = velocity(points[half : half + 1])
        square = x1 * x1 + x2 * x2 + x3 * x3
        coarse = square.astype(BF16).astype(F32)
        one, zero = jnp.ones_like(x1), jnp.zeros_like(x1)
        left = [one, x1, x2, x3, coarse, square - coarse] + [zero] * 10
        right = [zero] * 6 + [one, x1, x2, x3] + [zero] * 6
        weights += [jnp.concatenate(pair, axis=1) for pair in zip(left, right)]
    weights = jnp.concatenate(weights, axis=0).astype(BF16)
    weight_ref[...] = jnp.concatenate([weights] * 3 + [jnp.zeros_like(weights)], axis=0)
    table = jnp.concatenate(tables, axis=0).astype(BF16)
    table = jnp.concatenate([table] * 3, axis=1)
    low_lane = (lax.broadcasted_iota(jnp.int32, (8, LANES), 1) & 2) == 0
    pairs = velocity(points)
    for k in range(3):
        pattern_ref[k] = by_half(pairs[k])
    small[1].wait()
    for x in range(DEPTH):
        for wall in range(2):
            planes = wall_ref[wall, :, x : x + 1].astype(F32)
            planes = jnp.broadcast_to(planes, (PLANES, LANES))
            pattern_ref[3 + 2 * x + wall] = jnp.concatenate([planes] * 4, axis=0)
    small[2].wait()
    for half in range(2):
        slot_ref[half] = jnp.broadcast_to(mirror_ref[half : half + 1], (8, LANES))

    x2 = pairs[1]
    for x in range(DEPTH):
        if x % 2 == 0:
            chunks[x // 2].wait()
            f = f_ref[pl.ds(x * XROWS, 2 * XROWS), :]
            high = f.astype(BF16)
            rest = f - high.astype(F32)
            middle = rest.astype(BF16)
            low = (rest - middle.astype(F32)).astype(BF16)
            both = lax.dot_general(
                table,
                jnp.concatenate([high, middle, low], axis=1),
                (((1,), (1,)), ((), ())),
                preferred_element_type=F32,
            )
        sums = both[:, XROWS * (x % 2) : XROWS * (x % 2 + 1)]
        packed = jnp.where(
            low_lane,
            sums[0:8] + pltpu.roll(sums[16:24], LANES - 2, 1),
            sums[24:32] + pltpu.roll(sums[8:16], 2, 1),
        )
        out_ref[pl.ds(x, 8, stride=DEPTH), :] = packed
        for half in range(2):
            low = f_ref[pl.ds(x * XROWS + 2 * half, 2), :]
            high = f_ref[pl.ds((x + 1) * XROWS - 4 + 2 * half, 2), :]
            out_ref[pl.ds(32 + 8 * half + 2 * x, 2), :] = jnp.where(
                x2[half : half + 1] < 0, low, high
            )


def cell_quantities(sums):
    low_lane = (lax.broadcasted_iota(jnp.int32, (DEPTH, LANES), 1) & 2) == 0
    low, high = [], []
    for m in range(8):
        own = sums[DEPTH * m : DEPTH * (m + 1)] * WEIGHT
        other = jnp.where(low_lane, pltpu.roll(own, LANES - 2, 1), pltpu.roll(own, 2, 1))
        low.append(jnp.where(low_lane, own, other))
        high.append(jnp.where(low_lane, other, own))
    n = low[0]
    inv = 1.0 / n
    u = [low[1 + k] * inv for k in range(3)]
    pressure = {(0, 0): low[4], (1, 1): low[5], (2, 2): low[6]}
    pressure.update({(0, 1): low[7], (0, 2): high[0], (1, 2): high[1]})
    energy = low[4] + low[5] + low[6]
    speed = u[0] * u[0] + u[1] * u[1] + u[2] * u[2]
    temperature = (energy - n * speed) * inv * (1.0 / 3.0)
    heat = []
    for k in range(3):
        cross = sum(u[j] * pressure[min(j, k), max(j, k)] for j in range(3))
        heat.append(0.5 * (high[2 + k] + high[5 + k] - 2.0 * cross + u[k] * (2.0 * n * speed - energy)))
    inv_t = 1.0 / temperature
    scale = (1.0 - diffusivity_ratio) / 5.0 * inv * inv_t * inv_t
    arg = 2.0 * math.pi * temperature
    norm = n / (arg * jnp.sqrt(arg))
    heat = [h * scale for h in heat]
    rate = relaxation_multiplier * n * jnp.exp((1.0 - shear_power_index) * jnp.log(temperature))
    ratio = [speed * inv_t] + [-2.0 * v * inv_t for v in u] + [inv_t]
    along = [-(u[0] * heat[0] + u[1] * heat[1] + u[2] * heat[2])] + heat
    return ratio + along, norm, rate


def blocks_kernel(
    copies, got_ref, f_ref, pattern_ref, slot_ref, weight_ref, send_ref, a_ref, h_ref, poly_ref
):
    sums = got_ref[0, 0:32, :]
    for k in range(1, 16):
        sums = sums + got_ref[k, 0:32, :]
    coefficients, norm, rates = cell_quantities(sums)
    parts = [[], [], []]
    for c in coefficients:
        for part in parts:
            piece = c.astype(BF16).astype(F32)
            part.append(piece)
            c = c - piece
    rows = parts[0] + parts[1] + parts[2] + [norm, rates]
    filler = jnp.zeros((LANES - DEPTH * len(rows), LANES), F32)
    columns = jnp.concatenate(rows + [filler], axis=0).T

    lane = lax.broadcasted_iota(jnp.int32, (8, LANES), 1)
    term = lane & 15
    term = jnp.where(term > 9, 0, jnp.where(term > 4, term - 1, term))
    part = jnp.where(lane < 96, lane >> 5, 0)
    source = DEPTH * (len(coefficients) * part + term)
    same = ((sublane((8, LANES)) >> 1) & 1) == ((lane >> 4) & 1)
    left = []
    for x in range(DEPTH):
        for i in range(XROWS // 8):
            value = jnp.take_along_axis(columns[8 * i : 8 * i + 8], source + x, axis=1)
            left.append(jnp.where(same, value, 0.0))
    poly_ref[...] = lax.dot_general(
        jnp.concatenate(left, axis=0).astype(BF16),
        weight_ref[...],
        (((1,), (0,)), ((), ())),
        preferred_element_type=F32,
    )

    lane = lax.broadcasted_iota(jnp.int32, (8, LANES), 1)
    cell = (lane >> 3) & 7
    source = 16 * sublane((8, LANES)) + 4 * (cell >> 1) + (cell & 1)
    speed = stream_x * SPACING * ((lane & 7).astype(F32) + 0.5)
    chunk_gain = jnp.ones((8, LANES), F32)
    for x in range(DEPTH):
        rate = jnp.broadcast_to(rates[x : x + 1], (8, LANES))
        rate = jnp.take_along_axis(rate, source, axis=1)
        chunk_gain = chunk_gain * (speed / (1.0 + speed + rate))
    for to in range(copies * CHUNKS):
        at = to % CHUNKS
        send_ref[pl.ds(CHUNK_ROWS * ORDER.index(to) + 16, 1), :] = chunk_gain[at : at + 1]

    found = []
    for half in range(2):
        slot = slot_ref[half]
        lane, group = slot & (LANES - 1), slot >> 7
        value = jnp.zeros((8, LANES), F32)
        for source in range(32):
            piece = got_ref[source // 2, pl.ds(32 + 8 * (source % 2), 8), :]
            value = jnp.where(
                group == source, jnp.take_along_axis(piece, lane, axis=1), value
            )
        found.append(value)

    x1, x2, x3 = pattern_ref[0], pattern_ref[1], pattern_ref[2]
    ahead = x1 > 0
    upward = x2 > 0
    sigma = stream_x * jnp.abs(x1)
    sigma1 = 1.0 + sigma
    flux_y = stream_y * jnp.abs(x2)
    flux_z = stream_z * jnp.abs(x3)
    own = 1.0 - flux_y - flux_z
    row = sublane((8, LANES))
    first_plane = (row & 1) == 0
    lower = row < 4
    here = lax.axis_index("space")
    edge = here == jnp.where(ahead, 0, lax.axis_size("space") - 1)

    ghosts = []
    for x in range(DEPTH):
        four = jnp.concatenate(
            [found[0][2 * x : 2 * x + 2], found[1][2 * x : 2 * x + 2]], axis=0
        )
        ghosts.append(jnp.concatenate([four, four], axis=0))

    for i in range(XROWS // 8):
        a, b, target = [], [], []
        for x in range(DEPTH):
            def column(q):
                at = DEPTH * (3 * len(coefficients) + q) + x
                return jnp.broadcast_to(
                    columns[8 * i : 8 * i + 8, at : at + 1], (8, LANES)
                )

            base = x * XROWS + 8 * i
            f = f_ref[pl.ds(base, 8), :]
            ratio = poly_ref[pl.ds(base, 8), 0:LANES]
            along = poly_ref[pl.ds(base, 8), LANES : 2 * LANES]
            shakhov = column(0) * jnp.exp(-0.5 * ratio) * (1.0 + along * (ratio - 5.0))
            rate = column(1)

            def ghost(wall):
                mask = pattern_ref[3 + 2 * x + wall]
                return jnp.where(mask == 1.0, ghosts[x], shakhov)

            if i == 0:
                below = jnp.where(lower, ghost(0), pltpu.roll(f, 4, 0))
            else:
                below = f_ref[pl.ds(base - 4, 8), :]
            if i == XROWS // 8 - 1:
                above = jnp.where(lower, pltpu.roll(f, 4, 0), ghost(1))
            else:
                above = f_ref[pl.ds(base + 4, 8), :]
            upwind = jnp.where(upward, below, above)
            other = jnp.where(first_plane, pltpu.roll(f, 7, 0), pltpu.roll(f, 1, 0))
            inverse = 1.0 / (sigma1 + rate)
            a.append(sigma * inverse)
            b.append(
                (own * f + rate * shakhov + flux_y * upwind + flux_z * other) * inverse
            )
            target.append(shakhov)
        order = lambda v, t: jnp.where(ahead, v[t], v[DEPTH - 1 - t])
        a0 = order(a, 0)
        hold = order(b, 0) + jnp.where(edge, a0 * order(target, 0), 0.0)
        gain = jnp.where(edge, 0.0, a0)
        a_ref[pl.ds(8 * i, 8), :] = gain
        h_ref[pl.ds(8 * i, 8), :] = hold
        for t in range(1, DEPTH):
            at = order(a, t)
            gain = at * gain
            hold = at * hold + order(b, t)
            a_ref[pl.ds(t * XROWS + 8 * i, 8), :] = gain
            h_ref[pl.ds(t * XROWS + 8 * i, 8), :] = hold
        for copy in range(copies):
            to = copy * CHUNKS + i // 2
            send_ref[pl.ds(CHUNK_ROWS * ORDER.index(to) + 8 * (i % 2), 8), :] = hold


def chain_kernel(copies, got_ref, pattern_ref, out_ref, gain_ref, keep_ref):
    blocks = copies * CHUNKS
    ahead = pattern_ref[0] > 0
    which = (jnp.abs(pattern_ref[0]) * (1.0 / SPACING) - 0.5).astype(jnp.int32)
    row = sublane((8, LANES))
    for half in range(2):
        cell = 2 * (2 * half + (row >> 2)) + (row & 1)
        source = 8 * cell + which
        for k in range(blocks):
            gain = jnp.broadcast_to(got_ref[pl.ds(CHUNK_ROWS * ORDER.index(k) + 16, 1), :], (8, LANES))
            gain_ref[k] = jnp.take_along_axis(gain, source, axis=1)
        enter = jnp.zeros((8, LANES), F32)
        for k in range(blocks):
            keep_ref[half, k] = enter
            back = blocks - 1 - k
            gain = jnp.where(ahead, gain_ref[k], gain_ref[back])
            hold = jnp.where(
                ahead,
                got_ref[pl.ds(CHUNK_ROWS * ORDER.index(k) + 8 * half, 8), :],
                got_ref[pl.ds(CHUNK_ROWS * ORDER.index(back) + 8 * half, 8), :],
            )
            enter = gain * enter + hold
    first = lax.axis_index("space") // CHUNKS * CHUNKS
    for half in range(2):
        for x in range(CHUNKS):
            out_ref[LINE.index(x), pl.ds(8 * half, 8), :] = jnp.where(
                ahead, keep_ref[half, first + x], keep_ref[half, blocks - 1 - x - first]
            )


def finish_kernel(enter_ref, a_ref, h_ref, pattern_ref, out_hbm, out_ref, sem):
    ahead = pattern_ref[0] > 0
    copies = []
    for x, mate in ((0, DEPTH - 1), (1, DEPTH - 2)):
        for i in range(XROWS // 8):
            enter = enter_ref[pl.ds(16 * LINE.index(i // 2) + 8 * (i % 2), 8), :]
            value = []
            for t in (x, mate):
                at = pl.ds(t * XROWS + 8 * i, 8)
                value.append(a_ref[at, :] * enter + h_ref[at, :])
            out_ref[pl.ds(x * XROWS + 8 * i, 8), :] = jnp.where(ahead, value[0], value[1])
            out_ref[pl.ds(mate * XROWS + 8 * i, 8), :] = jnp.where(ahead, value[1], value[0])
        for t in (x, mate):
            rows = pl.ds(t * XROWS, XROWS)
            copies.append(pltpu.make_async_copy(out_ref.at[rows], out_hbm.at[rows], sem.at[t]))
            copies[-1].start()
    for copy in copies:
        copy.wait()


ON_CHIP = pl.BlockSpec(memory_space=pltpu.VMEM)
ANYWHERE = pl.BlockSpec(memory_space=pl.ANY)


def held(x):
    return pltpu.with_memory_space_constraint(x, pltpu.VMEM)


def shards(distribution, wall_mask, grid_point, mirror_slot):
    blocks = lax.axis_size("space")
    copies = blocks // CHUNKS
    f = distribution.reshape(DEPTH, ROWS, PLANES, 2, LANES)
    f = f.transpose(0, 1, 3, 2, 4).reshape(DEPTH * XROWS, LANES)
    point = grid_point.reshape(2, LANES)
    mirror = mirror_slot.reshape(2, LANES)
    wall = wall_mask.transpose(1, 2, 0)

    mine, kept, pattern, slots, weights = pl.pallas_call(
        moments_kernel,
        out_shape=[
            pltpu.VMEM((48, LANES), F32),
            pltpu.VMEM((DEPTH * XROWS, LANES), F32),
            pltpu.VMEM((3 + 2 * DEPTH, 8, LANES), F32),
            pltpu.VMEM((2, 8, LANES), jnp.int32),
            pltpu.VMEM((LANES, 2 * LANES), BF16),
        ],
        in_specs=[ANYWHERE] * 4,
        out_specs=[ON_CHIP] * 5,
        scratch_shapes=[
            pltpu.VMEM((2, LANES), jnp.int32),
            pltpu.VMEM((2, LANES), jnp.int32),
            pltpu.VMEM((2, PLANES, DEPTH), jnp.int32),
            pltpu.SemaphoreType.DMA((2,)),
            pltpu.SemaphoreType.DMA((3,)),
        ],
    )(f, point, mirror, wall)
    everyone = lax.all_gather(mine, "vel")
    send, gains, holds = pl.pallas_call(
        lambda *refs: blocks_kernel(copies, *refs),
        out_shape=[
            pltpu.VMEM((blocks * CHUNK_ROWS, LANES), F32),
            pltpu.VMEM((DEPTH * XROWS, LANES), F32),
            pltpu.VMEM((DEPTH * XROWS, LANES), F32),
        ],
        in_specs=[ON_CHIP] * 5,
        out_specs=[ON_CHIP] * 3,
        scratch_shapes=[pltpu.VMEM((DEPTH * XROWS, 2 * LANES), F32)],
    )(held(everyone), held(kept), held(pattern), held(slots), held(weights))
    chain = lax.all_to_all(
        send.reshape(blocks, 1, CHUNK_ROWS * LANES), "space", 0, 0, axis_index_groups=[ORDER], tiled=True
    ).reshape(blocks * CHUNK_ROWS, LANES)
    enters = pl.pallas_call(
        lambda *refs: chain_kernel(copies, *refs),
        out_shape=pltpu.VMEM((CHUNKS, 16, LANES), F32),
        in_specs=[ON_CHIP] * 2,
        out_specs=ON_CHIP,
        scratch_shapes=[
            pltpu.VMEM((blocks, 8, LANES), F32),
            pltpu.VMEM((2, blocks, 8, LANES), F32),
        ],
    )(held(chain), held(pattern))
    lines = [[CHUNKS * z + x for x in LINE] for z in range(copies)]
    enter = lax.all_to_all(enters, "space", 0, 0, axis_index_groups=lines, tiled=True)
    out = pl.pallas_call(
        finish_kernel,
        out_shape=jax.ShapeDtypeStruct((DEPTH * XROWS, LANES), F32),
        in_specs=[ON_CHIP] * 4,
        out_specs=ANYWHERE,
        scratch_shapes=[
            pltpu.VMEM((DEPTH * XROWS, LANES), F32),
            pltpu.SemaphoreType.DMA((DEPTH,)),
        ],
    )(held(enter.reshape(XROWS, LANES)), held(gains), held(holds), held(pattern))
    out = out.reshape(DEPTH, ROWS, 2, PLANES, LANES).transpose(0, 1, 3, 2, 4)
    return out.reshape(DEPTH, ROWS, PLANES, WIDTH)


def solution(mesh):
    placed = (P("space", None, None, "vel"), P("space", None, None), P("vel"), P("vel"))
    return jax.shard_map(
        shards, mesh=mesh, in_specs=placed, out_specs=P("space", None, None, "vel"), check_vma=False
    )
```

```python
import math

import jax
import jax.numpy as jnp
from jax import lax
from jax.experimental import pallas as pl
from jax.experimental.pallas import tpu as pltpu
from jax.sharding import PartitionSpec as P

VS = 16
SPACING = 8.0 / VS
HALF = (VS - 1) / 2.0
WEIGHT = SPACING**3

stream_x = 40.0
stream_y = 0.15
stream_z = 0.05
relaxation_multiplier = 0.05
shear_power_index = 0.81
diffusivity_ratio = 2.0 / 3.0

DEPTH, ROWS, PLANES, WIDTH = 4, 32, 2, 256
LANES = 128
XROWS = ROWS * 2 * PLANES
F32 = jnp.float32
BF16 = jnp.bfloat16

CHUNKS = 8
CHUNK_ROWS = 17

ORDER = list(range(31, -1, -1))
LINE = [7, 6, 5, 4, 3, 2, 1, 0]

SHARE = 23


def velocity(points):
    first = (points >> 8).astype(F32)
    second = ((points >> 4) & 15).astype(F32)
    third = (points & 15).astype(F32)
    return [(v - HALF) * SPACING for v in (first, second, third)]


def sublane(shape):
    return lax.broadcasted_iota(jnp.int32, shape, 0)


def by_half(pair):
    low = jnp.broadcast_to(pair[0:1], (8, LANES))
    high = jnp.broadcast_to(pair[1:2], (8, LANES))
    return jnp.where((sublane((8, LANES)) & 2) == 0, low, high)


def moments_kernel(
    f_hbm, point_hbm, mirror_hbm, wall_hbm,
    send_ref, f_ref, pattern_ref, weight_ref,
    half_ref, point_ref, mirror_ref, wall_ref, f_sem, small_sem,
):
    small = [
        pltpu.make_async_copy(src, dst, small_sem.at[k])
        for k, (src, dst) in enumerate(
            [(point_hbm, point_ref), (wall_hbm, wall_ref), (mirror_hbm, mirror_ref)]
        )
    ]
    for copy in small:
        copy.start()
    chunks = []
    for x in range(2):
        rows = pl.ds(2 * x * XROWS, 2 * XROWS)
        chunks.append(pltpu.make_async_copy(f_hbm.at[rows], f_ref.at[rows], f_sem.at[x]))
        chunks[x].start()

    small[0].wait()
    points = point_ref[...]
    tables = []
    for half in range(2):
        x1, x2, x3 = velocity(points[half : half + 1])
        square = x1 * x1 + x2 * x2 + x3 * x3
        cubes = [x1 * square, x2 * square, x3 * square]
        coarse = [c.astype(BF16).astype(F32) for c in cubes]
        tables += [
            jnp.ones_like(x1), x1, x2, x3,
            x1 * x1, x2 * x2, x3 * x3, x1 * x2,
            x1 * x3, x2 * x3, *coarse,
            *[c - r for c, r in zip(cubes, coarse)],
        ]
    weights = []
    for half in range(2):
        x1, x2, x3 = velocity(points[half : half + 1])
        square = x1 * x1 + x2 * x2 + x3 * x3
        coarse = square.astype(BF16).astype(F32)
        one, zero = jnp.ones_like(x1), jnp.zeros_like(x1)
        left = [one, x1, x2, x3, coarse, square - coarse] + [zero] * 10
        right = [zero] * 6 + [one, x1, x2, x3] + [zero] * 6
        weights += [jnp.concatenate(pair, axis=1) for pair in zip(left, right)]
    weights = jnp.concatenate(weights, axis=0).astype(BF16)
    weight_ref[...] = jnp.concatenate([weights] * 3 + [jnp.zeros_like(weights)], axis=0)
    table = jnp.concatenate(tables, axis=0).astype(BF16)
    table = jnp.concatenate([table] * 3, axis=1)
    low_lane = (lax.broadcasted_iota(jnp.int32, (8, LANES), 1) & 2) == 0
    pairs = velocity(points)
    for k in range(3):
        pattern_ref[k] = by_half(pairs[k])
    small[1].wait()
    for x in range(DEPTH):
        for wall in range(2):
            planes = wall_ref[wall, :, x : x + 1].astype(F32)
            planes = jnp.broadcast_to(planes, (PLANES, LANES))
            pattern_ref[3 + 2 * x + wall] = jnp.concatenate([planes] * 4, axis=0)
    small[2].wait()
    for core in range(2):
        half_ref[core, 21:23, :] = mirror_ref[...].astype(F32)

    x2 = pairs[1]
    for x in range(DEPTH):
        if x % 2 == 0:
            chunks[x // 2].wait()
            f = f_ref[pl.ds(x * XROWS, 2 * XROWS), :]
            high = f.astype(BF16)
            rest = f - high.astype(F32)
            middle = rest.astype(BF16)
            low = (rest - middle.astype(F32)).astype(BF16)
            both = lax.dot_general(
                table,
                jnp.concatenate([high, middle, low], axis=1),
                (((1,), (1,)), ((), ())),
                preferred_element_type=F32,
            )
        sums = both[:, XROWS * (x % 2) : XROWS * (x % 2 + 1)]
        packed = jnp.where(
            low_lane,
            sums[0:8] + pltpu.roll(sums[16:24], LANES - 2, 1),
            sums[24:32] + pltpu.roll(sums[8:16], 2, 1),
        )
        core, second = divmod(x, 2)
        tail = packed[5:8]
        half_ref[core, pl.ds(5 * second, 2), :] = packed[0:2]
        half_ref[core, pl.ds(5 * second + 2, 3), :] = packed[2:5] + jnp.where(
            low_lane[0:3], 0.0, tail
        )
        if second:
            half_ref[core, 10:13, :] = jnp.where(
                low_lane[0:3], before, pltpu.roll(packed, 2, 1)[5:8]
            )
        before = tail
        for half in range(2):
            low = f_ref[pl.ds(x * XROWS + 2 * half, 2), :]
            high = f_ref[pl.ds((x + 1) * XROWS - 4 + 2 * half, 2), :]
            half_ref[core, pl.ds(13 + 4 * half + 2 * second, 2), :] = jnp.where(
                x2[half : half + 1] < 0, low, high
            )
        if second:
            for to in range(1 - core, send_ref.shape[0] // SHARE, 2):
                send_ref[pl.ds(SHARE * to, SHARE), :] = half_ref[core, 0:SHARE, :]


def cell_quantities(sums):
    low_lane = (lax.broadcasted_iota(jnp.int32, (2, LANES), 1) & 2) == 0
    low, high = [], []
    for m in range(8):
        if m < 5:
            own = jnp.concatenate([sums[m : m + 1], sums[5 + m : 6 + m]], axis=0)
            own = own * WEIGHT
            other = jnp.where(
                low_lane, pltpu.roll(own, LANES - 2, 1), pltpu.roll(own, 2, 1)
            )
            low.append(jnp.where(low_lane, own, other))
            high.append(jnp.where(low_lane, other, own))
        else:
            own = jnp.broadcast_to(sums[5 + m : 6 + m], (2, LANES)) * WEIGHT
            first = jnp.where(low_lane, own, pltpu.roll(own, 2, 1))
            second = jnp.where(low_lane, pltpu.roll(own, LANES - 2, 1), own)
            low.append(jnp.where(sublane((2, LANES)) == 0, first, second))
    n = low[0]
    inv = 1.0 / n
    u = [low[1 + k] * inv for k in range(3)]
    pressure = {(0, 0): low[4], (1, 1): low[5], (2, 2): low[6]}
    pressure.update({(0, 1): low[7], (0, 2): high[0], (1, 2): high[1]})
    energy = low[4] + low[5] + low[6]
    speed = u[0] * u[0] + u[1] * u[1] + u[2] * u[2]
    temperature = (energy - n * speed) * inv * (1.0 / 3.0)
    heat = []
    for k in range(3):
        cross = sum(u[j] * pressure[min(j, k), max(j, k)] for j in range(3))
        heat.append(0.5 * (high[2 + k] - 2.0 * cross + u[k] * (2.0 * n * speed - energy)))
    inv_t = 1.0 / temperature
    scale = (1.0 - diffusivity_ratio) / 5.0 * inv * inv_t * inv_t
    arg = 2.0 * math.pi * temperature
    norm = n / (arg * jnp.sqrt(arg))
    heat = [h * scale for h in heat]
    rate = relaxation_multiplier * n * jnp.exp((1.0 - shear_power_index) * jnp.log(temperature))
    ratio = [speed * inv_t] + [-2.0 * v * inv_t for v in u] + [inv_t]
    along = [-(u[0] * heat[0] + u[1] * heat[1] + u[2] * heat[2])] + heat
    return ratio + along + [norm, rate]


def cells_kernel(sources, got_ref, out_ref):
    sums = got_ref[pl.ds(0, 16), :]
    for k in range(1, sources):
        sums = sums + got_ref[pl.ds(SHARE * k, 16), :]
    quantities = cell_quantities(sums)
    filler = jnp.zeros((24 - 2 * len(quantities), LANES), F32)
    table = jnp.concatenate(quantities + [filler], axis=0)
    for k in range(3):
        out_ref[k] = table[8 * k : 8 * k + 8]

    upper = (sublane((8, LANES)) >> 2) & 1
    even = sources - 1 - lax.axis_index("vel") // 2 * 2
    lanes, kept, rolled, values = [], [], [], []
    for core in range(2):
        at = SHARE * (even - core) + 21
        first = jnp.broadcast_to(got_ref[pl.ds(at, 1), :], (8, LANES))
        second = jnp.broadcast_to(got_ref[pl.ds(at + 1, 1), :], (8, LANES))
        slot = jnp.where(upper == 0, first, second).astype(jnp.int32)
        lanes.append(slot & (LANES - 1))
        kept.append((slot >> 7) - upper)
        rolled.append((slot >> 7) + upper)
        values.append(jnp.zeros((8, LANES), F32))
    for k in range(sources):
        piece = got_ref[pl.ds(SHARE * k + 13, 8), :]
        swapped = pltpu.roll(piece, 4, 0)
        owner = sources - 1 - k
        for core in range(2):
            there = jnp.take_along_axis(piece, lanes[core], axis=1)
            across = jnp.take_along_axis(swapped, lanes[core], axis=1)
            value = jnp.where(kept[core] == 2 * owner, there, values[core])
            values[core] = jnp.where(rolled[core] == 2 * owner + 1, across, value)
    for core in range(2):
        out_ref[3 + core] = values[core]


def blocks_kernel(
    copies, got_ref, f_ref, pattern_ref, weight_ref, send_ref, a_ref, h_ref, poly_ref
):
    halves = [
        jnp.concatenate([got_ref[half, k] for k in range(3)], axis=0) for half in range(2)
    ]
    rates = [halves[x // 2][20 + x % 2 : 21 + x % 2] for x in range(DEPTH)]
    rows, left = [], halves
    for part in range(3):
        pieces = [h.astype(BF16).astype(F32) for h in left]
        rows += [p[0:18] for p in pieces]
        left = [h - p for h, p in zip(left, pieces)]
    rows += [h[18:22] for h in halves]
    filler = jnp.zeros((LANES - 116, LANES), F32)
    columns = jnp.concatenate(rows + [filler], axis=0).T

    lane = lax.broadcasted_iota(jnp.int32, (8, LANES), 1)
    term = lane & 15
    term = jnp.where(term > 9, 0, jnp.where(term > 4, term - 1, term))
    source = 36 * jnp.where(lane < 96, lane >> 5, 0) + 2 * term
    same = ((sublane((8, LANES)) >> 1) & 1) == ((lane >> 4) & 1)
    left = []
    for x in range(DEPTH):
        at = source + (18 * (x // 2) + x % 2)
        for i in range(XROWS // 8):
            value = jnp.take_along_axis(columns[8 * i : 8 * i + 8], at, axis=1)
            left.append(jnp.where(same, value, 0.0))
    poly_ref[...] = lax.dot_general(
        jnp.concatenate(left, axis=0).astype(BF16),
        weight_ref[...],
        (((1,), (0,)), ((), ())),
        preferred_element_type=F32,
    )
    core = lax.axis_index("vel") % 2
    found = [got_ref[half, 3 + core] for half in range(2)]

    lane = lax.broadcasted_iota(jnp.int32, (8, LANES), 1)
    cell = (lane >> 3) & 7
    source = 16 * sublane((8, LANES)) + 4 * (cell >> 1) + (cell & 1)
    speed = stream_x * SPACING * ((lane & 7).astype(F32) + 0.5)
    chunk_gain = jnp.ones((8, LANES), F32)
    for x in range(DEPTH):
        rate = jnp.broadcast_to(rates[x], (8, LANES))
        rate = jnp.take_along_axis(rate, source, axis=1)
        chunk_gain = chunk_gain * (speed / (1.0 + speed + rate))
    for to in range(copies * CHUNKS):
        at = to % CHUNKS
        send_ref[pl.ds(CHUNK_ROWS * ORDER.index(to) + 16, 1), :] = chunk_gain[at : at + 1]

    x1, x2, x3 = pattern_ref[0], pattern_ref[1], pattern_ref[2]
    ahead = x1 > 0
    upward = x2 > 0
    sigma = stream_x * jnp.abs(x1)
    sigma1 = 1.0 + sigma
    flux_y = stream_y * jnp.abs(x2)
    flux_z = stream_z * jnp.abs(x3)
    own = 1.0 - flux_y - flux_z
    row = sublane((8, LANES))
    first_plane = (row & 1) == 0
    lower = row < 4
    here = lax.axis_index("space")
    edge = here == jnp.where(ahead, 0, lax.axis_size("space") - 1)

    ghosts = []
    for x in range(DEPTH):
        wall = found[x // 2]
        at = 2 * (x % 2)
        four = jnp.concatenate([wall[at : at + 2], wall[at + 4 : at + 6]], axis=0)
        ghosts.append(jnp.concatenate([four, four], axis=0))

    for i in range(XROWS // 8):
        a, b, target = [], [], []
        for x in range(DEPTH):
            def column(q):
                at = 108 + 4 * (x // 2) + 2 * q + x % 2
                return jnp.broadcast_to(
                    columns[8 * i : 8 * i + 8, at : at + 1], (8, LANES)
                )

            base = x * XROWS + 8 * i
            f = f_ref[pl.ds(base, 8), :]
            ratio = poly_ref[pl.ds(base, 8), 0:LANES]
            along = poly_ref[pl.ds(base, 8), LANES : 2 * LANES]
            shakhov = column(0) * jnp.exp(-0.5 * ratio) * (1.0 + along * (ratio - 5.0))
            rate = column(1)

            def ghost(wall):
                mask = pattern_ref[3 + 2 * x + wall]
                return jnp.where(mask == 1.0, ghosts[x], shakhov)

            if i == 0:
                below = jnp.where(lower, ghost(0), pltpu.roll(f, 4, 0))
            else:
                below = f_ref[pl.ds(base - 4, 8), :]
            if i == XROWS // 8 - 1:
                above = jnp.where(lower, pltpu.roll(f, 4, 0), ghost(1))
            else:
                above = f_ref[pl.ds(base + 4, 8), :]
            upwind = jnp.where(upward, below, above)
            other = jnp.where(first_plane, pltpu.roll(f, 7, 0), pltpu.roll(f, 1, 0))
            inverse = 1.0 / (sigma1 + rate)
            a.append(sigma * inverse)
            b.append(
                (own * f + rate * shakhov + flux_y * upwind + flux_z * other) * inverse
            )
            target.append(shakhov)
        order = lambda v, t: jnp.where(ahead, v[t], v[DEPTH - 1 - t])
        a0 = order(a, 0)
        hold = order(b, 0) + jnp.where(edge, a0 * order(target, 0), 0.0)
        gain = jnp.where(edge, 0.0, a0)
        a_ref[pl.ds(8 * i, 8), :] = gain
        h_ref[pl.ds(8 * i, 8), :] = hold
        for t in range(1, DEPTH):
            at = order(a, t)
            gain = at * gain
            hold = at * hold + order(b, t)
            a_ref[pl.ds(t * XROWS + 8 * i, 8), :] = gain
            h_ref[pl.ds(t * XROWS + 8 * i, 8), :] = hold
        for copy in range(copies):
            to = copy * CHUNKS + i // 2
            send_ref[pl.ds(CHUNK_ROWS * ORDER.index(to) + 8 * (i % 2), 8), :] = hold


def chain_kernel(copies, got_ref, pattern_ref, out_ref, gain_ref, keep_ref):
    blocks = copies * CHUNKS
    ahead = pattern_ref[0] > 0
    which = (jnp.abs(pattern_ref[0]) * (1.0 / SPACING) - 0.5).astype(jnp.int32)
    row = sublane((8, LANES))
    for half in range(2):
        cell = 2 * (2 * half + (row >> 2)) + (row & 1)
        source = 8 * cell + which
        for k in range(blocks):
            gain = jnp.broadcast_to(got_ref[pl.ds(CHUNK_ROWS * ORDER.index(k) + 16, 1), :], (8, LANES))
            gain_ref[k] = jnp.take_along_axis(gain, source, axis=1)
        enter = jnp.zeros((8, LANES), F32)
        for k in range(blocks):
            keep_ref[half, k] = enter
            back = blocks - 1 - k
            gain = jnp.where(ahead, gain_ref[k], gain_ref[back])
            hold = jnp.where(
                ahead,
                got_ref[pl.ds(CHUNK_ROWS * ORDER.index(k) + 8 * half, 8), :],
                got_ref[pl.ds(CHUNK_ROWS * ORDER.index(back) + 8 * half, 8), :],
            )
            enter = gain * enter + hold
    first = lax.axis_index("space") // CHUNKS * CHUNKS
    for half in range(2):
        for x in range(CHUNKS):
            out_ref[LINE.index(x), pl.ds(8 * half, 8), :] = jnp.where(
                ahead, keep_ref[half, first + x], keep_ref[half, blocks - 1 - x - first]
            )


def finish_kernel(enter_ref, a_ref, h_ref, pattern_ref, out_hbm, out_ref, sem):
    ahead = pattern_ref[0] > 0
    copies = []
    for x, mate in ((0, DEPTH - 1), (1, DEPTH - 2)):
        for i in range(XROWS // 8):
            enter = enter_ref[pl.ds(16 * LINE.index(i // 2) + 8 * (i % 2), 8), :]
            value = []
            for t in (x, mate):
                at = pl.ds(t * XROWS + 8 * i, 8)
                value.append(a_ref[at, :] * enter + h_ref[at, :])
            out_ref[pl.ds(x * XROWS + 8 * i, 8), :] = jnp.where(ahead, value[0], value[1])
            out_ref[pl.ds(mate * XROWS + 8 * i, 8), :] = jnp.where(ahead, value[1], value[0])
        for t in (x, mate):
            rows = pl.ds(t * XROWS, XROWS)
            copies.append(pltpu.make_async_copy(out_ref.at[rows], out_hbm.at[rows], sem.at[t]))
            copies[-1].start()
    for copy in copies:
        copy.wait()


ON_CHIP = pl.BlockSpec(memory_space=pltpu.VMEM)
ANYWHERE = pl.BlockSpec(memory_space=pl.ANY)


def held(x):
    return pltpu.with_memory_space_constraint(x, pltpu.VMEM)


def shards(distribution, wall_mask, grid_point, mirror_slot):
    blocks = lax.axis_size("space")
    copies = blocks // CHUNKS
    f = distribution.reshape(DEPTH, ROWS, PLANES, 2, LANES)
    f = f.transpose(0, 1, 3, 2, 4).reshape(DEPTH * XROWS, LANES)
    point = grid_point.reshape(2, LANES)
    mirror = mirror_slot.reshape(2, LANES)
    wall = wall_mask.transpose(1, 2, 0)

    sources = lax.axis_size("vel")
    shares, kept, pattern, weights = pl.pallas_call(
        moments_kernel,
        out_shape=[
            pltpu.VMEM((sources * SHARE, LANES), F32),
            pltpu.VMEM((DEPTH * XROWS, LANES), F32),
            pltpu.VMEM((3 + 2 * DEPTH, 8, LANES), F32),
            pltpu.VMEM((LANES, 2 * LANES), BF16),
        ],
        in_specs=[ANYWHERE] * 4,
        out_specs=[ON_CHIP] * 4,
        scratch_shapes=[
            pltpu.VMEM((2, 24, LANES), F32),
            pltpu.VMEM((2, LANES), jnp.int32),
            pltpu.VMEM((2, LANES), jnp.int32),
            pltpu.VMEM((2, PLANES, DEPTH), jnp.int32),
            pltpu.SemaphoreType.DMA((2,)),
            pltpu.SemaphoreType.DMA((3,)),
        ],
    )(f, point, mirror, wall)
    partial = lax.all_to_all(
        shares.reshape(sources, 1, SHARE * LANES),
        "vel",
        0,
        0,
        axis_index_groups=[[*range(sources - 1, -1, -1)]],
        tiled=True,
    ).reshape(sources * SHARE, LANES)
    cells = pl.pallas_call(
        lambda *refs: cells_kernel(sources, *refs),
        out_shape=pltpu.VMEM((5, 8, LANES), F32),
        in_specs=[ON_CHIP],
        out_specs=ON_CHIP,
    )(held(partial))
    pairs = [[k, k + 1] for k in range(0, sources, 2)]
    everyone = lax.all_gather(cells, "vel", axis_index_groups=pairs)
    send, gains, holds = pl.pallas_call(
        lambda *refs: blocks_kernel(copies, *refs),
        out_shape=[
            pltpu.VMEM((blocks * CHUNK_ROWS, LANES), F32),
            pltpu.VMEM((DEPTH * XROWS, LANES), F32),
            pltpu.VMEM((DEPTH * XROWS, LANES), F32),
        ],
        in_specs=[ON_CHIP] * 4,
        out_specs=[ON_CHIP] * 3,
        scratch_shapes=[pltpu.VMEM((DEPTH * XROWS, 2 * LANES), F32)],
    )(held(everyone), held(kept), held(pattern), held(weights))
    chain = lax.all_to_all(
        send.reshape(blocks, 1, CHUNK_ROWS * LANES), "space", 0, 0, axis_index_groups=[ORDER], tiled=True
    ).reshape(blocks * CHUNK_ROWS, LANES)
    enters = pl.pallas_call(
        lambda *refs: chain_kernel(copies, *refs),
        out_shape=pltpu.VMEM((CHUNKS, 16, LANES), F32),
        in_specs=[ON_CHIP] * 2,
        out_specs=ON_CHIP,
        scratch_shapes=[
            pltpu.VMEM((blocks, 8, LANES), F32),
            pltpu.VMEM((2, blocks, 8, LANES), F32),
        ],
    )(held(chain), held(pattern))
    lines = [[CHUNKS * z + x for x in LINE] for z in range(copies)]
    enter = lax.all_to_all(enters, "space", 0, 0, axis_index_groups=lines, tiled=True)
    out = pl.pallas_call(
        finish_kernel,
        out_shape=jax.ShapeDtypeStruct((DEPTH * XROWS, LANES), F32),
        in_specs=[ON_CHIP] * 4,
        out_specs=ANYWHERE,
        scratch_shapes=[
            pltpu.VMEM((DEPTH * XROWS, LANES), F32),
            pltpu.SemaphoreType.DMA((DEPTH,)),
        ],
    )(held(enter.reshape(XROWS, LANES)), held(gains), held(holds), held(pattern))
    out = out.reshape(DEPTH, ROWS, 2, PLANES, LANES).transpose(0, 1, 3, 2, 4)
    return out.reshape(DEPTH, ROWS, PLANES, WIDTH)


def solution(mesh):
    placed = (P("space", None, None, "vel"), P("space", None, None), P("vel"), P("vel"))
    return jax.shard_map(
        shards, mesh=mesh, in_specs=placed, out_specs=P("space", None, None, "vel"), check_vma=False
    )
```

```python
import math

import jax
import jax.numpy as jnp
from jax import lax
from jax.experimental import pallas as pl
from jax.experimental.pallas import tpu as pltpu
from jax.sharding import PartitionSpec as P

VS = 16
SPACING = 8.0 / VS
HALF = (VS - 1) / 2.0
WEIGHT = SPACING**3

stream_x = 40.0
stream_y = 0.15
stream_z = 0.05
relaxation_multiplier = 0.05
shear_power_index = 0.81
diffusivity_ratio = 2.0 / 3.0

DEPTH, ROWS, PLANES, WIDTH = 4, 32, 2, 256
LANES = 128
XROWS = ROWS * 2 * PLANES
F32 = jnp.float32
BF16 = jnp.bfloat16

CHUNKS = 8
CHUNK_ROWS = 17

VELO = [*range(11, -1, -1), *range(15, 11, -1)]
ORDER = list(range(31, -1, -1))
LINE = [6, 5, 4, 3, 2, 1, 0, 7]

SHARE = 23


def velocity(points):
    first = (points >> 8).astype(F32)
    second = ((points >> 4) & 15).astype(F32)
    third = (points & 15).astype(F32)
    return [(v - HALF) * SPACING for v in (first, second, third)]


def sublane(shape):
    return lax.broadcasted_iota(jnp.int32, shape, 0)


def by_half(pair):
    low = jnp.broadcast_to(pair[0:1], (8, LANES))
    high = jnp.broadcast_to(pair[1:2], (8, LANES))
    return jnp.where((sublane((8, LANES)) & 2) == 0, low, high)


def moments_kernel(
    f_hbm, point_hbm, mirror_hbm, wall_hbm,
    send_ref, f_ref, pattern_ref, weight_ref,
    half_ref, point_ref, mirror_ref, wall_ref, f_sem, small_sem,
):
    small = [
        pltpu.make_async_copy(src, dst, small_sem.at[k])
        for k, (src, dst) in enumerate(
            [(point_hbm, point_ref), (wall_hbm, wall_ref), (mirror_hbm, mirror_ref)]
        )
    ]
    for copy in small:
        copy.start()
    chunks = []
    for x in range(2):
        rows = pl.ds(2 * x * XROWS, 2 * XROWS)
        chunks.append(pltpu.make_async_copy(f_hbm.at[rows], f_ref.at[rows], f_sem.at[x]))
        chunks[x].start()

    small[0].wait()
    points = point_ref[...]
    tables = []
    for half in range(2):
        x1, x2, x3 = velocity(points[half : half + 1])
        square = x1 * x1 + x2 * x2 + x3 * x3
        cubes = [x1 * square, x2 * square, x3 * square]
        coarse = [c.astype(BF16).astype(F32) for c in cubes]
        tables += [
            jnp.ones_like(x1), x1, x2, x3,
            x1 * x1, x2 * x2, x3 * x3, x1 * x2,
            x1 * x3, x2 * x3, *coarse,
            *[c - r for c, r in zip(cubes, coarse)],
        ]
    weights = []
    for half in range(2):
        x1, x2, x3 = velocity(points[half : half + 1])
        square = x1 * x1 + x2 * x2 + x3 * x3
        coarse = square.astype(BF16).astype(F32)
        one, zero = jnp.ones_like(x1), jnp.zeros_like(x1)
        left = [one, x1, x2, x3, coarse, square - coarse] + [zero] * 10
        right = [zero] * 6 + [one, x1, x2, x3] + [zero] * 6
        weights += [jnp.concatenate(pair, axis=1) for pair in zip(left, right)]
    weights = jnp.concatenate(weights, axis=0).astype(BF16)
    weight_ref[...] = jnp.concatenate([weights] * 3 + [jnp.zeros_like(weights)], axis=0)
    table = jnp.concatenate(tables, axis=0).astype(BF16)
    table = jnp.concatenate([table] * 3, axis=1)
    low_lane = (lax.broadcasted_iota(jnp.int32, (8, LANES), 1) & 2) == 0
    pairs = velocity(points)
    for k in range(3):
        pattern_ref[k] = by_half(pairs[k])
    small[1].wait()
    for x in range(DEPTH):
        for wall in range(2):
            planes = wall_ref[wall, :, x : x + 1].astype(F32)
            planes = jnp.broadcast_to(planes, (PLANES, LANES))
            pattern_ref[3 + 2 * x + wall] = jnp.concatenate([planes] * 4, axis=0)
    small[2].wait()
    for core in range(2):
        half_ref[core, 21:23, :] = mirror_ref[...].astype(F32)

    x2 = pairs[1]
    for x in range(DEPTH):
        if x % 2 == 0:
            chunks[x // 2].wait()
            f = f_ref[pl.ds(x * XROWS, 2 * XROWS), :]
            high = f.astype(BF16)
            rest = f - high.astype(F32)
            middle = rest.astype(BF16)
            low = (rest - middle.astype(F32)).astype(BF16)
            both = lax.dot_general(
                table,
                jnp.concatenate([high, middle, low], axis=1),
                (((1,), (1,)), ((), ())),
                preferred_element_type=F32,
            )
        sums = both[:, XROWS * (x % 2) : XROWS * (x % 2 + 1)]
        packed = jnp.where(
            low_lane,
            sums[0:8] + pltpu.roll(sums[16:24], LANES - 2, 1),
            sums[24:32] + pltpu.roll(sums[8:16], 2, 1),
        )
        core, second = divmod(x, 2)
        tail = packed[5:8]
        half_ref[core, pl.ds(5 * second, 2), :] = packed[0:2]
        half_ref[core, pl.ds(5 * second + 2, 3), :] = packed[2:5] + jnp.where(
            low_lane[0:3], 0.0, tail
        )
        if second:
            half_ref[core, 10:13, :] = jnp.where(
                low_lane[0:3], before, pltpu.roll(packed, 2, 1)[5:8]
            )
        before = tail
        for half in range(2):
            low = f_ref[pl.ds(x * XROWS + 2 * half, 2), :]
            high = f_ref[pl.ds((x + 1) * XROWS - 4 + 2 * half, 2), :]
            half_ref[core, pl.ds(13 + 4 * half + 2 * second, 2), :] = jnp.where(
                x2[half : half + 1] < 0, low, high
            )
        if second:
            for to in [p for p in range(16) if VELO[p] % 2 == core]:
                send_ref[pl.ds(SHARE * to, SHARE), :] = half_ref[core, 0:SHARE, :]


def cell_quantities(sums):
    low_lane = (lax.broadcasted_iota(jnp.int32, (2, LANES), 1) & 2) == 0
    low, high = [], []
    for m in range(8):
        if m < 5:
            own = jnp.concatenate([sums[m : m + 1], sums[5 + m : 6 + m]], axis=0)
            own = own * WEIGHT
            other = jnp.where(
                low_lane, pltpu.roll(own, LANES - 2, 1), pltpu.roll(own, 2, 1)
            )
            low.append(jnp.where(low_lane, own, other))
            high.append(jnp.where(low_lane, other, own))
        else:
            own = jnp.broadcast_to(sums[5 + m : 6 + m], (2, LANES)) * WEIGHT
            first = jnp.where(low_lane, own, pltpu.roll(own, 2, 1))
            second = jnp.where(low_lane, pltpu.roll(own, LANES - 2, 1), own)
            low.append(jnp.where(sublane((2, LANES)) == 0, first, second))
    n = low[0]
    inv = 1.0 / n
    u = [low[1 + k] * inv for k in range(3)]
    pressure = {(0, 0): low[4], (1, 1): low[5], (2, 2): low[6]}
    pressure.update({(0, 1): low[7], (0, 2): high[0], (1, 2): high[1]})
    energy = low[4] + low[5] + low[6]
    speed = u[0] * u[0] + u[1] * u[1] + u[2] * u[2]
    temperature = (energy - n * speed) * inv * (1.0 / 3.0)
    heat = []
    for k in range(3):
        cross = sum(u[j] * pressure[min(j, k), max(j, k)] for j in range(3))
        heat.append(0.5 * (high[2 + k] - 2.0 * cross + u[k] * (2.0 * n * speed - energy)))
    inv_t = 1.0 / temperature
    scale = (1.0 - diffusivity_ratio) / 5.0 * inv * inv_t * inv_t
    arg = 2.0 * math.pi * temperature
    norm = n / (arg * jnp.sqrt(arg))
    heat = [h * scale for h in heat]
    rate = relaxation_multiplier * n * jnp.exp((1.0 - shear_power_index) * jnp.log(temperature))
    ratio = [speed * inv_t] + [-2.0 * v * inv_t for v in u] + [inv_t]
    along = [-(u[0] * heat[0] + u[1] * heat[1] + u[2] * heat[2])] + heat
    return ratio + along + [norm, rate]


def cells_kernel(sources, got_ref, out_ref):
    sums = got_ref[pl.ds(0, 16), :]
    for k in range(1, sources):
        sums = sums + got_ref[pl.ds(SHARE * k, 16), :]
    quantities = cell_quantities(sums)
    filler = jnp.zeros((24 - 2 * len(quantities), LANES), F32)
    table = jnp.concatenate(quantities + [filler], axis=0)
    for k in range(3):
        out_ref[k] = table[8 * k : 8 * k + 8]

    upper = (sublane((8, LANES)) >> 2) & 1
    chip = lax.axis_index("vel") // 2
    lanes, kept, rolled, values = [], [], [], []
    for core in range(2):
        at = SHARE * ((11 - 2 * chip - core) % 16) + 21
        first = jnp.broadcast_to(got_ref[pl.ds(at, 1), :], (8, LANES))
        second = jnp.broadcast_to(got_ref[pl.ds(at + 1, 1), :], (8, LANES))
        slot = jnp.where(upper == 0, first, second).astype(jnp.int32)
        lanes.append(slot & (LANES - 1))
        kept.append((slot >> 7) - upper)
        rolled.append((slot >> 7) + upper)
        values.append(jnp.zeros((8, LANES), F32))
    for k in range(sources):
        piece = got_ref[pl.ds(SHARE * k + 13, 8), :]
        swapped = pltpu.roll(piece, 4, 0)
        owner = VELO[k]
        for core in range(2):
            there = jnp.take_along_axis(piece, lanes[core], axis=1)
            across = jnp.take_along_axis(swapped, lanes[core], axis=1)
            value = jnp.where(kept[core] == 2 * owner, there, values[core])
            values[core] = jnp.where(rolled[core] == 2 * owner + 1, across, value)
    for core in range(2):
        out_ref[3 + core] = values[core]


def blocks_kernel(
    copies, got_ref, f_ref, pattern_ref, weight_ref, send_ref, a_ref, h_ref, poly_ref
):
    halves = [
        jnp.concatenate([got_ref[half, k] for k in range(3)], axis=0) for half in range(2)
    ]
    rates = [halves[x // 2][20 + x % 2 : 21 + x % 2] for x in range(DEPTH)]
    rows, left = [], halves
    for part in range(3):
        pieces = [h.astype(BF16).astype(F32) for h in left]
        rows += [p[0:18] for p in pieces]
        left = [h - p for h, p in zip(left, pieces)]
    rows += [h[18:22] for h in halves]
    filler = jnp.zeros((LANES - 116, LANES), F32)
    columns = jnp.concatenate(rows + [filler], axis=0).T

    lane = lax.broadcasted_iota(jnp.int32, (8, LANES), 1)
    term = lane & 15
    term = jnp.where(term > 9, 0, jnp.where(term > 4, term - 1, term))
    source = 36 * jnp.where(lane < 96, lane >> 5, 0) + 2 * term
    same = ((sublane((8, LANES)) >> 1) & 1) == ((lane >> 4) & 1)
    left = []
    for x in range(DEPTH):
        at = source + (18 * (x // 2) + x % 2)
        for i in range(XROWS // 8):
            value = jnp.take_along_axis(columns[8 * i : 8 * i + 8], at, axis=1)
            left.append(jnp.where(same, value, 0.0))
    poly_ref[...] = lax.dot_general(
        jnp.concatenate(left, axis=0).astype(BF16),
        weight_ref[...],
        (((1,), (0,)), ((), ())),
        preferred_element_type=F32,
    )
    core = lax.axis_index("vel") % 2
    found = [got_ref[half, 3 + core] for half in range(2)]

    lane = lax.broadcasted_iota(jnp.int32, (8, LANES), 1)
    cell = (lane >> 3) & 7
    source = 16 * sublane((8, LANES)) + 4 * (cell >> 1) + (cell & 1)
    speed = stream_x * SPACING * ((lane & 7).astype(F32) + 0.5)
    chunk_gain = jnp.ones((8, LANES), F32)
    for x in range(DEPTH):
        rate = jnp.broadcast_to(rates[x], (8, LANES))
        rate = jnp.take_along_axis(rate, source, axis=1)
        chunk_gain = chunk_gain * (speed / (1.0 + speed + rate))
    for to in range(copies * CHUNKS):
        at = to % CHUNKS
        send_ref[pl.ds(CHUNK_ROWS * ORDER.index(to) + 16, 1), :] = chunk_gain[at : at + 1]

    x1, x2, x3 = pattern_ref[0], pattern_ref[1], pattern_ref[2]
    ahead = x1 > 0
    upward = x2 > 0
    sigma = stream_x * jnp.abs(x1)
    sigma1 = 1.0 + sigma
    flux_y = stream_y * jnp.abs(x2)
    flux_z = stream_z * jnp.abs(x3)
    own = 1.0 - flux_y - flux_z
    row = sublane((8, LANES))
    first_plane = (row & 1) == 0
    lower = row < 4
    here = lax.axis_index("space")
    edge = here == jnp.where(ahead, 0, lax.axis_size("space") - 1)

    ghosts = []
    for x in range(DEPTH):
        wall = found[x // 2]
        at = 2 * (x % 2)
        four = jnp.concatenate([wall[at : at + 2], wall[at + 4 : at + 6]], axis=0)
        ghosts.append(jnp.concatenate([four, four], axis=0))

    for i in range(XROWS // 8):
        a, b, target = [], [], []
        for x in range(DEPTH):
            def column(q):
                at = 108 + 4 * (x // 2) + 2 * q + x % 2
                return jnp.broadcast_to(
                    columns[8 * i : 8 * i + 8, at : at + 1], (8, LANES)
                )

            base = x * XROWS + 8 * i
            f = f_ref[pl.ds(base, 8), :]
            ratio = poly_ref[pl.ds(base, 8), 0:LANES]
            along = poly_ref[pl.ds(base, 8), LANES : 2 * LANES]
            shakhov = column(0) * jnp.exp(-0.5 * ratio) * (1.0 + along * (ratio - 5.0))
            rate = column(1)

            def ghost(wall):
                mask = pattern_ref[3 + 2 * x + wall]
                return jnp.where(mask == 1.0, ghosts[x], shakhov)

            if i == 0:
                below = jnp.where(lower, ghost(0), pltpu.roll(f, 4, 0))
            else:
                below = f_ref[pl.ds(base - 4, 8), :]
            if i == XROWS // 8 - 1:
                above = jnp.where(lower, pltpu.roll(f, 4, 0), ghost(1))
            else:
                above = f_ref[pl.ds(base + 4, 8), :]
            upwind = jnp.where(upward, below, above)
            other = jnp.where(first_plane, pltpu.roll(f, 7, 0), pltpu.roll(f, 1, 0))
            inverse = 1.0 / (sigma1 + rate)
            a.append(sigma * inverse)
            b.append(
                (own * f + rate * shakhov + flux_y * upwind + flux_z * other) * inverse
            )
            target.append(shakhov)
        order = lambda v, t: jnp.where(ahead, v[t], v[DEPTH - 1 - t])
        a0 = order(a, 0)
        hold = order(b, 0) + jnp.where(edge, a0 * order(target, 0), 0.0)
        gain = jnp.where(edge, 0.0, a0)
        a_ref[pl.ds(8 * i, 8), :] = gain
        h_ref[pl.ds(8 * i, 8), :] = hold
        for t in range(1, DEPTH):
            at = order(a, t)
            gain = at * gain
            hold = at * hold + order(b, t)
            a_ref[pl.ds(t * XROWS + 8 * i, 8), :] = gain
            h_ref[pl.ds(t * XROWS + 8 * i, 8), :] = hold
        for copy in range(copies):
            to = copy * CHUNKS + i // 2
            send_ref[pl.ds(CHUNK_ROWS * ORDER.index(to) + 8 * (i % 2), 8), :] = hold


def chain_kernel(copies, got_ref, pattern_ref, out_ref, gain_ref, keep_ref):
    blocks = copies * CHUNKS
    ahead = pattern_ref[0] > 0
    which = (jnp.abs(pattern_ref[0]) * (1.0 / SPACING) - 0.5).astype(jnp.int32)
    row = sublane((8, LANES))
    for half in range(2):
        cell = 2 * (2 * half + (row >> 2)) + (row & 1)
        source = 8 * cell + which
        for k in range(blocks):
            gain = jnp.broadcast_to(got_ref[pl.ds(CHUNK_ROWS * ORDER.index(k) + 16, 1), :], (8, LANES))
            gain_ref[k] = jnp.take_along_axis(gain, source, axis=1)
        enter = jnp.zeros((8, LANES), F32)
        for k in range(blocks):
            keep_ref[half, k] = enter
            back = blocks - 1 - k
            gain = jnp.where(ahead, gain_ref[k], gain_ref[back])
            hold = jnp.where(
                ahead,
                got_ref[pl.ds(CHUNK_ROWS * ORDER.index(k) + 8 * half, 8), :],
                got_ref[pl.ds(CHUNK_ROWS * ORDER.index(back) + 8 * half, 8), :],
            )
            enter = gain * enter + hold
    first = lax.axis_index("space") // CHUNKS * CHUNKS
    for half in range(2):
        for x in range(CHUNKS):
            out_ref[LINE.index(x), pl.ds(8 * half, 8), :] = jnp.where(
                ahead, keep_ref[half, first + x], keep_ref[half, blocks - 1 - x - first]
            )


def finish_kernel(enter_ref, a_ref, h_ref, pattern_ref, out_hbm, out_ref, sem):
    ahead = pattern_ref[0] > 0
    copies = []
    for x, mate in ((0, DEPTH - 1), (1, DEPTH - 2)):
        for i in range(XROWS // 8):
            enter = enter_ref[pl.ds(16 * LINE.index(i // 2) + 8 * (i % 2), 8), :]
            value = []
            for t in (x, mate):
                at = pl.ds(t * XROWS + 8 * i, 8)
                value.append(a_ref[at, :] * enter + h_ref[at, :])
            out_ref[pl.ds(x * XROWS + 8 * i, 8), :] = jnp.where(ahead, value[0], value[1])
            out_ref[pl.ds(mate * XROWS + 8 * i, 8), :] = jnp.where(ahead, value[1], value[0])
        for t in (x, mate):
            rows = pl.ds(t * XROWS, XROWS)
            copies.append(pltpu.make_async_copy(out_ref.at[rows], out_hbm.at[rows], sem.at[t]))
            copies[-1].start()
    for copy in copies:
        copy.wait()


ON_CHIP = pl.BlockSpec(memory_space=pltpu.VMEM)
ANYWHERE = pl.BlockSpec(memory_space=pl.ANY)


def held(x):
    return pltpu.with_memory_space_constraint(x, pltpu.VMEM)


def shards(distribution, wall_mask, grid_point, mirror_slot):
    blocks = lax.axis_size("space")
    copies = blocks // CHUNKS
    f = distribution.reshape(DEPTH, ROWS, PLANES, 2, LANES)
    f = f.transpose(0, 1, 3, 2, 4).reshape(DEPTH * XROWS, LANES)
    point = grid_point.reshape(2, LANES)
    mirror = mirror_slot.reshape(2, LANES)
    wall = wall_mask.transpose(1, 2, 0)

    sources = lax.axis_size("vel")
    shares, kept, pattern, weights = pl.pallas_call(
        moments_kernel,
        out_shape=[
            pltpu.VMEM((sources * SHARE, LANES), F32),
            pltpu.VMEM((DEPTH * XROWS, LANES), F32),
            pltpu.VMEM((3 + 2 * DEPTH, 8, LANES), F32),
            pltpu.VMEM((LANES, 2 * LANES), BF16),
        ],
        in_specs=[ANYWHERE] * 4,
        out_specs=[ON_CHIP] * 4,
        scratch_shapes=[
            pltpu.VMEM((2, 24, LANES), F32),
            pltpu.VMEM((2, LANES), jnp.int32),
            pltpu.VMEM((2, LANES), jnp.int32),
            pltpu.VMEM((2, PLANES, DEPTH), jnp.int32),
            pltpu.SemaphoreType.DMA((2,)),
            pltpu.SemaphoreType.DMA((3,)),
        ],
    )(f, point, mirror, wall)
    partial = lax.all_to_all(
        shares.reshape(sources, 1, SHARE * LANES),
        "vel",
        0,
        0,
        axis_index_groups=[VELO],
        tiled=True,
    ).reshape(sources * SHARE, LANES)
    cells = pl.pallas_call(
        lambda *refs: cells_kernel(sources, *refs),
        out_shape=pltpu.VMEM((5, 8, LANES), F32),
        in_specs=[ON_CHIP],
        out_specs=ON_CHIP,
    )(held(partial))
    pairs = [[k, k + 1] for k in range(0, sources, 2)]
    everyone = lax.all_gather(cells, "vel", axis_index_groups=pairs)
    send, gains, holds = pl.pallas_call(
        lambda *refs: blocks_kernel(copies, *refs),
        out_shape=[
            pltpu.VMEM((blocks * CHUNK_ROWS, LANES), F32),
            pltpu.VMEM((DEPTH * XROWS, LANES), F32),
            pltpu.VMEM((DEPTH * XROWS, LANES), F32),
        ],
        in_specs=[ON_CHIP] * 4,
        out_specs=[ON_CHIP] * 3,
        scratch_shapes=[pltpu.VMEM((DEPTH * XROWS, 2 * LANES), F32)],
    )(held(everyone), held(kept), held(pattern), held(weights))
    chain = lax.all_to_all(
        send.reshape(blocks, 1, CHUNK_ROWS * LANES), "space", 0, 0, axis_index_groups=[ORDER], tiled=True
    ).reshape(blocks * CHUNK_ROWS, LANES)
    enters = pl.pallas_call(
        lambda *refs: chain_kernel(copies, *refs),
        out_shape=pltpu.VMEM((CHUNKS, 16, LANES), F32),
        in_specs=[ON_CHIP] * 2,
        out_specs=ON_CHIP,
        scratch_shapes=[
            pltpu.VMEM((blocks, 8, LANES), F32),
            pltpu.VMEM((2, blocks, 8, LANES), F32),
        ],
    )(held(chain), held(pattern))
    lines = [[CHUNKS * z + x for x in LINE] for z in range(copies)]
    enter = lax.all_to_all(enters, "space", 0, 0, axis_index_groups=lines, tiled=True)
    out = pl.pallas_call(
        finish_kernel,
        out_shape=jax.ShapeDtypeStruct((DEPTH * XROWS, LANES), F32),
        in_specs=[ON_CHIP] * 4,
        out_specs=ANYWHERE,
        scratch_shapes=[
            pltpu.VMEM((DEPTH * XROWS, LANES), F32),
            pltpu.SemaphoreType.DMA((DEPTH,)),
        ],
    )(held(enter.reshape(XROWS, LANES)), held(gains), held(holds), held(pattern))
    out = out.reshape(DEPTH, ROWS, 2, PLANES, LANES).transpose(0, 1, 3, 2, 4)
    return out.reshape(DEPTH, ROWS, PLANES, WIDTH)


def solution(mesh):
    placed = (P("space", None, None, "vel"), P("space", None, None), P("vel"), P("vel"))
    return jax.shard_map(
        shards, mesh=mesh, in_specs=placed, out_specs=P("space", None, None, "vel"), check_vma=False
    )
```

```python
import math

import jax
import jax.numpy as jnp
from jax import lax
from jax.experimental import pallas as pl
from jax.experimental.pallas import tpu as pltpu
from jax.sharding import PartitionSpec as P

VS = 16
SPACING = 8.0 / VS
HALF = (VS - 1) / 2.0
WEIGHT = SPACING**3

stream_x = 40.0
stream_y = 0.15
stream_z = 0.05
relaxation_multiplier = 0.05
shear_power_index = 0.81
diffusivity_ratio = 2.0 / 3.0

DEPTH, ROWS, PLANES, WIDTH = 4, 32, 2, 256
LANES = 128
XROWS = ROWS * 2 * PLANES
F32 = jnp.float32
BF16 = jnp.bfloat16

CHUNKS = 8
CHUNK_ROWS = 17

VELO = [*range(9, -1, -1), *range(15, 9, -1)]
ORDER = list(range(31, -1, -1))
LINE = [6, 5, 4, 3, 2, 1, 0, 7]

SHARE = 23


def velocity(points):
    first = (points >> 8).astype(F32)
    second = ((points >> 4) & 15).astype(F32)
    third = (points & 15).astype(F32)
    return [(v - HALF) * SPACING for v in (first, second, third)]


def sublane(shape):
    return lax.broadcasted_iota(jnp.int32, shape, 0)


def by_half(pair):
    low = jnp.broadcast_to(pair[0:1], (8, LANES))
    high = jnp.broadcast_to(pair[1:2], (8, LANES))
    return jnp.where((sublane((8, LANES)) & 2) == 0, low, high)


def moments_kernel(
    f_hbm, point_hbm, mirror_hbm, wall_hbm,
    send_ref, f_ref, pattern_ref, weight_ref,
    half_ref, point_ref, mirror_ref, wall_ref, f_sem, small_sem,
):
    small = [
        pltpu.make_async_copy(src, dst, small_sem.at[k])
        for k, (src, dst) in enumerate(
            [(point_hbm, point_ref), (wall_hbm, wall_ref), (mirror_hbm, mirror_ref)]
        )
    ]
    for copy in small:
        copy.start()
    chunks = []
    for x in range(2):
        rows = pl.ds(2 * x * XROWS, 2 * XROWS)
        chunks.append(pltpu.make_async_copy(f_hbm.at[rows], f_ref.at[rows], f_sem.at[x]))
        chunks[x].start()

    small[0].wait()
    points = point_ref[...]
    tables = []
    for half in range(2):
        x1, x2, x3 = velocity(points[half : half + 1])
        square = x1 * x1 + x2 * x2 + x3 * x3
        cubes = [x1 * square, x2 * square, x3 * square]
        coarse = [c.astype(BF16).astype(F32) for c in cubes]
        tables += [
            jnp.ones_like(x1), x1, x2, x3,
            x1 * x1, x2 * x2, x3 * x3, x1 * x2,
            x1 * x3, x2 * x3, *coarse,
            *[c - r for c, r in zip(cubes, coarse)],
        ]
    weights = []
    for half in range(2):
        x1, x2, x3 = velocity(points[half : half + 1])
        square = x1 * x1 + x2 * x2 + x3 * x3
        coarse = square.astype(BF16).astype(F32)
        one, zero = jnp.ones_like(x1), jnp.zeros_like(x1)
        left = [one, x1, x2, x3, coarse, square - coarse] + [zero] * 10
        right = [zero] * 6 + [one, x1, x2, x3] + [zero] * 6
        weights += [jnp.concatenate(pair, axis=1) for pair in zip(left, right)]
    weights = jnp.concatenate(weights, axis=0).astype(BF16)
    weight_ref[...] = jnp.concatenate([weights] * 3 + [jnp.zeros_like(weights)], axis=0)
    table = jnp.concatenate(tables, axis=0).astype(BF16)
    table = jnp.concatenate([table] * 3, axis=1)
    low_lane = (lax.broadcasted_iota(jnp.int32, (8, LANES), 1) & 2) == 0
    pairs = velocity(points)
    for k in range(3):
        pattern_ref[k] = by_half(pairs[k])
    small[1].wait()
    for x in range(DEPTH):
        for wall in range(2):
            planes = wall_ref[wall, :, x : x + 1].astype(F32)
            planes = jnp.broadcast_to(planes, (PLANES, LANES))
            pattern_ref[3 + 2 * x + wall] = jnp.concatenate([planes] * 4, axis=0)
    small[2].wait()
    for core in range(2):
        half_ref[core, 21:23, :] = mirror_ref[...].astype(F32)

    x2 = pairs[1]
    for x in range(DEPTH):
        if x % 2 == 0:
            chunks[x // 2].wait()
            f = f_ref[pl.ds(x * XROWS, 2 * XROWS), :]
            high = f.astype(BF16)
            rest = f - high.astype(F32)
            middle = rest.astype(BF16)
            low = (rest - middle.astype(F32)).astype(BF16)
            both = lax.dot_general(
                table,
                jnp.concatenate([high, middle, low], axis=1),
                (((1,), (1,)), ((), ())),
                preferred_element_type=F32,
            )
        sums = both[:, XROWS * (x % 2) : XROWS * (x % 2 + 1)]
        packed = jnp.where(
            low_lane,
            sums[0:8] + pltpu.roll(sums[16:24], LANES - 2, 1),
            sums[24:32] + pltpu.roll(sums[8:16], 2, 1),
        )
        core, second = divmod(x, 2)
        tail = packed[5:8]
        half_ref[core, pl.ds(5 * second, 2), :] = packed[0:2]
        half_ref[core, pl.ds(5 * second + 2, 3), :] = packed[2:5] + jnp.where(
            low_lane[0:3], 0.0, tail
        )
        if second:
            half_ref[core, 10:13, :] = jnp.where(
                low_lane[0:3], before, pltpu.roll(packed, 2, 1)[5:8]
            )
        before = tail
        for half in range(2):
            low = f_ref[pl.ds(x * XROWS + 2 * half, 2), :]
            high = f_ref[pl.ds((x + 1) * XROWS - 4 + 2 * half, 2), :]
            half_ref[core, pl.ds(13 + 4 * half + 2 * second, 2), :] = jnp.where(
                x2[half : half + 1] < 0, low, high
            )
        if second:
            for to in [p for p in range(16) if VELO[p] % 2 == core]:
                send_ref[pl.ds(SHARE * to, SHARE), :] = half_ref[core, 0:SHARE, :]


def cell_quantities(sums):
    low_lane = (lax.broadcasted_iota(jnp.int32, (2, LANES), 1) & 2) == 0
    low, high = [], []
    for m in range(8):
        if m < 5:
            own = jnp.concatenate([sums[m : m + 1], sums[5 + m : 6 + m]], axis=0)
            own = own * WEIGHT
            other = jnp.where(
                low_lane, pltpu.roll(own, LANES - 2, 1), pltpu.roll(own, 2, 1)
            )
            low.append(jnp.where(low_lane, own, other))
            high.append(jnp.where(low_lane, other, own))
        else:
            own = jnp.broadcast_to(sums[5 + m : 6 + m], (2, LANES)) * WEIGHT
            first = jnp.where(low_lane, own, pltpu.roll(own, 2, 1))
            second = jnp.where(low_lane, pltpu.roll(own, LANES - 2, 1), own)
            low.append(jnp.where(sublane((2, LANES)) == 0, first, second))
    n = low[0]
    inv = 1.0 / n
    u = [low[1 + k] * inv for k in range(3)]
    pressure = {(0, 0): low[4], (1, 1): low[5], (2, 2): low[6]}
    pressure.update({(0, 1): low[7], (0, 2): high[0], (1, 2): high[1]})
    energy = low[4] + low[5] + low[6]
    speed = u[0] * u[0] + u[1] * u[1] + u[2] * u[2]
    temperature = (energy - n * speed) * inv * (1.0 / 3.0)
    heat = []
    for k in range(3):
        cross = sum(u[j] * pressure[min(j, k), max(j, k)] for j in range(3))
        heat.append(0.5 * (high[2 + k] - 2.0 * cross + u[k] * (2.0 * n * speed - energy)))
    inv_t = 1.0 / temperature
    scale = (1.0 - diffusivity_ratio) / 5.0 * inv * inv_t * inv_t
    arg = 2.0 * math.pi * temperature
    norm = n / (arg * jnp.sqrt(arg))
    heat = [h * scale for h in heat]
    rate = relaxation_multiplier * n * jnp.exp((1.0 - shear_power_index) * jnp.log(temperature))
    ratio = [speed * inv_t] + [-2.0 * v * inv_t for v in u] + [inv_t]
    along = [-(u[0] * heat[0] + u[1] * heat[1] + u[2] * heat[2])] + heat
    return ratio + along + [norm, rate]


def cells_kernel(sources, got_ref, out_ref):
    sums = got_ref[pl.ds(0, 16), :]
    for k in range(1, sources):
        sums = sums + got_ref[pl.ds(SHARE * k, 16), :]
    quantities = cell_quantities(sums)
    filler = jnp.zeros((24 - 2 * len(quantities), LANES), F32)
    table = jnp.concatenate(quantities + [filler], axis=0)
    for k in range(3):
        out_ref[k] = table[8 * k : 8 * k + 8]

    upper = (sublane((8, LANES)) >> 2) & 1
    chip = lax.axis_index("vel") // 2
    lanes, kept, rolled, values = [], [], [], []
    for core in range(2):
        at = SHARE * ((9 - 2 * chip - core) % 16) + 21
        first = jnp.broadcast_to(got_ref[pl.ds(at, 1), :], (8, LANES))
        second = jnp.broadcast_to(got_ref[pl.ds(at + 1, 1), :], (8, LANES))
        slot = jnp.where(upper == 0, first, second).astype(jnp.int32)
        lanes.append(slot & (LANES - 1))
        kept.append((slot >> 7) - upper)
        rolled.append((slot >> 7) + upper)
        values.append(jnp.zeros((8, LANES), F32))
    for k in range(sources):
        piece = got_ref[pl.ds(SHARE * k + 13, 8), :]
        swapped = pltpu.roll(piece, 4, 0)
        owner = VELO[k]
        for core in range(2):
            there = jnp.take_along_axis(piece, lanes[core], axis=1)
            across = jnp.take_along_axis(swapped, lanes[core], axis=1)
            value = jnp.where(kept[core] == 2 * owner, there, values[core])
            values[core] = jnp.where(rolled[core] == 2 * owner + 1, across, value)
    for core in range(2):
        out_ref[3 + core] = values[core]


def blocks_kernel(
    copies, got_ref, f_ref, pattern_ref, weight_ref, send_ref, a_ref, h_ref, poly_ref
):
    halves = [
        jnp.concatenate([got_ref[half, k] for k in range(3)], axis=0) for half in range(2)
    ]
    rates = [halves[x // 2][20 + x % 2 : 21 + x % 2] for x in range(DEPTH)]
    rows, left = [], halves
    for part in range(3):
        pieces = [h.astype(BF16).astype(F32) for h in left]
        rows += [p[0:18] for p in pieces]
        left = [h - p for h, p in zip(left, pieces)]
    rows += [h[18:22] for h in halves]
    filler = jnp.zeros((LANES - 116, LANES), F32)
    columns = jnp.concatenate(rows + [filler], axis=0).T

    lane = lax.broadcasted_iota(jnp.int32, (8, LANES), 1)
    term = lane & 15
    term = jnp.where(term > 9, 0, jnp.where(term > 4, term - 1, term))
    source = 36 * jnp.where(lane < 96, lane >> 5, 0) + 2 * term
    same = ((sublane((8, LANES)) >> 1) & 1) == ((lane >> 4) & 1)
    left = []
    for x in range(DEPTH):
        at = source + (18 * (x // 2) + x % 2)
        for i in range(XROWS // 8):
            value = jnp.take_along_axis(columns[8 * i : 8 * i + 8], at, axis=1)
            left.append(jnp.where(same, value, 0.0))
    poly_ref[...] = lax.dot_general(
        jnp.concatenate(left, axis=0).astype(BF16),
        weight_ref[...],
        (((1,), (0,)), ((), ())),
        preferred_element_type=F32,
    )
    core = lax.axis_index("vel") % 2
    found = [got_ref[half, 3 + core] for half in range(2)]

    lane = lax.broadcasted_iota(jnp.int32, (8, LANES), 1)
    cell = (lane >> 3) & 7
    source = 16 * sublane((8, LANES)) + 4 * (cell >> 1) + (cell & 1)
    speed = stream_x * SPACING * ((lane & 7).astype(F32) + 0.5)
    chunk_gain = jnp.ones((8, LANES), F32)
    for x in range(DEPTH):
        rate = jnp.broadcast_to(rates[x], (8, LANES))
        rate = jnp.take_along_axis(rate, source, axis=1)
        chunk_gain = chunk_gain * (speed / (1.0 + speed + rate))
    for to in range(copies * CHUNKS):
        at = to % CHUNKS
        send_ref[pl.ds(CHUNK_ROWS * ORDER.index(to) + 16, 1), :] = chunk_gain[at : at + 1]

    x1, x2, x3 = pattern_ref[0], pattern_ref[1], pattern_ref[2]
    ahead = x1 > 0
    upward = x2 > 0
    sigma = stream_x * jnp.abs(x1)
    sigma1 = 1.0 + sigma
    flux_y = stream_y * jnp.abs(x2)
    flux_z = stream_z * jnp.abs(x3)
    own = 1.0 - flux_y - flux_z
    row = sublane((8, LANES))
    first_plane = (row & 1) == 0
    lower = row < 4
    here = lax.axis_index("space")
    edge = here == jnp.where(ahead, 0, lax.axis_size("space") - 1)

    ghosts = []
    for x in range(DEPTH):
        wall = found[x // 2]
        at = 2 * (x % 2)
        four = jnp.concatenate([wall[at : at + 2], wall[at + 4 : at + 6]], axis=0)
        ghosts.append(jnp.concatenate([four, four], axis=0))

    for i in range(XROWS // 8):
        a, b, target = [], [], []
        for x in range(DEPTH):
            def column(q):
                at = 108 + 4 * (x // 2) + 2 * q + x % 2
                return jnp.broadcast_to(
                    columns[8 * i : 8 * i + 8, at : at + 1], (8, LANES)
                )

            base = x * XROWS + 8 * i
            f = f_ref[pl.ds(base, 8), :]
            ratio = poly_ref[pl.ds(base, 8), 0:LANES]
            along = poly_ref[pl.ds(base, 8), LANES : 2 * LANES]
            shakhov = column(0) * jnp.exp(-0.5 * ratio) * (1.0 + along * (ratio - 5.0))
            rate = column(1)

            def ghost(wall):
                mask = pattern_ref[3 + 2 * x + wall]
                return jnp.where(mask == 1.0, ghosts[x], shakhov)

            if i == 0:
                below = jnp.where(lower, ghost(0), pltpu.roll(f, 4, 0))
            else:
                below = f_ref[pl.ds(base - 4, 8), :]
            if i == XROWS // 8 - 1:
                above = jnp.where(lower, pltpu.roll(f, 4, 0), ghost(1))
            else:
                above = f_ref[pl.ds(base + 4, 8), :]
            upwind = jnp.where(upward, below, above)
            other = jnp.where(first_plane, pltpu.roll(f, 7, 0), pltpu.roll(f, 1, 0))
            inverse = 1.0 / (sigma1 + rate)
            a.append(sigma * inverse)
            b.append(
                (own * f + rate * shakhov + flux_y * upwind + flux_z * other) * inverse
            )
            target.append(shakhov)
        order = lambda v, t: jnp.where(ahead, v[t], v[DEPTH - 1 - t])
        a0 = order(a, 0)
        hold = order(b, 0) + jnp.where(edge, a0 * order(target, 0), 0.0)
        gain = jnp.where(edge, 0.0, a0)
        a_ref[pl.ds(8 * i, 8), :] = gain
        h_ref[pl.ds(8 * i, 8), :] = hold
        for t in range(1, DEPTH):
            at = order(a, t)
            gain = at * gain
            hold = at * hold + order(b, t)
            a_ref[pl.ds(t * XROWS + 8 * i, 8), :] = gain
            h_ref[pl.ds(t * XROWS + 8 * i, 8), :] = hold
        for copy in range(copies):
            to = copy * CHUNKS + i // 2
            send_ref[pl.ds(CHUNK_ROWS * ORDER.index(to) + 8 * (i % 2), 8), :] = hold


def chain_kernel(copies, got_ref, pattern_ref, out_ref, gain_ref, keep_ref):
    blocks = copies * CHUNKS
    ahead = pattern_ref[0] > 0
    which = (jnp.abs(pattern_ref[0]) * (1.0 / SPACING) - 0.5).astype(jnp.int32)
    row = sublane((8, LANES))
    for half in range(2):
        cell = 2 * (2 * half + (row >> 2)) + (row & 1)
        source = 8 * cell + which
        for k in range(blocks):
            gain = jnp.broadcast_to(got_ref[pl.ds(CHUNK_ROWS * ORDER.index(k) + 16, 1), :], (8, LANES))
            gain_ref[k] = jnp.take_along_axis(gain, source, axis=1)
        enter = jnp.zeros((8, LANES), F32)
        for k in range(blocks):
            keep_ref[half, k] = enter
            back = blocks - 1 - k
            gain = jnp.where(ahead, gain_ref[k], gain_ref[back])
            hold = jnp.where(
                ahead,
                got_ref[pl.ds(CHUNK_ROWS * ORDER.index(k) + 8 * half, 8), :],
                got_ref[pl.ds(CHUNK_ROWS * ORDER.index(back) + 8 * half, 8), :],
            )
            enter = gain * enter + hold
    first = lax.axis_index("space") // CHUNKS * CHUNKS
    for half in range(2):
        for x in range(CHUNKS):
            out_ref[LINE.index(x), pl.ds(8 * half, 8), :] = jnp.where(
                ahead, keep_ref[half, first + x], keep_ref[half, blocks - 1 - x - first]
            )


def finish_kernel(enter_ref, a_ref, h_ref, pattern_ref, out_hbm, out_ref, sem):
    ahead = pattern_ref[0] > 0
    copies = []
    for x, mate in ((0, DEPTH - 1), (1, DEPTH - 2)):
        for i in range(XROWS // 8):
            enter = enter_ref[pl.ds(16 * LINE.index(i // 2) + 8 * (i % 2), 8), :]
            value = []
            for t in (x, mate):
                at = pl.ds(t * XROWS + 8 * i, 8)
                value.append(a_ref[at, :] * enter + h_ref[at, :])
            out_ref[pl.ds(x * XROWS + 8 * i, 8), :] = jnp.where(ahead, value[0], value[1])
            out_ref[pl.ds(mate * XROWS + 8 * i, 8), :] = jnp.where(ahead, value[1], value[0])
        for t in (x, mate):
            rows = pl.ds(t * XROWS, XROWS)
            copies.append(pltpu.make_async_copy(out_ref.at[rows], out_hbm.at[rows], sem.at[t]))
            copies[-1].start()
    for copy in copies:
        copy.wait()


ON_CHIP = pl.BlockSpec(memory_space=pltpu.VMEM)
ANYWHERE = pl.BlockSpec(memory_space=pl.ANY)


def held(x):
    return pltpu.with_memory_space_constraint(x, pltpu.VMEM)


def shards(distribution, wall_mask, grid_point, mirror_slot):
    blocks = lax.axis_size("space")
    copies = blocks // CHUNKS
    f = distribution.reshape(DEPTH, ROWS, PLANES, 2, LANES)
    f = f.transpose(0, 1, 3, 2, 4).reshape(DEPTH * XROWS, LANES)
    point = grid_point.reshape(2, LANES)
    mirror = mirror_slot.reshape(2, LANES)
    wall = wall_mask.transpose(1, 2, 0)

    sources = lax.axis_size("vel")
    shares, kept, pattern, weights = pl.pallas_call(
        moments_kernel,
        out_shape=[
            pltpu.VMEM((sources * SHARE, LANES), F32),
            pltpu.VMEM((DEPTH * XROWS, LANES), F32),
            pltpu.VMEM((3 + 2 * DEPTH, 8, LANES), F32),
            pltpu.VMEM((LANES, 2 * LANES), BF16),
        ],
        in_specs=[ANYWHERE] * 4,
        out_specs=[ON_CHIP] * 4,
        scratch_shapes=[
            pltpu.VMEM((2, 24, LANES), F32),
            pltpu.VMEM((2, LANES), jnp.int32),
            pltpu.VMEM((2, LANES), jnp.int32),
            pltpu.VMEM((2, PLANES, DEPTH), jnp.int32),
            pltpu.SemaphoreType.DMA((2,)),
            pltpu.SemaphoreType.DMA((3,)),
        ],
    )(f, point, mirror, wall)
    partial = lax.all_to_all(
        shares.reshape(sources, 1, SHARE * LANES),
        "vel",
        0,
        0,
        axis_index_groups=[VELO],
        tiled=True,
    ).reshape(sources * SHARE, LANES)
    cells = pl.pallas_call(
        lambda *refs: cells_kernel(sources, *refs),
        out_shape=pltpu.VMEM((5, 8, LANES), F32),
        in_specs=[ON_CHIP],
        out_specs=ON_CHIP,
    )(held(partial))
    pairs = [[k, k + 1] for k in range(0, sources, 2)]
    everyone = lax.all_gather(cells, "vel", axis_index_groups=pairs)
    send, gains, holds = pl.pallas_call(
        lambda *refs: blocks_kernel(copies, *refs),
        out_shape=[
            pltpu.VMEM((blocks * CHUNK_ROWS, LANES), F32),
            pltpu.VMEM((DEPTH * XROWS, LANES), F32),
            pltpu.VMEM((DEPTH * XROWS, LANES), F32),
        ],
        in_specs=[ON_CHIP] * 4,
        out_specs=[ON_CHIP] * 3,
        scratch_shapes=[pltpu.VMEM((DEPTH * XROWS, 2 * LANES), F32)],
    )(held(everyone), held(kept), held(pattern), held(weights))
    chain = lax.all_to_all(
        send.reshape(blocks, 1, CHUNK_ROWS * LANES), "space", 0, 0, axis_index_groups=[ORDER], tiled=True
    ).reshape(blocks * CHUNK_ROWS, LANES)
    enters = pl.pallas_call(
        lambda *refs: chain_kernel(copies, *refs),
        out_shape=pltpu.VMEM((CHUNKS, 16, LANES), F32),
        in_specs=[ON_CHIP] * 2,
        out_specs=ON_CHIP,
        scratch_shapes=[
            pltpu.VMEM((blocks, 8, LANES), F32),
            pltpu.VMEM((2, blocks, 8, LANES), F32),
        ],
    )(held(chain), held(pattern))
    lines = [[CHUNKS * z + x for x in LINE] for z in range(copies)]
    enter = lax.all_to_all(enters, "space", 0, 0, axis_index_groups=lines, tiled=True)
    out = pl.pallas_call(
        finish_kernel,
        out_shape=jax.ShapeDtypeStruct((DEPTH * XROWS, LANES), F32),
        in_specs=[ON_CHIP] * 4,
        out_specs=ANYWHERE,
        scratch_shapes=[
            pltpu.VMEM((DEPTH * XROWS, LANES), F32),
            pltpu.SemaphoreType.DMA((DEPTH,)),
        ],
    )(held(enter.reshape(XROWS, LANES)), held(gains), held(holds), held(pattern))
    out = out.reshape(DEPTH, ROWS, 2, PLANES, LANES).transpose(0, 1, 3, 2, 4)
    return out.reshape(DEPTH, ROWS, PLANES, WIDTH)


def solution(mesh):
    placed = (P("space", None, None, "vel"), P("space", None, None), P("vel"), P("vel"))
    return jax.shard_map(
        shards, mesh=mesh, in_specs=placed, out_specs=P("space", None, None, "vel"), check_vma=False
    )
```

```python
import math

import jax
import jax.numpy as jnp
from jax import lax
from jax.experimental import pallas as pl
from jax.experimental.pallas import tpu as pltpu
from jax.sharding import PartitionSpec as P

VS = 16
SPACING = 8.0 / VS
HALF = (VS - 1) / 2.0
WEIGHT = SPACING**3

stream_x = 40.0
stream_y = 0.15
stream_z = 0.05
relaxation_multiplier = 0.05
shear_power_index = 0.81
diffusivity_ratio = 2.0 / 3.0

DEPTH, ROWS, PLANES, WIDTH = 4, 32, 2, 256
LANES = 128
XROWS = ROWS * 2 * PLANES
F32 = jnp.float32
BF16 = jnp.bfloat16

CHUNKS = 8
CHUNK_ROWS = 17

VELO = [*range(9, -1, -1), *range(15, 9, -1)]
LINE = [6, 5, 4, 3, 2, 1, 0, 7]
ORDER = [8 * z + x for z in range(3, -1, -1) for x in LINE]

SHARE = 23


def velocity(points):
    first = (points >> 8).astype(F32)
    second = ((points >> 4) & 15).astype(F32)
    third = (points & 15).astype(F32)
    return [(v - HALF) * SPACING for v in (first, second, third)]


def sublane(shape):
    return lax.broadcasted_iota(jnp.int32, shape, 0)


def by_half(pair):
    low = jnp.broadcast_to(pair[0:1], (8, LANES))
    high = jnp.broadcast_to(pair[1:2], (8, LANES))
    return jnp.where((sublane((8, LANES)) & 2) == 0, low, high)


def moments_kernel(
    f_hbm, point_hbm, mirror_hbm, wall_hbm,
    send_ref, f_ref, pattern_ref, weight_ref,
    half_ref, point_ref, mirror_ref, wall_ref, f_sem, small_sem,
):
    small = [
        pltpu.make_async_copy(src, dst, small_sem.at[k])
        for k, (src, dst) in enumerate(
            [(point_hbm, point_ref), (wall_hbm, wall_ref), (mirror_hbm, mirror_ref)]
        )
    ]
    for copy in small:
        copy.start()
    chunks = []
    for x in range(2):
        rows = pl.ds(2 * x * XROWS, 2 * XROWS)
        chunks.append(pltpu.make_async_copy(f_hbm.at[rows], f_ref.at[rows], f_sem.at[x]))
        chunks[x].start()

    small[0].wait()
    points = point_ref[...]
    tables = []
    for half in range(2):
        x1, x2, x3 = velocity(points[half : half + 1])
        square = x1 * x1 + x2 * x2 + x3 * x3
        cubes = [x1 * square, x2 * square, x3 * square]
        coarse = [c.astype(BF16).astype(F32) for c in cubes]
        tables += [
            jnp.ones_like(x1), x1, x2, x3,
            x1 * x1, x2 * x2, x3 * x3, x1 * x2,
            x1 * x3, x2 * x3, *coarse,
            *[c - r for c, r in zip(cubes, coarse)],
        ]
    weights = []
    for half in range(2):
        x1, x2, x3 = velocity(points[half : half + 1])
        square = x1 * x1 + x2 * x2 + x3 * x3
        coarse = square.astype(BF16).astype(F32)
        one, zero = jnp.ones_like(x1), jnp.zeros_like(x1)
        left = [one, x1, x2, x3, coarse, square - coarse] + [zero] * 10
        right = [zero] * 6 + [one, x1, x2, x3] + [zero] * 6
        weights += [jnp.concatenate(pair, axis=1) for pair in zip(left, right)]
    weights = jnp.concatenate(weights, axis=0).astype(BF16)
    weight_ref[...] = jnp.concatenate([weights] * 3 + [jnp.zeros_like(weights)], axis=0)
    table = jnp.concatenate(tables, axis=0).astype(BF16)
    table = jnp.concatenate([table] * 3, axis=1)
    low_lane = (lax.broadcasted_iota(jnp.int32, (8, LANES), 1) & 2) == 0
    pairs = velocity(points)
    for k in range(3):
        pattern_ref[k] = by_half(pairs[k])
    small[1].wait()
    for x in range(DEPTH):
        for wall in range(2):
            planes = wall_ref[wall, :, x : x + 1].astype(F32)
            planes = jnp.broadcast_to(planes, (PLANES, LANES))
            pattern_ref[3 + 2 * x + wall] = jnp.concatenate([planes] * 4, axis=0)
    small[2].wait()
    for core in range(2):
        half_ref[core, 21:23, :] = mirror_ref[...].astype(F32)

    x2 = pairs[1]
    for x in range(DEPTH):
        if x % 2 == 0:
            chunks[x // 2].wait()
            f = f_ref[pl.ds(x * XROWS, 2 * XROWS), :]
            high = f.astype(BF16)
            rest = f - high.astype(F32)
            middle = rest.astype(BF16)
            low = (rest - middle.astype(F32)).astype(BF16)
            both = lax.dot_general(
                table,
                jnp.concatenate([high, middle, low], axis=1),
                (((1,), (1,)), ((), ())),
                preferred_element_type=F32,
            )
        sums = both[:, XROWS * (x % 2) : XROWS * (x % 2 + 1)]
        packed = jnp.where(
            low_lane,
            sums[0:8] + pltpu.roll(sums[16:24], LANES - 2, 1),
            sums[24:32] + pltpu.roll(sums[8:16], 2, 1),
        )
        core, second = divmod(x, 2)
        tail = packed[5:8]
        half_ref[core, pl.ds(5 * second, 2), :] = packed[0:2]
        half_ref[core, pl.ds(5 * second + 2, 3), :] = packed[2:5] + jnp.where(
            low_lane[0:3], 0.0, tail
        )
        if second:
            half_ref[core, 10:13, :] = jnp.where(
                low_lane[0:3], before, pltpu.roll(packed, 2, 1)[5:8]
            )
        before = tail
        for half in range(2):
            low = f_ref[pl.ds(x * XROWS + 2 * half, 2), :]
            high = f_ref[pl.ds((x + 1) * XROWS - 4 + 2 * half, 2), :]
            half_ref[core, pl.ds(13 + 4 * half + 2 * second, 2), :] = jnp.where(
                x2[half : half + 1] < 0, low, high
            )
        if second:
            for to in [p for p in range(16) if VELO[p] % 2 == core]:
                send_ref[pl.ds(SHARE * to, SHARE), :] = half_ref[core, 0:SHARE, :]


def cell_quantities(sums):
    low_lane = (lax.broadcasted_iota(jnp.int32, (2, LANES), 1) & 2) == 0
    low, high = [], []
    for m in range(8):
        if m < 5:
            own = jnp.concatenate([sums[m : m + 1], sums[5 + m : 6 + m]], axis=0)
            own = own * WEIGHT
            other = jnp.where(
                low_lane, pltpu.roll(own, LANES - 2, 1), pltpu.roll(own, 2, 1)
            )
            low.append(jnp.where(low_lane, own, other))
            high.append(jnp.where(low_lane, other, own))
        else:
            own = jnp.broadcast_to(sums[5 + m : 6 + m], (2, LANES)) * WEIGHT
            first = jnp.where(low_lane, own, pltpu.roll(own, 2, 1))
            second = jnp.where(low_lane, pltpu.roll(own, LANES - 2, 1), own)
            low.append(jnp.where(sublane((2, LANES)) == 0, first, second))
    n = low[0]
    inv = 1.0 / n
    u = [low[1 + k] * inv for k in range(3)]
    pressure = {(0, 0): low[4], (1, 1): low[5], (2, 2): low[6]}
    pressure.update({(0, 1): low[7], (0, 2): high[0], (1, 2): high[1]})
    energy = low[4] + low[5] + low[6]
    speed = u[0] * u[0] + u[1] * u[1] + u[2] * u[2]
    temperature = (energy - n * speed) * inv * (1.0 / 3.0)
    heat = []
    for k in range(3):
        cross = sum(u[j] * pressure[min(j, k), max(j, k)] for j in range(3))
        heat.append(0.5 * (high[2 + k] - 2.0 * cross + u[k] * (2.0 * n * speed - energy)))
    inv_t = 1.0 / temperature
    scale = (1.0 - diffusivity_ratio) / 5.0 * inv * inv_t * inv_t
    arg = 2.0 * math.pi * temperature
    norm = n / (arg * jnp.sqrt(arg))
    heat = [h * scale for h in heat]
    rate = relaxation_multiplier * n * jnp.exp((1.0 - shear_power_index) * jnp.log(temperature))
    ratio = [speed * inv_t] + [-2.0 * v * inv_t for v in u] + [inv_t]
    along = [-(u[0] * heat[0] + u[1] * heat[1] + u[2] * heat[2])] + heat
    return ratio + along + [norm, rate]


def cells_kernel(sources, got_ref, out_ref):
    sums = got_ref[pl.ds(0, 16), :]
    for k in range(1, sources):
        sums = sums + got_ref[pl.ds(SHARE * k, 16), :]
    quantities = cell_quantities(sums)
    filler = jnp.zeros((24 - 2 * len(quantities), LANES), F32)
    table = jnp.concatenate(quantities + [filler], axis=0)
    for k in range(3):
        out_ref[k] = table[8 * k : 8 * k + 8]

    upper = (sublane((8, LANES)) >> 2) & 1
    chip = lax.axis_index("vel") // 2
    lanes, kept, rolled, values = [], [], [], []
    for core in range(2):
        at = SHARE * ((9 - 2 * chip - core) % 16) + 21
        first = jnp.broadcast_to(got_ref[pl.ds(at, 1), :], (8, LANES))
        second = jnp.broadcast_to(got_ref[pl.ds(at + 1, 1), :], (8, LANES))
        slot = jnp.where(upper == 0, first, second).astype(jnp.int32)
        lanes.append(slot & (LANES - 1))
        kept.append((slot >> 7) - upper)
        rolled.append((slot >> 7) + upper)
        values.append(jnp.zeros((8, LANES), F32))
    for k in range(sources):
        piece = got_ref[pl.ds(SHARE * k + 13, 8), :]
        swapped = pltpu.roll(piece, 4, 0)
        owner = VELO[k]
        for core in range(2):
            there = jnp.take_along_axis(piece, lanes[core], axis=1)
            across = jnp.take_along_axis(swapped, lanes[core], axis=1)
            value = jnp.where(kept[core] == 2 * owner, there, values[core])
            values[core] = jnp.where(rolled[core] == 2 * owner + 1, across, value)
    for core in range(2):
        out_ref[3 + core] = values[core]


def blocks_kernel(
    copies, got_ref, f_ref, pattern_ref, weight_ref, send_ref, a_ref, h_ref, poly_ref
):
    halves = [
        jnp.concatenate([got_ref[half, k] for k in range(3)], axis=0) for half in range(2)
    ]
    rates = [halves[x // 2][20 + x % 2 : 21 + x % 2] for x in range(DEPTH)]
    rows, left = [], halves
    for part in range(3):
        pieces = [h.astype(BF16).astype(F32) for h in left]
        rows += [p[0:18] for p in pieces]
        left = [h - p for h, p in zip(left, pieces)]
    rows += [h[18:22] for h in halves]
    filler = jnp.zeros((LANES - 116, LANES), F32)
    columns = jnp.concatenate(rows + [filler], axis=0).T

    lane = lax.broadcasted_iota(jnp.int32, (8, LANES), 1)
    term = lane & 15
    term = jnp.where(term > 9, 0, jnp.where(term > 4, term - 1, term))
    source = 36 * jnp.where(lane < 96, lane >> 5, 0) + 2 * term
    same = ((sublane((8, LANES)) >> 1) & 1) == ((lane >> 4) & 1)
    left = []
    for x in range(DEPTH):
        at = source + (18 * (x // 2) + x % 2)
        for i in range(XROWS // 8):
            value = jnp.take_along_axis(columns[8 * i : 8 * i + 8], at, axis=1)
            left.append(jnp.where(same, value, 0.0))
    poly_ref[...] = lax.dot_general(
        jnp.concatenate(left, axis=0).astype(BF16),
        weight_ref[...],
        (((1,), (0,)), ((), ())),
        preferred_element_type=F32,
    )
    core = lax.axis_index("vel") % 2
    found = [got_ref[half, 3 + core] for half in range(2)]

    lane = lax.broadcasted_iota(jnp.int32, (8, LANES), 1)
    cell = (lane >> 3) & 7
    source = 16 * sublane((8, LANES)) + 4 * (cell >> 1) + (cell & 1)
    speed = stream_x * SPACING * ((lane & 7).astype(F32) + 0.5)
    chunk_gain = jnp.ones((8, LANES), F32)
    for x in range(DEPTH):
        rate = jnp.broadcast_to(rates[x], (8, LANES))
        rate = jnp.take_along_axis(rate, source, axis=1)
        chunk_gain = chunk_gain * (speed / (1.0 + speed + rate))
    for to in range(copies * CHUNKS):
        at = to % CHUNKS
        send_ref[pl.ds(CHUNK_ROWS * ORDER.index(to) + 16, 1), :] = chunk_gain[at : at + 1]

    x1, x2, x3 = pattern_ref[0], pattern_ref[1], pattern_ref[2]
    ahead = x1 > 0
    upward = x2 > 0
    sigma = stream_x * jnp.abs(x1)
    sigma1 = 1.0 + sigma
    flux_y = stream_y * jnp.abs(x2)
    flux_z = stream_z * jnp.abs(x3)
    own = 1.0 - flux_y - flux_z
    row = sublane((8, LANES))
    first_plane = (row & 1) == 0
    lower = row < 4
    here = lax.axis_index("space")
    edge = here == jnp.where(ahead, 0, lax.axis_size("space") - 1)

    ghosts = []
    for x in range(DEPTH):
        wall = found[x // 2]
        at = 2 * (x % 2)
        four = jnp.concatenate([wall[at : at + 2], wall[at + 4 : at + 6]], axis=0)
        ghosts.append(jnp.concatenate([four, four], axis=0))

    for i in range(XROWS // 8):
        a, b, target = [], [], []
        for x in range(DEPTH):
            def column(q):
                at = 108 + 4 * (x // 2) + 2 * q + x % 2
                return jnp.broadcast_to(
                    columns[8 * i : 8 * i + 8, at : at + 1], (8, LANES)
                )

            base = x * XROWS + 8 * i
            f = f_ref[pl.ds(base, 8), :]
            ratio = poly_ref[pl.ds(base, 8), 0:LANES]
            along = poly_ref[pl.ds(base, 8), LANES : 2 * LANES]
            shakhov = column(0) * jnp.exp(-0.5 * ratio) * (1.0 + along * (ratio - 5.0))
            rate = column(1)

            def ghost(wall):
                mask = pattern_ref[3 + 2 * x + wall]
                return jnp.where(mask == 1.0, ghosts[x], shakhov)

            if i == 0:
                below = jnp.where(lower, ghost(0), pltpu.roll(f, 4, 0))
            else:
                below = f_ref[pl.ds(base - 4, 8), :]
            if i == XROWS // 8 - 1:
                above = jnp.where(lower, pltpu.roll(f, 4, 0), ghost(1))
            else:
                above = f_ref[pl.ds(base + 4, 8), :]
            upwind = jnp.where(upward, below, above)
            other = jnp.where(first_plane, pltpu.roll(f, 7, 0), pltpu.roll(f, 1, 0))
            inverse = 1.0 / (sigma1 + rate)
            a.append(sigma * inverse)
            b.append(
                (own * f + rate * shakhov + flux_y * upwind + flux_z * other) * inverse
            )
            target.append(shakhov)
        order = lambda v, t: jnp.where(ahead, v[t], v[DEPTH - 1 - t])
        a0 = order(a, 0)
        hold = order(b, 0) + jnp.where(edge, a0 * order(target, 0), 0.0)
        gain = jnp.where(edge, 0.0, a0)
        a_ref[pl.ds(8 * i, 8), :] = gain
        h_ref[pl.ds(8 * i, 8), :] = hold
        for t in range(1, DEPTH):
            at = order(a, t)
            gain = at * gain
            hold = at * hold + order(b, t)
            a_ref[pl.ds(t * XROWS + 8 * i, 8), :] = gain
            h_ref[pl.ds(t * XROWS + 8 * i, 8), :] = hold
        for copy in range(copies):
            to = copy * CHUNKS + i // 2
            send_ref[pl.ds(CHUNK_ROWS * ORDER.index(to) + 8 * (i % 2), 8), :] = hold


def chain_kernel(copies, got_ref, pattern_ref, out_ref, gain_ref, keep_ref):
    blocks = copies * CHUNKS
    ahead = pattern_ref[0] > 0
    which = (jnp.abs(pattern_ref[0]) * (1.0 / SPACING) - 0.5).astype(jnp.int32)
    row = sublane((8, LANES))
    for half in range(2):
        cell = 2 * (2 * half + (row >> 2)) + (row & 1)
        source = 8 * cell + which
        for k in range(blocks):
            gain = jnp.broadcast_to(got_ref[pl.ds(CHUNK_ROWS * ORDER.index(k) + 16, 1), :], (8, LANES))
            gain_ref[k] = jnp.take_along_axis(gain, source, axis=1)
        enter = jnp.zeros((8, LANES), F32)
        for k in range(blocks):
            keep_ref[half, k] = enter
            back = blocks - 1 - k
            gain = jnp.where(ahead, gain_ref[k], gain_ref[back])
            hold = jnp.where(
                ahead,
                got_ref[pl.ds(CHUNK_ROWS * ORDER.index(k) + 8 * half, 8), :],
                got_ref[pl.ds(CHUNK_ROWS * ORDER.index(back) + 8 * half, 8), :],
            )
            enter = gain * enter + hold
    first = lax.axis_index("space") // CHUNKS * CHUNKS
    for half in range(2):
        for x in range(CHUNKS):
            out_ref[LINE.index(x), pl.ds(8 * half, 8), :] = jnp.where(
                ahead, keep_ref[half, first + x], keep_ref[half, blocks - 1 - x - first]
            )


def finish_kernel(enter_ref, a_ref, h_ref, pattern_ref, out_hbm, out_ref, sem):
    ahead = pattern_ref[0] > 0
    copies = []
    for x, mate in ((0, DEPTH - 1), (1, DEPTH - 2)):
        for i in range(XROWS // 8):
            enter = enter_ref[pl.ds(16 * LINE.index(i // 2) + 8 * (i % 2), 8), :]
            value = []
            for t in (x, mate):
                at = pl.ds(t * XROWS + 8 * i, 8)
                value.append(a_ref[at, :] * enter + h_ref[at, :])
            out_ref[pl.ds(x * XROWS + 8 * i, 8), :] = jnp.where(ahead, value[0], value[1])
            out_ref[pl.ds(mate * XROWS + 8 * i, 8), :] = jnp.where(ahead, value[1], value[0])
        for t in (x, mate):
            rows = pl.ds(t * XROWS, XROWS)
            copies.append(pltpu.make_async_copy(out_ref.at[rows], out_hbm.at[rows], sem.at[t]))
            copies[-1].start()
    for copy in copies:
        copy.wait()


ON_CHIP = pl.BlockSpec(memory_space=pltpu.VMEM)
ANYWHERE = pl.BlockSpec(memory_space=pl.ANY)


def held(x):
    return pltpu.with_memory_space_constraint(x, pltpu.VMEM)


def shards(distribution, wall_mask, grid_point, mirror_slot):
    blocks = lax.axis_size("space")
    copies = blocks // CHUNKS
    f = distribution.reshape(DEPTH, ROWS, PLANES, 2, LANES)
    f = f.transpose(0, 1, 3, 2, 4).reshape(DEPTH * XROWS, LANES)
    point = grid_point.reshape(2, LANES)
    mirror = mirror_slot.reshape(2, LANES)
    wall = wall_mask.transpose(1, 2, 0)

    sources = lax.axis_size("vel")
    shares, kept, pattern, weights = pl.pallas_call(
        moments_kernel,
        out_shape=[
            pltpu.VMEM((sources * SHARE, LANES), F32),
            pltpu.VMEM((DEPTH * XROWS, LANES), F32),
            pltpu.VMEM((3 + 2 * DEPTH, 8, LANES), F32),
            pltpu.VMEM((LANES, 2 * LANES), BF16),
        ],
        in_specs=[ANYWHERE] * 4,
        out_specs=[ON_CHIP] * 4,
        scratch_shapes=[
            pltpu.VMEM((2, 24, LANES), F32),
            pltpu.VMEM((2, LANES), jnp.int32),
            pltpu.VMEM((2, LANES), jnp.int32),
            pltpu.VMEM((2, PLANES, DEPTH), jnp.int32),
            pltpu.SemaphoreType.DMA((2,)),
            pltpu.SemaphoreType.DMA((3,)),
        ],
    )(f, point, mirror, wall)
    partial = lax.all_to_all(
        shares.reshape(sources, 1, SHARE * LANES),
        "vel",
        0,
        0,
        axis_index_groups=[VELO],
        tiled=True,
    ).reshape(sources * SHARE, LANES)
    cells = pl.pallas_call(
        lambda *refs: cells_kernel(sources, *refs),
        out_shape=pltpu.VMEM((5, 8, LANES), F32),
        in_specs=[ON_CHIP],
        out_specs=ON_CHIP,
    )(held(partial))
    pairs = [[k, k + 1] for k in range(0, sources, 2)]
    everyone = lax.all_gather(cells, "vel", axis_index_groups=pairs)
    send, gains, holds = pl.pallas_call(
        lambda *refs: blocks_kernel(copies, *refs),
        out_shape=[
            pltpu.VMEM((blocks * CHUNK_ROWS, LANES), F32),
            pltpu.VMEM((DEPTH * XROWS, LANES), F32),
            pltpu.VMEM((DEPTH * XROWS, LANES), F32),
        ],
        in_specs=[ON_CHIP] * 4,
        out_specs=[ON_CHIP] * 3,
        scratch_shapes=[pltpu.VMEM((DEPTH * XROWS, 2 * LANES), F32)],
    )(held(everyone), held(kept), held(pattern), held(weights))
    chain = lax.all_to_all(
        send.reshape(blocks, 1, CHUNK_ROWS * LANES), "space", 0, 0, axis_index_groups=[ORDER], tiled=True
    ).reshape(blocks * CHUNK_ROWS, LANES)
    enters = pl.pallas_call(
        lambda *refs: chain_kernel(copies, *refs),
        out_shape=pltpu.VMEM((CHUNKS, 16, LANES), F32),
        in_specs=[ON_CHIP] * 2,
        out_specs=ON_CHIP,
        scratch_shapes=[
            pltpu.VMEM((blocks, 8, LANES), F32),
            pltpu.VMEM((2, blocks, 8, LANES), F32),
        ],
    )(held(chain), held(pattern))
    lines = [[CHUNKS * z + x for x in LINE] for z in range(copies)]
    enter = lax.all_to_all(enters, "space", 0, 0, axis_index_groups=lines, tiled=True)
    out = pl.pallas_call(
        finish_kernel,
        out_shape=jax.ShapeDtypeStruct((DEPTH * XROWS, LANES), F32),
        in_specs=[ON_CHIP] * 4,
        out_specs=ANYWHERE,
        scratch_shapes=[
            pltpu.VMEM((DEPTH * XROWS, LANES), F32),
            pltpu.SemaphoreType.DMA((DEPTH,)),
        ],
    )(held(enter.reshape(XROWS, LANES)), held(gains), held(holds), held(pattern))
    out = out.reshape(DEPTH, ROWS, 2, PLANES, LANES).transpose(0, 1, 3, 2, 4)
    return out.reshape(DEPTH, ROWS, PLANES, WIDTH)


def solution(mesh):
    placed = (P("space", None, None, "vel"), P("space", None, None), P("vel"), P("vel"))
    return jax.shard_map(
        shards, mesh=mesh, in_specs=placed, out_specs=P("space", None, None, "vel"), check_vma=False
    )
```

```python
import math

import jax
import jax.numpy as jnp
from jax import lax
from jax.experimental import pallas as pl
from jax.experimental.pallas import tpu as pltpu
from jax.sharding import PartitionSpec as P

VS = 16
SPACING = 8.0 / VS
HALF = (VS - 1) / 2.0
WEIGHT = SPACING**3

stream_x = 40.0
stream_y = 0.15
stream_z = 0.05
relaxation_multiplier = 0.05
shear_power_index = 0.81
diffusivity_ratio = 2.0 / 3.0

DEPTH, ROWS, PLANES, WIDTH = 4, 32, 2, 256
LANES = 128
XROWS = ROWS * 2 * PLANES
F32 = jnp.float32
BF16 = jnp.bfloat16

CHUNKS = 8
CHUNK_ROWS = 17

VELO = [8, 9, 6, 7, 4, 5, 2, 3, 0, 1, 14, 15, 12, 13, 10, 11]
LINE = [6, 5, 4, 3, 2, 1, 0, 7]
ORDER = [8 * z + x for z in range(3, -1, -1) for x in LINE]

SHARE = 23


def velocity(points):
    first = (points >> 8).astype(F32)
    second = ((points >> 4) & 15).astype(F32)
    third = (points & 15).astype(F32)
    return [(v - HALF) * SPACING for v in (first, second, third)]


def sublane(shape):
    return lax.broadcasted_iota(jnp.int32, shape, 0)


def by_half(pair):
    low = jnp.broadcast_to(pair[0:1], (8, LANES))
    high = jnp.broadcast_to(pair[1:2], (8, LANES))
    return jnp.where((sublane((8, LANES)) & 2) == 0, low, high)


def moments_kernel(
    f_hbm, point_hbm, mirror_hbm, wall_hbm,
    send_ref, f_ref, pattern_ref, weight_ref,
    half_ref, point_ref, mirror_ref, wall_ref, f_sem, small_sem,
):
    small = [
        pltpu.make_async_copy(src, dst, small_sem.at[k])
        for k, (src, dst) in enumerate(
            [(point_hbm, point_ref), (wall_hbm, wall_ref), (mirror_hbm, mirror_ref)]
        )
    ]
    for copy in small:
        copy.start()
    chunks = []
    for x in range(2):
        rows = pl.ds(2 * x * XROWS, 2 * XROWS)
        chunks.append(pltpu.make_async_copy(f_hbm.at[rows], f_ref.at[rows], f_sem.at[x]))
        chunks[x].start()

    small[0].wait()
    points = point_ref[...]
    tables = []
    for half in range(2):
        x1, x2, x3 = velocity(points[half : half + 1])
        square = x1 * x1 + x2 * x2 + x3 * x3
        cubes = [x1 * square, x2 * square, x3 * square]
        coarse = [c.astype(BF16).astype(F32) for c in cubes]
        tables += [
            jnp.ones_like(x1), x1, x2, x3,
            x1 * x1, x2 * x2, x3 * x3, x1 * x2,
            x1 * x3, x2 * x3, *coarse,
            *[c - r for c, r in zip(cubes, coarse)],
        ]
    weights = []
    for half in range(2):
        x1, x2, x3 = velocity(points[half : half + 1])
        square = x1 * x1 + x2 * x2 + x3 * x3
        coarse = square.astype(BF16).astype(F32)
        one, zero = jnp.ones_like(x1), jnp.zeros_like(x1)
        left = [one, x1, x2, x3, coarse, square - coarse] + [zero] * 10
        right = [zero] * 6 + [one, x1, x2, x3] + [zero] * 6
        weights += [jnp.concatenate(pair, axis=1) for pair in zip(left, right)]
    weights = jnp.concatenate(weights, axis=0).astype(BF16)
    weight_ref[...] = jnp.concatenate([weights] * 3 + [jnp.zeros_like(weights)], axis=0)
    table = jnp.concatenate(tables, axis=0).astype(BF16)
    table = jnp.concatenate([table] * 3, axis=1)
    low_lane = (lax.broadcasted_iota(jnp.int32, (8, LANES), 1) & 2) == 0
    pairs = velocity(points)
    for k in range(3):
        pattern_ref[k] = by_half(pairs[k])
    small[1].wait()
    for x in range(DEPTH):
        for wall in range(2):
            planes = wall_ref[wall, :, x : x + 1].astype(F32)
            planes = jnp.broadcast_to(planes, (PLANES, LANES))
            pattern_ref[3 + 2 * x + wall] = jnp.concatenate([planes] * 4, axis=0)
    small[2].wait()
    for core in range(2):
        half_ref[core, 21:23, :] = mirror_ref[...].astype(F32)

    x2 = pairs[1]
    for x in range(DEPTH):
        if x % 2 == 0:
            chunks[x // 2].wait()
            f = f_ref[pl.ds(x * XROWS, 2 * XROWS), :]
            high = f.astype(BF16)
            rest = f - high.astype(F32)
            middle = rest.astype(BF16)
            low = (rest - middle.astype(F32)).astype(BF16)
            both = lax.dot_general(
                table,
                jnp.concatenate([high, middle, low], axis=1),
                (((1,), (1,)), ((), ())),
                preferred_element_type=F32,
            )
        sums = both[:, XROWS * (x % 2) : XROWS * (x % 2 + 1)]
        packed = jnp.where(
            low_lane,
            sums[0:8] + pltpu.roll(sums[16:24], LANES - 2, 1),
            sums[24:32] + pltpu.roll(sums[8:16], 2, 1),
        )
        core, second = divmod(x, 2)
        tail = packed[5:8]
        half_ref[core, pl.ds(5 * second, 2), :] = packed[0:2]
        half_ref[core, pl.ds(5 * second + 2, 3), :] = packed[2:5] + jnp.where(
            low_lane[0:3], 0.0, tail
        )
        if second:
            half_ref[core, 10:13, :] = jnp.where(
                low_lane[0:3], before, pltpu.roll(packed, 2, 1)[5:8]
            )
        before = tail
        for half in range(2):
            low = f_ref[pl.ds(x * XROWS + 2 * half, 2), :]
            high = f_ref[pl.ds((x + 1) * XROWS - 4 + 2 * half, 2), :]
            half_ref[core, pl.ds(13 + 4 * half + 2 * second, 2), :] = jnp.where(
                x2[half : half + 1] < 0, low, high
            )
        if second:
            for to in [p for p in range(16) if VELO[p] % 2 == core]:
                send_ref[pl.ds(SHARE * to, SHARE), :] = half_ref[core, 0:SHARE, :]


def cell_quantities(sums):
    low_lane = (lax.broadcasted_iota(jnp.int32, (2, LANES), 1) & 2) == 0
    low, high = [], []
    for m in range(8):
        if m < 5:
            own = jnp.concatenate([sums[m : m + 1], sums[5 + m : 6 + m]], axis=0)
            own = own * WEIGHT
            other = jnp.where(
                low_lane, pltpu.roll(own, LANES - 2, 1), pltpu.roll(own, 2, 1)
            )
            low.append(jnp.where(low_lane, own, other))
            high.append(jnp.where(low_lane, other, own))
        else:
            own = jnp.broadcast_to(sums[5 + m : 6 + m], (2, LANES)) * WEIGHT
            first = jnp.where(low_lane, own, pltpu.roll(own, 2, 1))
            second = jnp.where(low_lane, pltpu.roll(own, LANES - 2, 1), own)
            low.append(jnp.where(sublane((2, LANES)) == 0, first, second))
    n = low[0]
    inv = 1.0 / n
    u = [low[1 + k] * inv for k in range(3)]
    pressure = {(0, 0): low[4], (1, 1): low[5], (2, 2): low[6]}
    pressure.update({(0, 1): low[7], (0, 2): high[0], (1, 2): high[1]})
    energy = low[4] + low[5] + low[6]
    speed = u[0] * u[0] + u[1] * u[1] + u[2] * u[2]
    temperature = (energy - n * speed) * inv * (1.0 / 3.0)
    heat = []
    for k in range(3):
        cross = sum(u[j] * pressure[min(j, k), max(j, k)] for j in range(3))
        heat.append(0.5 * (high[2 + k] - 2.0 * cross + u[k] * (2.0 * n * speed - energy)))
    inv_t = 1.0 / temperature
    scale = (1.0 - diffusivity_ratio) / 5.0 * inv * inv_t * inv_t
    arg = 2.0 * math.pi * temperature
    norm = n / (arg * jnp.sqrt(arg))
    heat = [h * scale for h in heat]
    rate = relaxation_multiplier * n * jnp.exp((1.0 - shear_power_index) * jnp.log(temperature))
    ratio = [speed * inv_t] + [-2.0 * v * inv_t for v in u] + [inv_t]
    along = [-(u[0] * heat[0] + u[1] * heat[1] + u[2] * heat[2])] + heat
    return ratio + along + [norm, rate]


def cells_kernel(sources, got_ref, out_ref):
    sums = got_ref[pl.ds(0, 16), :]
    for k in range(1, sources):
        sums = sums + got_ref[pl.ds(SHARE * k, 16), :]
    quantities = cell_quantities(sums)
    filler = jnp.zeros((24 - 2 * len(quantities), LANES), F32)
    table = jnp.concatenate(quantities + [filler], axis=0)
    for k in range(3):
        out_ref[k] = table[8 * k : 8 * k + 8]

    upper = (sublane((8, LANES)) >> 2) & 1
    chip = lax.axis_index("vel") // 2
    lanes, kept, rolled, values = [], [], [], []
    for core in range(2):
        at = SHARE * ((8 - 2 * chip) % 16 + core) + 21
        first = jnp.broadcast_to(got_ref[pl.ds(at, 1), :], (8, LANES))
        second = jnp.broadcast_to(got_ref[pl.ds(at + 1, 1), :], (8, LANES))
        slot = jnp.where(upper == 0, first, second).astype(jnp.int32)
        lanes.append(slot & (LANES - 1))
        kept.append((slot >> 7) - upper)
        rolled.append((slot >> 7) + upper)
        values.append(jnp.zeros((8, LANES), F32))
    for k in range(sources):
        piece = got_ref[pl.ds(SHARE * k + 13, 8), :]
        swapped = pltpu.roll(piece, 4, 0)
        owner = VELO[k]
        for core in range(2):
            there = jnp.take_along_axis(piece, lanes[core], axis=1)
            across = jnp.take_along_axis(swapped, lanes[core], axis=1)
            value = jnp.where(kept[core] == 2 * owner, there, values[core])
            values[core] = jnp.where(rolled[core] == 2 * owner + 1, across, value)
    for core in range(2):
        out_ref[3 + core] = values[core]


def blocks_kernel(
    copies, got_ref, f_ref, pattern_ref, weight_ref, send_ref, a_ref, h_ref, poly_ref
):
    halves = [
        jnp.concatenate([got_ref[half, k] for k in range(3)], axis=0) for half in range(2)
    ]
    rates = [halves[x // 2][20 + x % 2 : 21 + x % 2] for x in range(DEPTH)]
    rows, left = [], halves
    for part in range(3):
        pieces = [h.astype(BF16).astype(F32) for h in left]
        rows += [p[0:18] for p in pieces]
        left = [h - p for h, p in zip(left, pieces)]
    rows += [h[18:22] for h in halves]
    filler = jnp.zeros((LANES - 116, LANES), F32)
    columns = jnp.concatenate(rows + [filler], axis=0).T

    lane = lax.broadcasted_iota(jnp.int32, (8, LANES), 1)
    term = lane & 15
    term = jnp.where(term > 9, 0, jnp.where(term > 4, term - 1, term))
    source = 36 * jnp.where(lane < 96, lane >> 5, 0) + 2 * term
    same = ((sublane((8, LANES)) >> 1) & 1) == ((lane >> 4) & 1)
    left = []
    for x in range(DEPTH):
        at = source + (18 * (x // 2) + x % 2)
        for i in range(XROWS // 8):
            value = jnp.take_along_axis(columns[8 * i : 8 * i + 8], at, axis=1)
            left.append(jnp.where(same, value, 0.0))
    poly_ref[...] = lax.dot_general(
        jnp.concatenate(left, axis=0).astype(BF16),
        weight_ref[...],
        (((1,), (0,)), ((), ())),
        preferred_element_type=F32,
    )
    core = lax.axis_index("vel") % 2
    found = [got_ref[half, 3 + core] for half in range(2)]

    lane = lax.broadcasted_iota(jnp.int32, (8, LANES), 1)
    cell = (lane >> 3) & 7
    source = 16 * sublane((8, LANES)) + 4 * (cell >> 1) + (cell & 1)
    speed = stream_x * SPACING * ((lane & 7).astype(F32) + 0.5)
    chunk_gain = jnp.ones((8, LANES), F32)
    for x in range(DEPTH):
        rate = jnp.broadcast_to(rates[x], (8, LANES))
        rate = jnp.take_along_axis(rate, source, axis=1)
        chunk_gain = chunk_gain * (speed / (1.0 + speed + rate))
    for to in range(copies * CHUNKS):
        at = to % CHUNKS
        send_ref[pl.ds(CHUNK_ROWS * ORDER.index(to) + 16, 1), :] = chunk_gain[at : at + 1]

    x1, x2, x3 = pattern_ref[0], pattern_ref[1], pattern_ref[2]
    ahead = x1 > 0
    upward = x2 > 0
    sigma = stream_x * jnp.abs(x1)
    sigma1 = 1.0 + sigma
    flux_y = stream_y * jnp.abs(x2)
    flux_z = stream_z * jnp.abs(x3)
    own = 1.0 - flux_y - flux_z
    row = sublane((8, LANES))
    first_plane = (row & 1) == 0
    lower = row < 4
    here = lax.axis_index("space")
    edge = here == jnp.where(ahead, 0, lax.axis_size("space") - 1)

    ghosts = []
    for x in range(DEPTH):
        wall = found[x // 2]
        at = 2 * (x % 2)
        four = jnp.concatenate([wall[at : at + 2], wall[at + 4 : at + 6]], axis=0)
        ghosts.append(jnp.concatenate([four, four], axis=0))

    for i in range(XROWS // 8):
        a, b, target = [], [], []
        for x in range(DEPTH):
            def column(q):
                at = 108 + 4 * (x // 2) + 2 * q + x % 2
                return jnp.broadcast_to(
                    columns[8 * i : 8 * i + 8, at : at + 1], (8, LANES)
                )

            base = x * XROWS + 8 * i
            f = f_ref[pl.ds(base, 8), :]
            ratio = poly_ref[pl.ds(base, 8), 0:LANES]
            along = poly_ref[pl.ds(base, 8), LANES : 2 * LANES]
            shakhov = column(0) * jnp.exp(-0.5 * ratio) * (1.0 + along * (ratio - 5.0))
            rate = column(1)

            def ghost(wall):
                mask = pattern_ref[3 + 2 * x + wall]
                return jnp.where(mask == 1.0, ghosts[x], shakhov)

            if i == 0:
                below = jnp.where(lower, ghost(0), pltpu.roll(f, 4, 0))
            else:
                below = f_ref[pl.ds(base - 4, 8), :]
            if i == XROWS // 8 - 1:
                above = jnp.where(lower, pltpu.roll(f, 4, 0), ghost(1))
            else:
                above = f_ref[pl.ds(base + 4, 8), :]
            upwind = jnp.where(upward, below, above)
            other = jnp.where(first_plane, pltpu.roll(f, 7, 0), pltpu.roll(f, 1, 0))
            inverse = 1.0 / (sigma1 + rate)
            a.append(sigma * inverse)
            b.append(
                (own * f + rate * shakhov + flux_y * upwind + flux_z * other) * inverse
            )
            target.append(shakhov)
        order = lambda v, t: jnp.where(ahead, v[t], v[DEPTH - 1 - t])
        a0 = order(a, 0)
        hold = order(b, 0) + jnp.where(edge, a0 * order(target, 0), 0.0)
        gain = jnp.where(edge, 0.0, a0)
        a_ref[pl.ds(8 * i, 8), :] = gain
        h_ref[pl.ds(8 * i, 8), :] = hold
        for t in range(1, DEPTH):
            at = order(a, t)
            gain = at * gain
            hold = at * hold + order(b, t)
            a_ref[pl.ds(t * XROWS + 8 * i, 8), :] = gain
            h_ref[pl.ds(t * XROWS + 8 * i, 8), :] = hold
        for copy in range(copies):
            to = copy * CHUNKS + i // 2
            send_ref[pl.ds(CHUNK_ROWS * ORDER.index(to) + 8 * (i % 2), 8), :] = hold


def chain_kernel(copies, got_ref, pattern_ref, out_ref, gain_ref, keep_ref):
    blocks = copies * CHUNKS
    ahead = pattern_ref[0] > 0
    which = (jnp.abs(pattern_ref[0]) * (1.0 / SPACING) - 0.5).astype(jnp.int32)
    row = sublane((8, LANES))
    for half in range(2):
        cell = 2 * (2 * half + (row >> 2)) + (row & 1)
        source = 8 * cell + which
        for k in range(blocks):
            gain = jnp.broadcast_to(got_ref[pl.ds(CHUNK_ROWS * ORDER.index(k) + 16, 1), :], (8, LANES))
            gain_ref[k] = jnp.take_along_axis(gain, source, axis=1)
        enter = jnp.zeros((8, LANES), F32)
        for k in range(blocks):
            keep_ref[half, k] = enter
            back = blocks - 1 - k
            gain = jnp.where(ahead, gain_ref[k], gain_ref[back])
            hold = jnp.where(
                ahead,
                got_ref[pl.ds(CHUNK_ROWS * ORDER.index(k) + 8 * half, 8), :],
                got_ref[pl.ds(CHUNK_ROWS * ORDER.index(back) + 8 * half, 8), :],
            )
            enter = gain * enter + hold
    first = lax.axis_index("space") // CHUNKS * CHUNKS
    for half in range(2):
        for x in range(CHUNKS):
            out_ref[LINE.index(x), pl.ds(8 * half, 8), :] = jnp.where(
                ahead, keep_ref[half, first + x], keep_ref[half, blocks - 1 - x - first]
            )


def finish_kernel(enter_ref, a_ref, h_ref, pattern_ref, out_hbm, out_ref, sem):
    ahead = pattern_ref[0] > 0
    copies = []
    for x, mate in ((0, DEPTH - 1), (1, DEPTH - 2)):
        for i in range(XROWS // 8):
            enter = enter_ref[pl.ds(16 * LINE.index(i // 2) + 8 * (i % 2), 8), :]
            value = []
            for t in (x, mate):
                at = pl.ds(t * XROWS + 8 * i, 8)
                value.append(a_ref[at, :] * enter + h_ref[at, :])
            out_ref[pl.ds(x * XROWS + 8 * i, 8), :] = jnp.where(ahead, value[0], value[1])
            out_ref[pl.ds(mate * XROWS + 8 * i, 8), :] = jnp.where(ahead, value[1], value[0])
        for t in (x, mate):
            rows = pl.ds(t * XROWS, XROWS)
            copies.append(pltpu.make_async_copy(out_ref.at[rows], out_hbm.at[rows], sem.at[t]))
            copies[-1].start()
    for copy in copies:
        copy.wait()


ON_CHIP = pl.BlockSpec(memory_space=pltpu.VMEM)
ANYWHERE = pl.BlockSpec(memory_space=pl.ANY)


def held(x):
    return pltpu.with_memory_space_constraint(x, pltpu.VMEM)


def shards(distribution, wall_mask, grid_point, mirror_slot):
    blocks = lax.axis_size("space")
    copies = blocks // CHUNKS
    f = distribution.reshape(DEPTH, ROWS, PLANES, 2, LANES)
    f = f.transpose(0, 1, 3, 2, 4).reshape(DEPTH * XROWS, LANES)
    point = grid_point.reshape(2, LANES)
    mirror = mirror_slot.reshape(2, LANES)
    wall = wall_mask.transpose(1, 2, 0)

    sources = lax.axis_size("vel")
    shares, kept, pattern, weights = pl.pallas_call(
        moments_kernel,
        out_shape=[
            pltpu.VMEM((sources * SHARE, LANES), F32),
            pltpu.VMEM((DEPTH * XROWS, LANES), F32),
            pltpu.VMEM((3 + 2 * DEPTH, 8, LANES), F32),
            pltpu.VMEM((LANES, 2 * LANES), BF16),
        ],
        in_specs=[ANYWHERE] * 4,
        out_specs=[ON_CHIP] * 4,
        scratch_shapes=[
            pltpu.VMEM((2, 24, LANES), F32),
            pltpu.VMEM((2, LANES), jnp.int32),
            pltpu.VMEM((2, LANES), jnp.int32),
            pltpu.VMEM((2, PLANES, DEPTH), jnp.int32),
            pltpu.SemaphoreType.DMA((2,)),
            pltpu.SemaphoreType.DMA((3,)),
        ],
    )(f, point, mirror, wall)
    partial = lax.all_to_all(
        shares.reshape(sources, 1, SHARE * LANES),
        "vel",
        0,
        0,
        axis_index_groups=[VELO],
        tiled=True,
    ).reshape(sources * SHARE, LANES)
    cells = pl.pallas_call(
        lambda *refs: cells_kernel(sources, *refs),
        out_shape=pltpu.VMEM((5, 8, LANES), F32),
        in_specs=[ON_CHIP],
        out_specs=ON_CHIP,
    )(held(partial))
    pairs = [[k, k + 1] for k in range(0, sources, 2)]
    everyone = lax.all_gather(cells, "vel", axis_index_groups=pairs)
    send, gains, holds = pl.pallas_call(
        lambda *refs: blocks_kernel(copies, *refs),
        out_shape=[
            pltpu.VMEM((blocks * CHUNK_ROWS, LANES), F32),
            pltpu.VMEM((DEPTH * XROWS, LANES), F32),
            pltpu.VMEM((DEPTH * XROWS, LANES), F32),
        ],
        in_specs=[ON_CHIP] * 4,
        out_specs=[ON_CHIP] * 3,
        scratch_shapes=[pltpu.VMEM((DEPTH * XROWS, 2 * LANES), F32)],
    )(held(everyone), held(kept), held(pattern), held(weights))
    chain = lax.all_to_all(
        send.reshape(blocks, 1, CHUNK_ROWS * LANES), "space", 0, 0, axis_index_groups=[ORDER], tiled=True
    ).reshape(blocks * CHUNK_ROWS, LANES)
    enters = pl.pallas_call(
        lambda *refs: chain_kernel(copies, *refs),
        out_shape=pltpu.VMEM((CHUNKS, 16, LANES), F32),
        in_specs=[ON_CHIP] * 2,
        out_specs=ON_CHIP,
        scratch_shapes=[
            pltpu.VMEM((blocks, 8, LANES), F32),
            pltpu.VMEM((2, blocks, 8, LANES), F32),
        ],
    )(held(chain), held(pattern))
    lines = [[CHUNKS * z + x for x in LINE] for z in range(copies)]
    enter = lax.all_to_all(enters, "space", 0, 0, axis_index_groups=lines, tiled=True)
    out = pl.pallas_call(
        finish_kernel,
        out_shape=jax.ShapeDtypeStruct((DEPTH * XROWS, LANES), F32),
        in_specs=[ON_CHIP] * 4,
        out_specs=ANYWHERE,
        scratch_shapes=[
            pltpu.VMEM((DEPTH * XROWS, LANES), F32),
            pltpu.SemaphoreType.DMA((DEPTH,)),
        ],
    )(held(enter.reshape(XROWS, LANES)), held(gains), held(holds), held(pattern))
    out = out.reshape(DEPTH, ROWS, 2, PLANES, LANES).transpose(0, 1, 3, 2, 4)
    return out.reshape(DEPTH, ROWS, PLANES, WIDTH)


def solution(mesh):
    placed = (P("space", None, None, "vel"), P("space", None, None), P("vel"), P("vel"))
    return jax.shard_map(
        shards, mesh=mesh, in_specs=placed, out_specs=P("space", None, None, "vel"), check_vma=False
    )
```
